32 devices in a mesh: dp: 4 (over x, core), seq: 8 (over z, y).
Axes of the slice: x: 2, y: 2, z: 4, core: 2. Of those that a mesh axis runs over, the one named last changes fastest.
Arguments:
- tokens: bfloat16 [2048, 4, 768], P('seq', 'dp'), may hold values from -6 to 6
- memory: bfloat16 [1536, 4, 768], P(None, 'dp'), may hold values from -6 to 6
- piece_starts: int32 [4, 3], P('dp'), may hold values from 0 to 1792, as said below
- memory_lengths: int32 [4], P('dp'), may hold values from 384 to 1536, as said below
- self_gain: bfloat16 [768], P(('dp', 'seq')), may hold values from 0.25 to 1.75
- self_shift: bfloat16 [768], P(('dp', 'seq')), may hold values from -3 to 3
- query_weight: bfloat16 [768, 768], P(('dp', 'seq')), may hold values from -0.21875 to 0.21875
- query_bias: bfloat16 [768], P(('dp', 'seq')), may hold values from -3 to 3
- key_weight: bfloat16 [768, 768], P(('dp', 'seq')), may hold values from -0.21875 to 0.21875
- value_weight: bfloat16 [768, 768], P(('dp', 'seq')), may hold values from -0.21875 to 0.21875
- value_bias: bfloat16 [768], P(('dp', 'seq')), may hold values from -3 to 3
- attn_out_weight: bfloat16 [768, 768], P(('dp', 'seq')), may hold values from -0.875 to 0.875
- attn_out_bias: bfloat16 [768], P(('dp', 'seq')), may hold values from -3 to 3
- cross_gain: bfloat16 [768], P(('dp', 'seq')), may hold values from 0.25 to 1.75
- cross_shift: bfloat16 [768], P(('dp', 'seq')), may hold values from -3 to 3
- cross_query_weight: bfloat16 [768, 768], P(('dp', 'seq')), may hold values from -0.21875 to 0.21875
- cross_query_bias: bfloat16 [768], P(('dp', 'seq')), may hold values from -3 to 3
- cross_key_weight: bfloat16 [768, 768], P(('dp', 'seq')), may hold values from -0.21875 to 0.21875
- cross_value_weight: bfloat16 [768, 768], P(('dp', 'seq')), may hold values from -0.21875 to 0.21875
- cross_value_bias: bfloat16 [768], P(('dp', 'seq')), may hold values from -3 to 3
- cross_out_weight: bfloat16 [768, 768], P(('dp', 'seq')), may hold values from -0.875 to 0.875
- cross_out_bias: bfloat16 [768], P(('dp', 'seq')), may hold values from -3 to 3
- mlp_gain: bfloat16 [768], P(('dp', 'seq')), may hold values from 0.25 to 1.75
- mlp_shift: bfloat16 [768], P(('dp', 'seq')), may hold values from -3 to 3
- fc_in_weight: bfloat16 [768, 3072], P(('dp', 'seq')), may hold values from -0.21875 to 0.21875
- fc_in_bias: bfloat16 [3072], P(('dp', 'seq')), may hold values from -3 to 3
- fc_out_weight: bfloat16 [3072, 768], P(('dp', 'seq')), may hold values from -0.109375 to 0.109375
- fc_out_bias: bfloat16 [768], P(('dp', 'seq')), may hold values from -3 to 3
- out_grad: float32 [2048, 4, 768], P('seq', 'dp'), may hold values from -6 to 6
Outputs:
- output: bfloat16 [2048, 4, 768], P('seq', 'dp')
- token_grad: float32 [2048, 4, 768], P('seq', 'dp')
- memory_grad: float32 [1536, 4, 768], P(None, 'dp')
- grad_self_gain: float32 [768], P(('dp', 'seq'))
- grad_self_shift: float32 [768], P(('dp', 'seq'))
- grad_query_weight: float32 [768, 768], P(('dp', 'seq'))
- grad_query_bias: float32 [768], P(('dp', 'seq'))
- grad_key_weight: float32 [768, 768], P(('dp', 'seq'))
- grad_value_weight: float32 [768, 768], P(('dp', 'seq'))
- grad_value_bias: float32 [768], P(('dp', 'seq'))
- grad_attn_out_weight: float32 [768, 768], P(('dp', 'seq'))
- grad_attn_out_bias: float32 [768], P(('dp', 'seq'))
- grad_cross_gain: float32 [768], P(('dp', 'seq'))
- grad_cross_shift: float32 [768], P(('dp', 'seq'))
- grad_cross_query_weight: float32 [768, 768], P(('dp', 'seq'))
- grad_cross_query_bias: float32 [768], P(('dp', 'seq'))
- grad_cross_key_weight: float32 [768, 768], P(('dp', 'seq'))
- grad_cross_value_weight: float32 [768, 768], P(('dp', 'seq'))
- grad_cross_value_bias: float32 [768], P(('dp', 'seq'))
- grad_cross_out_weight: float32 [768, 768], P(('dp', 'seq'))
- grad_cross_out_bias: float32 [768], P(('dp', 'seq'))
- grad_mlp_gain: float32 [768], P(('dp', 'seq'))
- grad_mlp_shift: float32 [768], P(('dp', 'seq'))
- grad_fc_in_weight: float32 [768, 3072], P(('dp', 'seq'))
- grad_fc_in_bias: float32 [3072], P(('dp', 'seq'))
- grad_fc_out_weight: float32 [3072, 768], P(('dp', 'seq'))
- grad_fc_out_bias: float32 [768], P(('dp', 'seq'))
The draws below stay inside these ranges and needn't reach their ends.
Inputs may be any that keep to these rules, and one draw needn't show every extreme that they name: `piece_starts`: each sequence has 3 audio-prompt pieces of 256 positions; each starts at a multiple of 128, the pieces of one sequence don't intersect and each lies inside the sequence. `memory_lengths`: frames at or beyond a sequence's length are padding; some sequence uses all 1536 frames.
All inputs are finite; a program needn't handle non-finite values.
Results may differ from the reference program's by a relative error of at most 0.035.
Values may be sent and summed in bfloat16 or wider, within the bound.
No kernel may reach another device: no remote copies, remote signals or barrier semaphores. Data moves between devices by JAX's collectives and lax.ppermute only.
A program may use at most 256 MiB of HBM per device.

```python
import math
import jax
import jax.numpy as jnp
from jax import lax

D = 768
HEADS = 12
HEAD = 64
FF = 3072
MEM = 1536
PIECE = 256
PIECES = 3
SEQ_LEN = 2048
SEQS = 4


def draw_piece_starts(key, part):
    slot_count = SEQ_LEN // (2 * PIECE)
    seq_keys = jax.random.split(key, SEQS)

    def draw_one(seq_key):
        perm_key, offset_key = jax.random.split(seq_key)
        chosen = jax.random.permutation(perm_key, slot_count - 1)[:PIECES]
        offset = jax.random.randint(offset_key, (PIECES,), 0, 3)
        return chosen * (2 * PIECE) + offset * (PIECE // 2)
    starts = jax.vmap(draw_one)(seq_keys).astype(jnp.int32)
    return starts.at[0, 0].set(SEQ_LEN - PIECE)


def draw_memory_lengths(key, part):
    length_key = jax.random.fold_in(key, 11)
    pick_key = jax.random.fold_in(key, 12)
    lengths = jax.random.randint(length_key, (SEQS,), MEM // 4, MEM + 1)
    chosen = jax.random.randint(pick_key, (), 0, SEQS)
    return jnp.where(jnp.arange(SEQS) == chosen, MEM, lengths).astype(jnp.int32)


def steps_of(own_key, shape, pieces, low, high):
    level = 1.0
    for dim, blocks in pieces:
        heights = jax.random.uniform(jax.random.fold_in(jax.random.fold_in(own_key, 6), dim), (blocks,), jnp.float32, low / len(pieces), high / len(pieces))
        level = level * jnp.repeat(jnp.exp(heights), shape[dim] // blocks).reshape((-1,) + (1,) * (len(shape) - 1 - dim))
    return level


def centred(key, shape, deviation, limit, pieces=(), kind=jnp.bfloat16):
    entries = deviation * jax.random.normal(key, shape, jnp.float32)
    if pieces:
        entries = entries * steps_of(key, shape, pieces, -0.22, 0.18)
    return jnp.clip(entries, -limit, limit).astype(kind)


def setup_inputs(seed: int = 0) -> dict:
    seeds = jax.random.split(jax.random.key(seed), 30)
    tokens = centred(seeds[0], (SEQ_LEN, SEQS, D), 1.0, 6.0, ((0, 8), (1, 4)))
    memory = centred(seeds[1], (MEM, SEQS, D), 1.0, 6.0, ((1, 4),))
    piece_starts = draw_piece_starts(jax.random.fold_in(seeds[29], 71), 0)
    memory_lengths = draw_memory_lengths(jax.random.fold_in(seeds[29], 71), 0)
    self_gain = jnp.clip(1.0 + 0.15 * jax.random.normal(seeds[4], (D,), jnp.float32), 0.25, 1.75).astype(jnp.bfloat16)
    self_shift = centred(seeds[5], (D,), 0.5, 3.0, ((0, 32),))
    query_weight = centred(seeds[6], (D, D), D ** -0.5, 0.21875, ((0, 32),))
    query_bias = centred(seeds[7], (D,), 0.5, 3.0, ((0, 32),))
    key_weight = centred(seeds[8], (D, D), D ** -0.5, 0.21875, ((0, 32),))
    value_weight = centred(seeds[9], (D, D), D ** -0.5, 0.21875, ((0, 32),))
    value_bias = centred(seeds[10], (D,), 0.5, 3.0, ((0, 32),))
    attn_out_weight = centred(seeds[11], (D, D), (D // 16) ** -0.5, 0.875, ((0, 32),))
    attn_out_bias = centred(seeds[12], (D,), 0.5, 3.0, ((0, 32),))
    cross_gain = jnp.clip(1.0 + 0.15 * jax.random.normal(seeds[13], (D,), jnp.float32), 0.25, 1.75).astype(jnp.bfloat16)
    cross_shift = centred(seeds[14], (D,), 0.5, 3.0, ((0, 32),))
    cross_query_weight = centred(seeds[15], (D, D), D ** -0.5, 0.21875, ((0, 32),))
    cross_query_bias = centred(seeds[16], (D,), 0.5, 3.0, ((0, 32),))
    cross_key_weight = centred(seeds[17], (D, D), D ** -0.5, 0.21875, ((0, 32),))
    cross_value_weight = centred(seeds[18], (D, D), D ** -0.5, 0.21875, ((0, 32),))
    cross_value_bias = centred(seeds[19], (D,), 0.5, 3.0, ((0, 32),))
    cross_out_weight = centred(seeds[20], (D, D), (D // 16) ** -0.5, 0.875, ((0, 32),))
    cross_out_bias = centred(seeds[21], (D,), 0.5, 3.0, ((0, 32),))
    mlp_gain = jnp.clip(1.0 + 0.15 * jax.random.normal(seeds[22], (D,), jnp.float32), 0.25, 1.75).astype(jnp.bfloat16)
    mlp_shift = centred(seeds[23], (D,), 0.5, 3.0, ((0, 32),))
    fc_in_weight = centred(seeds[24], (D, FF), D ** -0.5, 0.21875, ((0, 32),))
    fc_in_bias = centred(seeds[25], (FF,), 0.5, 3.0, ((0, 32),))
    fc_out_weight = centred(seeds[26], (FF, D), FF ** -0.5, 0.109375, ((0, 32),))
    fc_out_bias = centred(seeds[27], (D,), 0.5, 3.0, ((0, 32),))
    out_grad = centred(seeds[28], (SEQ_LEN, SEQS, D), 1.0, 6.0, ((0, 8), (1, 4)), jnp.float32)
    return {"tokens": tokens, "memory": memory, "piece_starts": piece_starts, "memory_lengths": memory_lengths, "self_gain": self_gain, "self_shift": self_shift, "query_weight": query_weight, "query_bias": query_bias, "key_weight": key_weight, "value_weight": value_weight, "value_bias": value_bias, "attn_out_weight": attn_out_weight, "attn_out_bias": attn_out_bias, "cross_gain": cross_gain, "cross_shift": cross_shift, "cross_query_weight": cross_query_weight, "cross_query_bias": cross_query_bias, "cross_key_weight": cross_key_weight, "cross_value_weight": cross_value_weight, "cross_value_bias": cross_value_bias, "cross_out_weight": cross_out_weight, "cross_out_bias": cross_out_bias, "mlp_gain": mlp_gain, "mlp_shift": mlp_shift, "fc_in_weight": fc_in_weight, "fc_in_bias": fc_in_bias, "fc_out_weight": fc_out_weight, "fc_out_bias": fc_out_bias, "out_grad": out_grad}


@jax.custom_vjp
def low(v):
    return lax.optimization_barrier(v.astype(jnp.bfloat16)).astype(jnp.float32)

@jax.custom_vjp
def low_back(v):
    return v

def low_keep(v):
    return (low(v), None)

def low_pass(kept, grad):
    return (grad,)

def back_keep(v):
    return (v, None)

def back_low(kept, grad):
    return (low(grad),)
low.defvjp(low_keep, low_pass)
low_back.defvjp(back_keep, back_low)
highest = lax.Precision.HIGHEST
norm_epsilon = 1e-05
neg_large = -1e+30

def matmul(left_rows, matrix):
    return jnp.matmul(left_rows, matrix, precision=highest)

def layer_norm(token_rows, norm_gain, norm_shift):
    centre = token_rows - lax.optimization_barrier(jnp.mean(token_rows, axis=-1, keepdims=True))
    variance = lax.optimization_barrier(jnp.mean(centre * centre, axis=-1, keepdims=True))
    return centre * lax.rsqrt(variance + norm_epsilon) * norm_gain + norm_shift

def split_heads(token_rows):
    return jnp.transpose(token_rows.reshape(token_rows.shape[0], HEADS, HEAD), (1, 0, 2))

def attention(queries, keys_heads, values_heads, visible_fn):
    length = queries.shape[1]
    block_rows = math.gcd(length, 512)

    def one_block(block_start):
        query_block = lax.dynamic_slice_in_dim(queries, block_start, block_rows, 1)
        raw_scores = jnp.einsum('hqd,hkd->hqk', query_block, keys_heads, precision=highest)
        scores = low_back(raw_scores) * 0.125
        allowed = visible_fn(block_start, block_rows)[None]
        row_max = lax.optimization_barrier(jnp.max(jnp.where(allowed, scores, neg_large), axis=-1, keepdims=True))
        exp_terms = jnp.where(allowed, jnp.exp(scores - row_max), 0.0)
        attn_probs = exp_terms / lax.optimization_barrier(jnp.sum(exp_terms, axis=-1, keepdims=True))
        return jnp.einsum('hqk,hkd->hqd', low(attn_probs), values_heads, precision=highest)
    block_starts = jnp.arange(length // block_rows, dtype=jnp.int32) * block_rows
    blocks = lax.map(jax.checkpoint(one_block), block_starts)
    return jnp.transpose(blocks, (0, 2, 1, 3)).reshape(length, HEADS * HEAD)

def forward_one(params, token_rows, memory_rows, labels, length):
    self_gain, self_shift, query_weight, query_bias, key_weight, value_weight, value_bias, attn_out_weight, attn_out_bias, cross_gain, cross_shift, cross_query_weight, cross_query_bias, cross_key_weight, cross_value_weight, cross_value_bias, cross_out_weight, cross_out_bias, mlp_gain, mlp_shift, fc_in_weight, fc_in_bias, fc_out_weight, fc_out_bias = params
    positions = jnp.arange(token_rows.shape[0], dtype=jnp.int32)
    frame_index = jnp.arange(memory_rows.shape[0], dtype=jnp.int32)

    def self_visible(block_start, block_rows):
        query_pos = block_start + jnp.arange(block_rows, dtype=jnp.int32)
        query_label = lax.dynamic_slice_in_dim(labels, block_start, block_rows, 0)
        causal = positions[None, :] <= query_pos[:, None]
        same_piece = (query_label[:, None] == labels[None, :]) & (query_label[:, None] > 0)
        return causal | same_piece

    def cross_visible(block_start, block_rows):
        return jnp.broadcast_to(frame_index[None, :] < length, (block_rows, frame_index.shape[0]))
    normed = low(layer_norm(token_rows, self_gain, self_shift))
    queries = low(low_back(matmul(normed, query_weight) + query_bias))
    keys_rows = low(low_back(matmul(normed, key_weight)))
    values_rows = low(low_back(matmul(normed, value_weight) + value_bias))
    attended = attention(split_heads(queries), split_heads(keys_rows), split_heads(values_rows), self_visible)
    branch = low_back(matmul(low(low_back(attended)), attn_out_weight) + attn_out_bias)
    middle = token_rows + branch
    normed = low(layer_norm(middle, cross_gain, cross_shift))
    cross_queries = low(low_back(matmul(normed, cross_query_weight) + cross_query_bias))
    memory_keys = low(low_back(matmul(memory_rows, cross_key_weight)))
    memory_values = low(low_back(matmul(memory_rows, cross_value_weight) + cross_value_bias))
    attended = attention(split_heads(cross_queries), split_heads(memory_keys), split_heads(memory_values), cross_visible)
    branch = low_back(matmul(low(low_back(attended)), cross_out_weight) + cross_out_bias)
    after = middle + branch
    normed = low(layer_norm(after, mlp_gain, mlp_shift))
    hidden = low_back(matmul(normed, fc_in_weight) + fc_in_bias)
    activated = low(jax.nn.gelu(hidden, approximate=False))
    return after + low_back(matmul(activated, fc_out_weight) + fc_out_bias)

def reference(tokens, memory, piece_starts, memory_lengths, self_gain, self_shift, query_weight, query_bias, key_weight, value_weight, value_bias, attn_out_weight, attn_out_bias, cross_gain, cross_shift, cross_query_weight, cross_query_bias, cross_key_weight, cross_value_weight, cross_value_bias, cross_out_weight, cross_out_bias, mlp_gain, mlp_shift, fc_in_weight, fc_in_bias, fc_out_weight, fc_out_bias, out_grad):
    weights = tuple((matrix.astype(jnp.float32) for matrix in (self_gain, self_shift, query_weight, query_bias, key_weight, value_weight, value_bias, attn_out_weight, attn_out_bias, cross_gain, cross_shift, cross_query_weight, cross_query_bias, cross_key_weight, cross_value_weight, cross_value_bias, cross_out_weight, cross_out_bias, mlp_gain, mlp_shift, fc_in_weight, fc_in_bias, fc_out_weight, fc_out_bias)))
    positions = jnp.arange(SEQ_LEN, dtype=jnp.int32)
    inside = (positions[None, :, None] >= piece_starts[:, None, :]) & (positions[None, :, None] < piece_starts[:, None, :] + PIECE)
    labels = lax.optimization_barrier(jnp.sum(jnp.where(inside, jnp.arange(1, PIECES + 1, dtype=jnp.int32), 0), axis=2)).astype(jnp.int32)

    def one_sequence(totals, scan_items):
        token_rows, memory_rows, label_row, length, cotangent = scan_items

        def forward(params, rows_in, memory_in):
            return forward_one(params, rows_in, memory_in, label_row, length)
        result, pullback = jax.vjp(forward, weights, token_rows, memory_rows)
        grad_params, grad_rows, grad_memory = pullback(cotangent)
        totals = jax.tree.map(jnp.add, totals, grad_params)
        return (totals, (result.astype(jnp.bfloat16), grad_rows, grad_memory))
    zero_grads = tuple((jnp.zeros_like(matrix) for matrix in weights))
    scan_items = (jnp.transpose(tokens, (1, 0, 2)).astype(jnp.float32), jnp.transpose(memory, (1, 0, 2)).astype(jnp.float32), labels, memory_lengths, jnp.transpose(out_grad, (1, 0, 2)).astype(jnp.float32))
    totals, (outputs, token_grads, memory_grads) = lax.scan(one_sequence, zero_grads, scan_items)
    grad_self_gain, grad_self_shift, grad_query_weight, grad_query_bias, grad_key_weight, grad_value_weight, grad_value_bias, grad_attn_out_weight, grad_attn_out_bias, grad_cross_gain, grad_cross_shift, grad_cross_query_weight, grad_cross_query_bias, grad_cross_key_weight, grad_cross_value_weight, grad_cross_value_bias, grad_cross_out_weight, grad_cross_out_bias, grad_mlp_gain, grad_mlp_shift, grad_fc_in_weight, grad_fc_in_bias, grad_fc_out_weight, grad_fc_out_bias = totals
    return (jnp.transpose(outputs, (1, 0, 2)), jnp.transpose(token_grads, (1, 0, 2)), jnp.transpose(memory_grads, (1, 0, 2)), grad_self_gain, grad_self_shift, grad_query_weight, grad_query_bias, grad_key_weight, grad_value_weight, grad_value_bias, grad_attn_out_weight, grad_attn_out_bias, grad_cross_gain, grad_cross_shift, grad_cross_query_weight, grad_cross_query_bias, grad_cross_key_weight, grad_cross_value_weight, grad_cross_value_bias, grad_cross_out_weight, grad_cross_out_bias, grad_mlp_gain, grad_mlp_shift, grad_fc_in_weight, grad_fc_in_bias, grad_fc_out_weight, grad_fc_out_bias)
```

```python
import math

import jax
import jax.numpy as jnp
from jax import lax
from jax.sharding import PartitionSpec as P

D = 768
HEADS = 12
HEAD = 64
PIECE = 256


norm_epsilon = 1e-05
neg_large = -1e30


def rounded(tensor):
    return tensor.astype(jnp.bfloat16)


def project(left_rows, matrix):
    return jnp.dot(left_rows, matrix, preferred_element_type=jnp.float32)


def project_back(left_rows, matrix):
    return lax.dot_general(
        left_rows, matrix, (((1,), (1,)), ((), ())), preferred_element_type=jnp.float32
    )


def weight_grad(inputs, grad_rows):
    return lax.dot_general(
        inputs, grad_rows, (((0,), (0,)), ((), ())), preferred_element_type=jnp.float32
    )


def column_sums(grad_rows):
    return jnp.sum(grad_rows.astype(jnp.float32), axis=0)


def exact_gelu(inputs):
    return jax.nn.gelu(inputs, approximate=False)


def norm_forward(token_rows, norm_gain, norm_shift):
    centre = token_rows - jnp.mean(token_rows, axis=-1, keepdims=True)
    inverse = lax.rsqrt(jnp.mean(centre * centre, axis=-1, keepdims=True) + norm_epsilon)
    scaled = centre * inverse
    return (scaled * norm_gain + norm_shift, scaled, inverse)


def norm_backward(grad_normed, scaled, inverse, norm_gain):
    grad_scaled = grad_normed * norm_gain
    mean_grad = jnp.mean(grad_scaled, axis=-1, keepdims=True)
    mean_cross = jnp.mean(grad_scaled * scaled, axis=-1, keepdims=True)
    grad_input = inverse * (grad_scaled - mean_grad - scaled * mean_cross)
    return (grad_input, jnp.sum(grad_normed * scaled, axis=0), jnp.sum(grad_normed, axis=0))


def piece_labels(positions, starts):
    inside = (positions[None, :, None] >= starts[:, None, :]) & (
        positions[None, :, None] < starts[:, None, :] + PIECE
    )
    numbers = jnp.arange(1, starts.shape[1] + 1, dtype=jnp.int32)
    return jnp.sum(jnp.where(inside, numbers, 0), axis=2)


def visible(query_pos, query_label, key_pos, key_label):
    causal = (key_pos[None, :] <= query_pos[:, None])[:, None, :]
    query_side = jnp.transpose(query_label)[:, :, None]
    same_piece = (query_side == key_label[None, :, :]) & (query_side > 0)
    return (causal | same_piece)[:, :, None, :]


def local(
    tokens,
    memory,
    piece_starts,
    memory_lengths,
    self_gain,
    self_shift,
    query_weight,
    query_bias,
    key_weight,
    value_weight,
    value_bias,
    attn_out_weight,
    attn_out_bias,
    cross_gain,
    cross_shift,
    cross_query_weight,
    cross_query_bias,
    cross_key_weight,
    cross_value_weight,
    cross_value_bias,
    cross_out_weight,
    cross_out_bias,
    mlp_gain,
    mlp_shift,
    fc_in_weight,
    fc_in_bias,
    fc_out_weight,
    fc_out_bias,
    out_grad,
):
    local_len, batch_count, model_width = tokens.shape
    seq_count = lax.axis_size("seq")
    seq_index = lax.axis_index("seq")
    full_length = local_len * seq_count
    token_count = local_len * batch_count
    query_pos = seq_index * local_len + jnp.arange(local_len, dtype=jnp.int32)
    query_label = piece_labels(query_pos, piece_starts)
    input_rows = tokens.reshape(token_count, D).astype(jnp.float32)
    shard_rows = query_weight.shape[0]
    wide_parts = fc_in_weight.shape[1] // D
    vectors = jnp.concatenate(
        (
            self_gain,
            self_shift,
            query_bias,
            value_bias,
            attn_out_bias,
            cross_gain,
            cross_shift,
            cross_query_bias,
            cross_value_bias,
            cross_out_bias,
            mlp_gain,
            mlp_shift,
            fc_out_bias,
            fc_in_bias,
        )
    )
    vector_rows = 8
    vector_block = jnp.pad(vectors, (0, vector_rows * D - vectors.shape[0])).reshape(vector_rows, D)
    fc_in_blocks = jnp.transpose(
        fc_in_weight.reshape(shard_rows, wide_parts, D), (1, 0, 2)
    ).reshape(wide_parts * shard_rows, D)
    packed = jnp.concatenate(
        (
            query_weight,
            key_weight,
            value_weight,
            attn_out_weight,
            cross_query_weight,
            cross_key_weight,
            cross_value_weight,
            cross_out_weight,
            fc_in_blocks,
            fc_out_weight,
            vector_block,
        )
    )
    gathered = lax.all_gather(packed, ("dp", "seq"), axis=0, tiled=False)
    owners = gathered.shape[0]

    def square_at(slot):
        return gathered[:, slot * shard_rows : (slot + 1) * shard_rows, :].reshape(D, D)

    full_query, full_key, full_value, full_self_out = (square_at(slot) for slot in range(4))
    full_cross_query, full_cross_key, full_cross_value, full_cross_out = (
        square_at(slot) for slot in range(4, 8)
    )
    wide_start = 8 * shard_rows
    wide_stop = wide_start + wide_parts * shard_rows
    full_fc_in = jnp.transpose(
        gathered[:, wide_start:wide_stop, :].reshape(owners, wide_parts, shard_rows, D),
        (0, 2, 1, 3),
    ).reshape(D, wide_parts * D)
    out_stop = wide_stop + fc_out_weight.shape[0]
    full_fc_out = gathered[:, wide_stop:out_stop, :].reshape(wide_parts * D, D)
    full_vectors = gathered[:, out_stop:, :].reshape(owners, vector_rows * D)

    def vector_at(slot):
        return full_vectors[:, slot * shard_rows : (slot + 1) * shard_rows].reshape(D)

    (
        full_self_gain,
        full_self_shift,
        full_query_bias,
        full_value_bias,
        full_self_out_bias,
        full_cross_gain,
        full_cross_shift,
        full_cross_query_bias,
        full_cross_value_bias,
        full_cross_out_bias,
        full_mlp_gain,
        full_mlp_shift,
        full_fc_out_bias,
    ) = (vector_at(slot) for slot in range(13))
    full_fc_in_bias = full_vectors[
        :, 13 * shard_rows : 13 * shard_rows + fc_in_bias.shape[0]
    ].reshape(-1)
    normed_self, scaled_self, inverse_self = norm_forward(
        input_rows, full_self_gain.astype(jnp.float32), full_self_shift.astype(jnp.float32)
    )
    normed_self_low = rounded(normed_self)
    query_rows = rounded(project(normed_self_low, full_query) + full_query_bias.astype(jnp.float32))
    key_rows = rounded(project(normed_self_low, full_key)).reshape(local_len, batch_count, D)
    value_rows = rounded(
        project(normed_self_low, full_value) + full_value_bias.astype(jnp.float32)
    ).reshape(local_len, batch_count, D)
    query_heads = query_rows.reshape(local_len, batch_count, HEADS, HEAD)

    def key_block_scores(key_block, key_pos):
        key_heads = key_block.reshape(key_block.shape[0], batch_count, HEADS, HEAD)
        raw_scores = jnp.einsum(
            "qbhd,kbhd->qbhk", query_heads, key_heads, preferred_element_type=jnp.float32
        )
        allowed = visible(query_pos, query_label, key_pos, piece_labels(key_pos, piece_starts))
        return (raw_scores * 0.125, allowed)

    start_state = (
        jnp.full((local_len, batch_count, HEADS), neg_large, jnp.float32),
        jnp.zeros((local_len, batch_count, HEADS), jnp.float32),
        jnp.zeros((local_len, batch_count, HEADS, HEAD), jnp.float32),
    )
    running = start_state
    kv_piece = lax.all_gather(
        jnp.concatenate((key_rows, value_rows), axis=2), "seq", axis=0, tiled=True
    )
    key_piece = kv_piece[:, :, :D]
    value_piece = kv_piece[:, :, D:]
    block_rows = math.gcd(key_piece.shape[0], 512)

    def fold_block(inner_state, block_index):
        row_max, row_total, weighted_sum = inner_state
        block_start = block_index * block_rows
        key_block = lax.dynamic_slice_in_dim(key_piece, block_start, block_rows, 0)
        value_block = lax.dynamic_slice_in_dim(value_piece, block_start, block_rows, 0).reshape(
            block_rows, batch_count, HEADS, HEAD
        )
        key_pos = block_start + jnp.arange(block_rows, dtype=jnp.int32)
        scores, allowed = key_block_scores(key_block, key_pos)
        new_max = jnp.maximum(row_max, jnp.max(jnp.where(allowed, scores, neg_large), axis=-1))
        exp_terms = jnp.where(allowed, jnp.exp(scores - new_max[..., None]), 0.0)
        factor = jnp.exp(row_max - new_max)
        row_total = row_total * factor + jnp.sum(exp_terms, axis=-1)
        weighted_sum = weighted_sum * factor[..., None] + jnp.einsum(
            "qbhk,kbhd->qbhd", rounded(exp_terms), value_block, preferred_element_type=jnp.float32
        )
        return ((new_max, row_total, weighted_sum), None)

    running, unused = lax.scan(
        fold_block, running, jnp.arange(key_piece.shape[0] // block_rows, dtype=jnp.int32)
    )
    row_max, row_total, weighted_sum = running
    attended_self = weighted_sum / row_total[..., None]
    log_total = row_max + jnp.log(row_total)
    attended_self_low = rounded(attended_self.reshape(token_count, D))
    middle_rows = (
        input_rows
        + project(attended_self_low, full_self_out)
        + full_self_out_bias.astype(jnp.float32)
    )
    normed_cross, scaled_cross, inverse_cross = norm_forward(
        middle_rows, full_cross_gain.astype(jnp.float32), full_cross_shift.astype(jnp.float32)
    )
    normed_cross_low = rounded(normed_cross)
    cross_queries = rounded(
        project(normed_cross_low, full_cross_query) + full_cross_query_bias.astype(jnp.float32)
    ).reshape(local_len, batch_count, HEADS, HEAD)
    frame_count = memory.shape[0]
    frame_part = frame_count // seq_count
    frame_start = seq_index * frame_part
    memory_part = lax.dynamic_slice_in_dim(memory, frame_start, frame_part, 0).reshape(
        frame_part * batch_count, D
    )
    memory_flat = memory.reshape(frame_count * batch_count, D)
    memory_keys = rounded(project(memory_flat, full_cross_key)).reshape(frame_count, batch_count, D)
    memory_values = rounded(
        project(memory_flat, full_cross_value) + full_cross_value_bias.astype(jnp.float32)
    ).reshape(frame_count, batch_count, D)
    memory_key_heads = memory_keys.reshape(frame_count, batch_count, HEADS, HEAD)
    memory_value_heads = memory_values.reshape(frame_count, batch_count, HEADS, HEAD)
    frame_valid = (jnp.arange(frame_count, dtype=jnp.int32)[None, :] < memory_lengths[:, None])[
        None, :, None, :
    ]
    cross_scores = (
        jnp.einsum(
            "qbhd,kbhd->qbhk", cross_queries, memory_key_heads, preferred_element_type=jnp.float32
        )
        * 0.125
    )
    cross_max = jnp.max(jnp.where(frame_valid, cross_scores, neg_large), axis=-1, keepdims=True)
    cross_exp = jnp.where(frame_valid, jnp.exp(cross_scores - cross_max), 0.0)
    cross_probs = cross_exp / jnp.sum(cross_exp, axis=-1, keepdims=True)
    cross_probs_low = rounded(cross_probs)
    attended_cross = jnp.einsum(
        "qbhk,kbhd->qbhd", cross_probs_low, memory_value_heads, preferred_element_type=jnp.float32
    )
    attended_cross_low = rounded(attended_cross.reshape(token_count, D))
    after_rows = (
        middle_rows
        + project(attended_cross_low, full_cross_out)
        + full_cross_out_bias.astype(jnp.float32)
    )
    normed_mlp, scaled_mlp, inverse_mlp = norm_forward(
        after_rows, full_mlp_gain.astype(jnp.float32), full_mlp_shift.astype(jnp.float32)
    )
    normed_mlp_low = rounded(normed_mlp)
    hidden_pre = project(normed_mlp_low, full_fc_in) + full_fc_in_bias.astype(jnp.float32)
    activated, gelu_pull = jax.vjp(exact_gelu, hidden_pre)
    activated_low = rounded(activated)
    result_rows = (
        after_rows + project(activated_low, full_fc_out) + full_fc_out_bias.astype(jnp.float32)
    )
    output = rounded(result_rows).reshape(local_len, batch_count, D)
    back_fc_in, back_fc_out = full_fc_in, full_fc_out
    grad_result = out_grad.reshape(token_count, D)
    grad_mlp_low = rounded(grad_result)
    grad_fc_out_weight = weight_grad(activated_low, grad_mlp_low)
    grad_fc_out_bias = column_sums(grad_mlp_low)
    grad_activated = project_back(grad_mlp_low, back_fc_out)
    grad_hidden_low = rounded(gelu_pull(grad_activated)[0])
    grad_fc_in_weight = weight_grad(normed_mlp_low, grad_hidden_low)
    grad_fc_in_bias = column_sums(grad_hidden_low)
    grad_normed_mlp = project_back(grad_hidden_low, back_fc_in)
    grad_rows_mlp, grad_mlp_gain, grad_mlp_shift = norm_backward(
        grad_normed_mlp, scaled_mlp, inverse_mlp, full_mlp_gain.astype(jnp.float32)
    )
    early_grads = jnp.concatenate(
        (
            jnp.transpose(
                grad_fc_in_weight.astype(jnp.bfloat16).reshape(
                    owners, shard_rows, wide_parts, D
                ),
                (0, 2, 1, 3),
            ).reshape(owners, wide_parts * shard_rows, D),
            grad_fc_out_weight.astype(jnp.bfloat16).reshape(owners, -1, D),
        ),
        axis=1,
    )
    owned_early = lax.psum_scatter(
        early_grads, ("dp", "seq"), scatter_dimension=0, tiled=False
    ).astype(jnp.float32)
    wide_rows = wide_parts * shard_rows
    owned_fc_in = jnp.transpose(
        owned_early[:wide_rows].reshape(wide_parts, shard_rows, D), (1, 0, 2)
    ).reshape(shard_rows, wide_parts * D)
    owned_fc_out = owned_early[wide_rows:]
    grad_after = grad_result + grad_rows_mlp
    back_cross_query, back_cross_key, back_cross_value, back_cross_out = (
        full_cross_query,
        full_cross_key,
        full_cross_value,
        full_cross_out,
    )
    grad_cross_low = rounded(grad_after)
    grad_cross_out_weight = weight_grad(attended_cross_low, grad_cross_low)
    grad_cross_out_bias = column_sums(grad_cross_low)
    grad_attended_cross = rounded(project_back(grad_cross_low, back_cross_out)).reshape(
        local_len, batch_count, HEADS, HEAD
    )
    grad_cross_probs = jnp.einsum(
        "qbhd,kbhd->qbhk",
        grad_attended_cross,
        memory_value_heads,
        preferred_element_type=jnp.float32,
    )
    cross_delta = jnp.sum(cross_probs * grad_cross_probs, axis=-1, keepdims=True)
    grad_cross_scores = rounded(cross_probs * (grad_cross_probs - cross_delta) * 0.125)
    grad_cross_queries = rounded(
        jnp.einsum(
            "qbhk,kbhd->qbhd",
            grad_cross_scores,
            memory_key_heads,
            preferred_element_type=jnp.float32,
        ).reshape(token_count, D)
    )
    grad_memory_keys = jnp.einsum(
        "qbhk,qbhd->kbhd", grad_cross_scores, cross_queries, preferred_element_type=jnp.float32
    ).reshape(frame_count, batch_count, D)
    grad_memory_values = jnp.einsum(
        "qbhk,qbhd->kbhd", cross_probs_low, grad_attended_cross, preferred_element_type=jnp.float32
    ).reshape(frame_count, batch_count, D)
    grad_memory_kv = jnp.concatenate((grad_memory_keys, grad_memory_values), axis=2)
    grad_cross_query_weight = weight_grad(normed_cross_low, grad_cross_queries)
    grad_cross_query_bias = column_sums(grad_cross_queries)
    grad_normed_cross = project_back(grad_cross_queries, back_cross_query)
    grad_rows_cross, grad_cross_gain, grad_cross_shift = norm_backward(
        grad_normed_cross, scaled_cross, inverse_cross, full_cross_gain.astype(jnp.float32)
    )
    grad_middle = grad_after + grad_rows_cross
    back_query, back_key, back_value, back_self_out = (
        full_query,
        full_key,
        full_value,
        full_self_out,
    )
    grad_self_low = rounded(grad_middle)
    grad_attn_out_weight = weight_grad(attended_self_low, grad_self_low)
    grad_attn_out_bias = column_sums(grad_self_low)
    grad_attended_self = rounded(project_back(grad_self_low, back_self_out)).reshape(
        local_len, batch_count, HEADS, HEAD
    )
    self_delta = jnp.sum(grad_attended_self.astype(jnp.float32) * attended_self, axis=-1)

    def score_grads(key_block, value_block, key_pos):
        scores, allowed = key_block_scores(key_block, key_pos)
        attn_probs = jnp.where(allowed, jnp.exp(scores - log_total[..., None]), 0.0)
        grad_probs = jnp.einsum(
            "qbhd,kbhd->qbhk", grad_attended_self, value_block, preferred_element_type=jnp.float32
        )
        grad_scores = rounded(attn_probs * (grad_probs - self_delta[..., None]) * 0.125)
        return (grad_scores, attn_probs)

    zero_query_grad = jnp.zeros((local_len, batch_count, HEADS, HEAD), jnp.float32)
    back_state = (zero_query_grad, jnp.zeros((full_length, batch_count, 2 * D), jnp.float32))
    running = back_state
    self_key_piece = key_piece
    self_value_piece = value_piece
    self_block_rows = math.gcd(self_key_piece.shape[0], 512)

    def back_block(inner_state, block_index):
        grad_query_sum, kv_grads = inner_state
        block_start = block_index * self_block_rows
        key_block = lax.dynamic_slice_in_dim(self_key_piece, block_start, self_block_rows, 0)
        value_block = lax.dynamic_slice_in_dim(
            self_value_piece, block_start, self_block_rows, 0
        ).reshape(self_block_rows, batch_count, HEADS, HEAD)
        key_pos = block_start + jnp.arange(self_block_rows, dtype=jnp.int32)
        grad_scores, attn_probs = score_grads(key_block, value_block, key_pos)
        key_heads = key_block.reshape(self_block_rows, batch_count, HEADS, HEAD)
        grad_query_sum = grad_query_sum + jnp.einsum(
            "qbhk,kbhd->qbhd", grad_scores, key_heads, preferred_element_type=jnp.float32
        )
        grad_key_block = jnp.einsum(
            "qbhk,qbhd->kbhd", grad_scores, query_heads, preferred_element_type=jnp.float32
        ).reshape(self_block_rows, batch_count, D)
        grad_value_block = jnp.einsum(
            "qbhk,qbhd->kbhd",
            rounded(attn_probs),
            grad_attended_self,
            preferred_element_type=jnp.float32,
        ).reshape(self_block_rows, batch_count, D)
        kv_grads = lax.dynamic_update_slice_in_dim(
            kv_grads, jnp.concatenate((grad_key_block, grad_value_block), axis=2), block_start, 0
        )
        return ((grad_query_sum, kv_grads), None)

    running, unused = lax.scan(
        back_block, running, jnp.arange(self_key_piece.shape[0] // self_block_rows, dtype=jnp.int32)
    )
    grad_query_sum = running[0]
    joint_kv = jnp.concatenate(
        (
            running[1].astype(jnp.bfloat16).reshape(seq_count, local_len, batch_count, 2 * D),
            grad_memory_kv.astype(jnp.bfloat16).reshape(
                seq_count, frame_part, batch_count, 2 * D
            ),
        ),
        axis=1,
    )
    own_joint = lax.psum_scatter(joint_kv, "seq", scatter_dimension=0, tiled=False)
    own_kv = own_joint[:local_len]
    part_kv = own_joint[local_len:]
    grad_key_low = own_kv[:, :, :D].reshape(token_count, D)
    grad_value_low = own_kv[:, :, D:].reshape(token_count, D)
    part_flat_keys = part_kv[:, :, :D].reshape(frame_part * batch_count, D)
    part_flat_values = part_kv[:, :, D:].reshape(frame_part * batch_count, D)
    part_memory_grad = (
        project_back(part_flat_keys, back_cross_key)
        + project_back(part_flat_values, back_cross_value)
    ).reshape(frame_part, batch_count, D)
    grad_cross_key_weight = weight_grad(memory_part, part_flat_keys)
    grad_cross_value_weight = weight_grad(memory_part, part_flat_values)
    grad_cross_value_bias = column_sums(part_flat_values)
    grad_query_low = rounded(grad_query_sum.reshape(token_count, D))
    grad_query_weight = weight_grad(normed_self_low, grad_query_low)
    grad_query_bias = column_sums(grad_query_low)
    grad_key_weight = weight_grad(normed_self_low, grad_key_low)
    grad_value_weight = weight_grad(normed_self_low, grad_value_low)
    grad_value_bias = column_sums(grad_value_low)
    grad_normed_self = (
        project_back(grad_query_low, back_query)
        + project_back(grad_key_low, back_key)
        + project_back(grad_value_low, back_value)
    )
    grad_rows_self, grad_self_gain, grad_self_shift = norm_backward(
        grad_normed_self, scaled_self, inverse_self, full_self_gain.astype(jnp.float32)
    )
    token_grad = (grad_middle + grad_rows_self).reshape(local_len, batch_count, D)
    def owner_rows(matrix):
        return matrix.astype(jnp.bfloat16).reshape(owners, -1, D)

    late_vectors = jnp.concatenate(
        tuple(
            vector.reshape(owners, -1)
            for vector in (
                grad_self_gain,
                grad_self_shift,
                grad_query_bias,
                grad_value_bias,
                grad_attn_out_bias,
                grad_cross_gain,
                grad_cross_shift,
                grad_cross_query_bias,
                grad_cross_value_bias,
                grad_cross_out_bias,
                grad_mlp_gain,
                grad_mlp_shift,
                grad_fc_out_bias,
                grad_fc_in_bias,
            )
        ),
        axis=1,
    )
    late_block = jnp.pad(
        late_vectors.astype(jnp.bfloat16),
        ((0, 0), (0, vector_rows * D - late_vectors.shape[1])),
    ).reshape(owners, vector_rows, D)
    late_grads = jnp.concatenate(
        (
            owner_rows(grad_query_weight),
            owner_rows(grad_key_weight),
            owner_rows(grad_value_weight),
            owner_rows(grad_attn_out_weight),
            owner_rows(grad_cross_query_weight),
            owner_rows(grad_cross_key_weight),
            owner_rows(grad_cross_value_weight),
            owner_rows(grad_cross_out_weight),
            late_block,
        ),
        axis=1,
    )
    owned_late = lax.psum_scatter(
        late_grads, ("dp", "seq"), scatter_dimension=0, tiled=False
    ).astype(jnp.float32)
    memory_grad = lax.all_gather(
        part_memory_grad.astype(jnp.bfloat16), "seq", axis=0, tiled=True
    ).astype(jnp.float32)
    owned_vectors = owned_late[8 * shard_rows :].reshape(-1)

    def own_square(slot):
        return owned_late[slot * shard_rows : (slot + 1) * shard_rows]

    def own_vector(slot):
        return owned_vectors[slot * shard_rows : (slot + 1) * shard_rows]

    owned_fc_in_bias = owned_vectors[13 * shard_rows : 13 * shard_rows + fc_in_bias.shape[0]]
    return (
        output,
        token_grad,
        memory_grad,
        own_vector(0),
        own_vector(1),
        own_square(0),
        own_vector(2),
        own_square(1),
        own_square(2),
        own_vector(3),
        own_square(3),
        own_vector(4),
        own_vector(5),
        own_vector(6),
        own_square(4),
        own_vector(7),
        own_square(5),
        own_square(6),
        own_vector(8),
        own_square(7),
        own_vector(9),
        own_vector(10),
        own_vector(11),
        owned_fc_in,
        owned_fc_in_bias,
        owned_fc_out,
        own_vector(12),
    )


def solution(mesh):
    in_specs = (
        P("seq", "dp", None),
        P(None, "dp", None),
        P("dp", None),
        P("dp"),
        P(("dp", "seq")),
        P(("dp", "seq")),
        P(("dp", "seq"), None),
        P(("dp", "seq")),
        P(("dp", "seq"), None),
        P(("dp", "seq"), None),
        P(("dp", "seq")),
        P(("dp", "seq"), None),
        P(("dp", "seq")),
        P(("dp", "seq")),
        P(("dp", "seq")),
        P(("dp", "seq"), None),
        P(("dp", "seq")),
        P(("dp", "seq"), None),
        P(("dp", "seq"), None),
        P(("dp", "seq")),
        P(("dp", "seq"), None),
        P(("dp", "seq")),
        P(("dp", "seq")),
        P(("dp", "seq")),
        P(("dp", "seq"), None),
        P(("dp", "seq")),
        P(("dp", "seq"), None),
        P(("dp", "seq")),
        P("seq", "dp", None),
    )
    out_specs = (
        P("seq", "dp", None),
        P("seq", "dp", None),
        P(None, "dp", None),
        P(("dp", "seq")),
        P(("dp", "seq")),
        P(("dp", "seq"), None),
        P(("dp", "seq")),
        P(("dp", "seq"), None),
        P(("dp", "seq"), None),
        P(("dp", "seq")),
        P(("dp", "seq"), None),
        P(("dp", "seq")),
        P(("dp", "seq")),
        P(("dp", "seq")),
        P(("dp", "seq"), None),
        P(("dp", "seq")),
        P(("dp", "seq"), None),
        P(("dp", "seq"), None),
        P(("dp", "seq")),
        P(("dp", "seq"), None),
        P(("dp", "seq")),
        P(("dp", "seq")),
        P(("dp", "seq")),
        P(("dp", "seq"), None),
        P(("dp", "seq")),
        P(("dp", "seq"), None),
        P(("dp", "seq")),
    )
    return jax.shard_map(local, mesh=mesh, in_specs=in_specs, out_specs=out_specs, check_vma=False)
```

```python
import math

import jax
import jax.numpy as jnp
from jax import lax
from jax.experimental import pallas as pl
from jax.experimental.pallas import tpu as pltpu
from jax.sharding import PartitionSpec as P

D = 768
HEADS = 12
HEAD = 64
PIECE = 256


norm_epsilon = 1e-05
neg_large = -1e30


def rounded(tensor):
    return tensor.astype(jnp.bfloat16)


def project(left_rows, matrix):
    return jnp.dot(left_rows, matrix, preferred_element_type=jnp.float32)


def project_back(left_rows, matrix):
    return lax.dot_general(
        left_rows, matrix, (((1,), (1,)), ((), ())), preferred_element_type=jnp.float32
    )


def weight_grad(inputs, grad_rows):
    return lax.dot_general(
        inputs, grad_rows, (((0,), (0,)), ((), ())), preferred_element_type=jnp.float32
    )


def column_sums(grad_rows):
    return jnp.sum(grad_rows.astype(jnp.float32), axis=0)


def exact_gelu(inputs):
    return jax.nn.gelu(inputs, approximate=False)


def norm_forward(token_rows, norm_gain, norm_shift):
    centre = token_rows - jnp.mean(token_rows, axis=-1, keepdims=True)
    inverse = lax.rsqrt(jnp.mean(centre * centre, axis=-1, keepdims=True) + norm_epsilon)
    scaled = centre * inverse
    return (scaled * norm_gain + norm_shift, scaled, inverse)


def norm_backward(grad_normed, scaled, inverse, norm_gain):
    grad_scaled = grad_normed * norm_gain
    mean_grad = jnp.mean(grad_scaled, axis=-1, keepdims=True)
    mean_cross = jnp.mean(grad_scaled * scaled, axis=-1, keepdims=True)
    grad_input = inverse * (grad_scaled - mean_grad - scaled * mean_cross)
    return (grad_input, jnp.sum(grad_normed * scaled, axis=0), jnp.sum(grad_normed, axis=0))


def piece_labels(positions, starts):
    inside = (positions[None, :, None] >= starts[:, None, :]) & (
        positions[None, :, None] < starts[:, None, :] + PIECE
    )
    numbers = jnp.arange(1, starts.shape[1] + 1, dtype=jnp.int32)
    return jnp.sum(jnp.where(inside, numbers, 0), axis=2)


def visible(query_pos, query_label, key_pos, key_label):
    causal = (key_pos[None, :] <= query_pos[:, None])[:, None, :]
    query_side = jnp.transpose(query_label)[:, :, None]
    same_piece = (query_side == key_label[None, :, :]) & (query_side > 0)
    return (causal | same_piece)[:, :, None, :]


PAIR = 2 * HEAD
QUERY_BLOCK = 256


def to_pairs(rows, seq_count):
    blocks = jnp.transpose(rows.reshape(rows.shape[0], D // PAIR, PAIR), (1, 0, 2))
    return jnp.pad(blocks, ((0, seq_count - D // PAIR), (0, 0), (0, 0)))


def from_pairs(blocks):
    kept = blocks[: D // PAIR]
    return jnp.transpose(kept, (1, 0, 2)).reshape(kept.shape[1], D)


def dot_rows(left, right):
    return lax.dot_general(left, right, (((1,), (1,)), ((), ())), preferred_element_type=jnp.float32)


def dot_plain(left, right):
    return lax.dot_general(left, right, (((1,), (0,)), ((), ())), preferred_element_type=jnp.float32)


def dot_columns(left, right):
    return lax.dot_general(left, right, (((0,), (0,)), ((), ())), preferred_element_type=jnp.float32)


def split_pair(block):
    lanes = lax.broadcasted_iota(jnp.int32, block.shape, 1)
    zero = jnp.zeros_like(block)
    return (jnp.where(lanes < HEAD, block, zero), jnp.where(lanes < HEAD, zero, block))


def join_pair(first, second, shape):
    lanes = lax.broadcasted_iota(jnp.int32, shape, 1)
    return jnp.where(lanes < HEAD, first, second)


def block_allowed(query_block, key_block, query_label, key_label):
    shape = (QUERY_BLOCK, QUERY_BLOCK)
    query_pos = query_block * QUERY_BLOCK + lax.broadcasted_iota(jnp.int32, shape, 0)
    key_pos = key_block * QUERY_BLOCK + lax.broadcasted_iota(jnp.int32, shape, 1)
    same_piece = (query_label == key_label) & (query_label > 0)
    return (key_pos <= query_pos) | same_piece


def self_forward_body(query_ref, key_ref, value_ref, column_ref, row_ref, out_ref, log_ref):
    block = pl.program_id(0)
    block_count = pl.num_programs(0)
    query_halves = split_pair(query_ref[...])
    query_label = column_ref[...]

    def step(key_block, state, masked):
        start = pl.multiple_of(key_block * QUERY_BLOCK, QUERY_BLOCK)
        keys = key_ref[pl.ds(start, QUERY_BLOCK), :]
        value_halves = split_pair(value_ref[pl.ds(start, QUERY_BLOCK), :])
        maxima, totals, weighted = state
        new_maxima, new_totals, factors, added = [], [], [], []
        if masked:
            allowed = block_allowed(
                block, key_block, query_label, row_ref[:, pl.ds(start, QUERY_BLOCK)]
            )
        for half in range(2):
            scores = dot_rows(query_halves[half], keys) * 0.125
            if masked:
                scores = jnp.where(allowed, scores, neg_large)
            new_max = jnp.maximum(maxima[half], jnp.max(scores, axis=1, keepdims=True))
            exp_terms = jnp.exp(scores - new_max)
            factor = jnp.exp(maxima[half] - new_max)
            new_maxima.append(new_max)
            new_totals.append(totals[half] * factor + jnp.sum(exp_terms, axis=1, keepdims=True))
            factors.append(factor)
            added.append(dot_plain(rounded(exp_terms), value_halves[half]))
        weighted = weighted * join_pair(factors[0], factors[1], weighted.shape)
        return (tuple(new_maxima), tuple(new_totals), weighted + added[0] + added[1])

    column = (QUERY_BLOCK, 1)
    state = (
        (jnp.full(column, neg_large, jnp.float32),) * 2,
        (jnp.zeros(column, jnp.float32),) * 2,
        jnp.zeros((QUERY_BLOCK, PAIR), jnp.float32),
    )
    state = lax.fori_loop(0, block, lambda index, state: step(index, state, False), state)
    last = jnp.minimum(block + 2, block_count)
    state = lax.fori_loop(block, last, lambda index, state: step(index, state, True), state)
    maxima, totals, weighted = state
    out_ref[...] = weighted / join_pair(totals[0], totals[1], weighted.shape)
    log_ref[...] = join_pair(
        maxima[0] + jnp.log(totals[0]), maxima[1] + jnp.log(totals[1]), weighted.shape
    )


def self_forward(queries, keys, values, labels):
    length = queries.shape[0]
    block_spec = pl.BlockSpec((QUERY_BLOCK, PAIR), lambda index: (index, 0))
    whole_spec = pl.BlockSpec((length, PAIR), lambda index: (0, 0))
    result = jax.ShapeDtypeStruct((length, PAIR), jnp.float32)
    return pl.pallas_call(
        self_forward_body,
        grid=(length // QUERY_BLOCK,),
        in_specs=[
            block_spec,
            whole_spec,
            whole_spec,
            pl.BlockSpec((QUERY_BLOCK, 1), lambda index: (index, 0)),
            pl.BlockSpec((1, length), lambda index: (0, 0)),
        ],
        out_specs=[block_spec, block_spec],
        out_shape=[result, result],
        name="self_forward",
    )(queries, keys, values, labels[:, None], labels[None, :])


def self_backward_body(
    query_ref,
    key_ref,
    value_ref,
    column_ref,
    row_ref,
    out_ref,
    log_ref,
    grad_ref,
    grad_query_ref,
    grad_key_ref,
    grad_value_ref,
    key_sum,
    value_sum,
):
    block = pl.program_id(0)
    block_count = pl.num_programs(0)

    @pl.when(block == 0)
    def clear():
        key_sum[...] = jnp.zeros_like(key_sum)
        value_sum[...] = jnp.zeros_like(value_sum)

    query_halves = split_pair(query_ref[...])
    grad_rows = grad_ref[...]
    grad_halves = split_pair(grad_rows)
    query_label = column_ref[...]
    products = grad_rows.astype(jnp.float32) * out_ref[...]
    deltas = tuple(jnp.sum(part, axis=1, keepdims=True) for part in split_pair(products))
    logs = (log_ref[:, :1], log_ref[:, HEAD : HEAD + 1])

    def step(key_block, query_sum, masked):
        start = pl.multiple_of(key_block * QUERY_BLOCK, QUERY_BLOCK)
        here = pl.ds(start, QUERY_BLOCK)
        keys = key_ref[here, :]
        values = value_ref[here, :]
        key_halves = split_pair(keys)
        if masked:
            allowed = block_allowed(block, key_block, query_label, row_ref[:, here])
        key_add = jnp.zeros((QUERY_BLOCK, PAIR), jnp.float32)
        value_add = jnp.zeros((QUERY_BLOCK, PAIR), jnp.float32)
        for half in range(2):
            scores = dot_rows(query_halves[half], keys) * 0.125
            if masked:
                scores = jnp.where(allowed, scores, neg_large)
            probs = jnp.exp(scores - logs[half])
            grad_probs = dot_rows(grad_halves[half], values)
            grad_scores = rounded(probs * (grad_probs - deltas[half]) * 0.125)
            query_sum = query_sum + dot_plain(grad_scores, key_halves[half])
            key_add = key_add + dot_columns(grad_scores, query_halves[half])
            value_add = value_add + dot_columns(rounded(probs), grad_halves[half])
        key_sum[here, :] = key_sum[here, :] + key_add
        value_sum[here, :] = value_sum[here, :] + value_add
        return query_sum

    query_sum = jnp.zeros((QUERY_BLOCK, PAIR), jnp.float32)
    query_sum = lax.fori_loop(0, block, lambda index, total: step(index, total, False), query_sum)
    last = jnp.minimum(block + 2, block_count)
    query_sum = lax.fori_loop(block, last, lambda index, total: step(index, total, True), query_sum)
    grad_query_ref[...] = rounded(query_sum)

    @pl.when(block == block_count - 1)
    def finish():
        grad_key_ref[...] = rounded(key_sum[...])
        grad_value_ref[...] = rounded(value_sum[...])


def self_backward(queries, keys, values, labels, attended, log_total, grad_attended):
    length = queries.shape[0]
    block_spec = pl.BlockSpec((QUERY_BLOCK, PAIR), lambda index: (index, 0))
    whole_spec = pl.BlockSpec((length, PAIR), lambda index: (0, 0))
    result = jax.ShapeDtypeStruct((length, PAIR), jnp.bfloat16)
    return pl.pallas_call(
        self_backward_body,
        grid=(length // QUERY_BLOCK,),
        in_specs=[
            block_spec,
            whole_spec,
            whole_spec,
            pl.BlockSpec((QUERY_BLOCK, 1), lambda index: (index, 0)),
            pl.BlockSpec((1, length), lambda index: (0, 0)),
            block_spec,
            block_spec,
            block_spec,
        ],
        out_specs=[block_spec, whole_spec, whole_spec],
        out_shape=[result, result, result],
        scratch_shapes=[
            pltpu.VMEM((length, PAIR), jnp.float32),
            pltpu.VMEM((length, PAIR), jnp.float32),
        ],
        name="self_backward",
    )(queries, keys, values, labels[:, None], labels[None, :], attended, log_total, grad_attended)


def local_heads(
    tokens,
    memory,
    piece_starts,
    memory_lengths,
    self_gain,
    self_shift,
    query_weight,
    query_bias,
    key_weight,
    value_weight,
    value_bias,
    attn_out_weight,
    attn_out_bias,
    cross_gain,
    cross_shift,
    cross_query_weight,
    cross_query_bias,
    cross_key_weight,
    cross_value_weight,
    cross_value_bias,
    cross_out_weight,
    cross_out_bias,
    mlp_gain,
    mlp_shift,
    fc_in_weight,
    fc_in_bias,
    fc_out_weight,
    fc_out_bias,
    out_grad,
):
    local_len, batch_count, model_width = tokens.shape
    seq_count = lax.axis_size("seq")
    seq_index = lax.axis_index("seq")
    full_length = local_len * seq_count
    token_count = local_len * batch_count
    query_pos = seq_index * local_len + jnp.arange(local_len, dtype=jnp.int32)
    labels = piece_labels(jnp.arange(full_length, dtype=jnp.int32), piece_starts).reshape(-1)
    input_rows = tokens.reshape(token_count, D).astype(jnp.float32)
    shard_rows = query_weight.shape[0]
    wide_parts = fc_in_weight.shape[1] // D
    vectors = jnp.concatenate(
        (
            self_gain,
            self_shift,
            query_bias,
            value_bias,
            attn_out_bias,
            cross_gain,
            cross_shift,
            cross_query_bias,
            cross_value_bias,
            cross_out_bias,
            mlp_gain,
            mlp_shift,
            fc_out_bias,
            fc_in_bias,
        )
    )
    vector_rows = 8
    vector_block = jnp.pad(vectors, (0, vector_rows * D - vectors.shape[0])).reshape(vector_rows, D)
    fc_in_blocks = jnp.transpose(
        fc_in_weight.reshape(shard_rows, wide_parts, D), (1, 0, 2)
    ).reshape(wide_parts * shard_rows, D)
    first_packed = jnp.concatenate((query_weight, key_weight, value_weight, vector_block))
    first = lax.all_gather(first_packed, ("dp", "seq"), axis=0, tiled=False)
    owners = first.shape[0]

    def first_at(slot):
        return first[:, slot * shard_rows : (slot + 1) * shard_rows, :].reshape(D, D)

    full_query, full_key, full_value = (first_at(slot) for slot in range(3))
    full_vectors = first[:, 3 * shard_rows :, :].reshape(owners, vector_rows * D)
    packed = jnp.concatenate(
        (
            attn_out_weight,
            cross_query_weight,
            cross_key_weight,
            cross_value_weight,
            cross_out_weight,
            fc_in_blocks,
            fc_out_weight,
        )
    )
    packed, first = lax.optimization_barrier((packed, first))
    gathered = lax.all_gather(packed, ("dp", "seq"), axis=0, tiled=False)

    def square_at(slot):
        return gathered[:, slot * shard_rows : (slot + 1) * shard_rows, :].reshape(D, D)

    full_self_out, full_cross_query, full_cross_key, full_cross_value, full_cross_out = (
        square_at(slot) for slot in range(5)
    )
    wide_start = 5 * shard_rows
    wide_stop = wide_start + wide_parts * shard_rows
    full_fc_in = jnp.transpose(
        gathered[:, wide_start:wide_stop, :].reshape(owners, wide_parts, shard_rows, D),
        (0, 2, 1, 3),
    ).reshape(D, wide_parts * D)
    out_stop = wide_stop + fc_out_weight.shape[0]
    full_fc_out = gathered[:, wide_stop:out_stop, :].reshape(wide_parts * D, D)

    def vector_at(slot):
        return full_vectors[:, slot * shard_rows : (slot + 1) * shard_rows].reshape(D)

    (
        full_self_gain,
        full_self_shift,
        full_query_bias,
        full_value_bias,
        full_self_out_bias,
        full_cross_gain,
        full_cross_shift,
        full_cross_query_bias,
        full_cross_value_bias,
        full_cross_out_bias,
        full_mlp_gain,
        full_mlp_shift,
        full_fc_out_bias,
    ) = (vector_at(slot) for slot in range(13))
    full_fc_in_bias = full_vectors[
        :, 13 * shard_rows : 13 * shard_rows + fc_in_bias.shape[0]
    ].reshape(-1)
    normed_self, scaled_self, inverse_self = norm_forward(
        input_rows, full_self_gain.astype(jnp.float32), full_self_shift.astype(jnp.float32)
    )
    normed_self_low = rounded(normed_self)
    query_rows = rounded(project(normed_self_low, full_query) + full_query_bias.astype(jnp.float32))
    key_rows = rounded(project(normed_self_low, full_key))
    value_rows = rounded(
        project(normed_self_low, full_value) + full_value_bias.astype(jnp.float32)
    )
    head_triple = lax.all_to_all(
        jnp.stack(
            tuple(to_pairs(rows, seq_count) for rows in (query_rows, key_rows, value_rows)), axis=1
        ),
        "seq",
        0,
        0,
    )
    head_queries, head_keys, head_values = (
        head_triple[:, slot].reshape(full_length, PAIR) for slot in range(3)
    )
    head_attended, head_log = self_forward(head_queries, head_keys, head_values, labels)
    attended_blocks = lax.all_to_all(
        rounded(head_attended).reshape(seq_count, local_len, PAIR), "seq", 0, 0
    )
    attended_self_low = from_pairs(attended_blocks)
    middle_rows = (
        input_rows
        + project(attended_self_low, full_self_out)
        + full_self_out_bias.astype(jnp.float32)
    )
    normed_cross, scaled_cross, inverse_cross = norm_forward(
        middle_rows, full_cross_gain.astype(jnp.float32), full_cross_shift.astype(jnp.float32)
    )
    normed_cross_low = rounded(normed_cross)
    cross_queries = rounded(
        project(normed_cross_low, full_cross_query) + full_cross_query_bias.astype(jnp.float32)
    ).reshape(local_len, batch_count, HEADS, HEAD)
    frame_count = memory.shape[0]
    frame_part = frame_count // seq_count
    frame_start = seq_index * frame_part
    memory_part = lax.dynamic_slice_in_dim(memory, frame_start, frame_part, 0).reshape(
        frame_part * batch_count, D
    )
    memory_flat = memory.reshape(frame_count * batch_count, D)
    memory_keys = rounded(project(memory_flat, full_cross_key)).reshape(frame_count, batch_count, D)
    memory_values = rounded(
        project(memory_flat, full_cross_value) + full_cross_value_bias.astype(jnp.float32)
    ).reshape(frame_count, batch_count, D)
    memory_key_heads = memory_keys.reshape(frame_count, batch_count, HEADS, HEAD)
    memory_value_heads = memory_values.reshape(frame_count, batch_count, HEADS, HEAD)
    frame_valid = (jnp.arange(frame_count, dtype=jnp.int32)[None, :] < memory_lengths[:, None])[
        None, :, None, :
    ]
    cross_scores = (
        jnp.einsum(
            "qbhd,kbhd->qbhk", cross_queries, memory_key_heads, preferred_element_type=jnp.float32
        )
        * 0.125
    )
    cross_max = jnp.max(jnp.where(frame_valid, cross_scores, neg_large), axis=-1, keepdims=True)
    cross_exp = jnp.where(frame_valid, jnp.exp(cross_scores - cross_max), 0.0)
    cross_probs = cross_exp / jnp.sum(cross_exp, axis=-1, keepdims=True)
    cross_probs_low = rounded(cross_probs)
    attended_cross = jnp.einsum(
        "qbhk,kbhd->qbhd", cross_probs_low, memory_value_heads, preferred_element_type=jnp.float32
    )
    attended_cross_low = rounded(attended_cross.reshape(token_count, D))
    after_rows = (
        middle_rows
        + project(attended_cross_low, full_cross_out)
        + full_cross_out_bias.astype(jnp.float32)
    )
    normed_mlp, scaled_mlp, inverse_mlp = norm_forward(
        after_rows, full_mlp_gain.astype(jnp.float32), full_mlp_shift.astype(jnp.float32)
    )
    normed_mlp_low = rounded(normed_mlp)
    hidden_pre = project(normed_mlp_low, full_fc_in) + full_fc_in_bias.astype(jnp.float32)
    activated, gelu_pull = jax.vjp(exact_gelu, hidden_pre)
    activated_low = rounded(activated)
    result_rows = (
        after_rows + project(activated_low, full_fc_out) + full_fc_out_bias.astype(jnp.float32)
    )
    output = rounded(result_rows).reshape(local_len, batch_count, D)
    back_fc_in, back_fc_out = full_fc_in, full_fc_out
    grad_result = out_grad.reshape(token_count, D)
    grad_mlp_low = rounded(grad_result)
    grad_fc_out_weight = weight_grad(activated_low, grad_mlp_low)
    grad_fc_out_bias = column_sums(grad_mlp_low)
    grad_activated = project_back(grad_mlp_low, back_fc_out)
    grad_hidden_low = rounded(gelu_pull(grad_activated)[0])
    grad_fc_in_weight = weight_grad(normed_mlp_low, grad_hidden_low)
    grad_fc_in_bias = column_sums(grad_hidden_low)
    grad_normed_mlp = project_back(grad_hidden_low, back_fc_in)
    grad_rows_mlp, grad_mlp_gain, grad_mlp_shift = norm_backward(
        grad_normed_mlp, scaled_mlp, inverse_mlp, full_mlp_gain.astype(jnp.float32)
    )
    early_grads = jnp.concatenate(
        (
            jnp.transpose(
                grad_fc_in_weight.astype(jnp.bfloat16).reshape(
                    owners, shard_rows, wide_parts, D
                ),
                (0, 2, 1, 3),
            ).reshape(owners, wide_parts * shard_rows, D),
            grad_fc_out_weight.astype(jnp.bfloat16).reshape(owners, -1, D),
        ),
        axis=1,
    )
    owned_early = lax.psum_scatter(
        early_grads, ("dp", "seq"), scatter_dimension=0, tiled=False
    )
    grad_after = grad_result + grad_rows_mlp
    back_cross_query, back_cross_key, back_cross_value, back_cross_out = (
        full_cross_query,
        full_cross_key,
        full_cross_value,
        full_cross_out,
    )
    grad_cross_low = rounded(grad_after)
    grad_cross_out_weight = weight_grad(attended_cross_low, grad_cross_low)
    grad_cross_out_bias = column_sums(grad_cross_low)
    grad_attended_cross = rounded(project_back(grad_cross_low, back_cross_out)).reshape(
        local_len, batch_count, HEADS, HEAD
    )
    grad_cross_probs = jnp.einsum(
        "qbhd,kbhd->qbhk",
        grad_attended_cross,
        memory_value_heads,
        preferred_element_type=jnp.float32,
    )
    cross_delta = jnp.sum(cross_probs * grad_cross_probs, axis=-1, keepdims=True)
    grad_cross_scores = rounded(cross_probs * (grad_cross_probs - cross_delta) * 0.125)
    grad_cross_queries = rounded(
        jnp.einsum(
            "qbhk,kbhd->qbhd",
            grad_cross_scores,
            memory_key_heads,
            preferred_element_type=jnp.float32,
        ).reshape(token_count, D)
    )
    grad_memory_keys = jnp.einsum(
        "qbhk,qbhd->kbhd", grad_cross_scores, cross_queries, preferred_element_type=jnp.float32
    ).reshape(frame_count, batch_count, D)
    grad_memory_values = jnp.einsum(
        "qbhk,qbhd->kbhd", cross_probs_low, grad_attended_cross, preferred_element_type=jnp.float32
    ).reshape(frame_count, batch_count, D)
    grad_memory_kv = jnp.concatenate(
        (grad_memory_keys.astype(jnp.bfloat16), grad_memory_values.astype(jnp.bfloat16)), axis=2
    ).reshape(seq_count, frame_part, batch_count, 2 * D)
    grad_memory_kv, owned_early = lax.optimization_barrier((grad_memory_kv, owned_early))
    part_kv = lax.psum_scatter(grad_memory_kv, "seq", scatter_dimension=0, tiled=False)
    wide_rows = wide_parts * shard_rows
    owned_fc_in = jnp.transpose(
        owned_early[:wide_rows].astype(jnp.float32).reshape(wide_parts, shard_rows, D), (1, 0, 2)
    ).reshape(shard_rows, wide_parts * D)
    owned_fc_out = owned_early[wide_rows:].astype(jnp.float32)
    part_flat_keys = part_kv[:, :, :D].reshape(frame_part * batch_count, D)
    part_flat_values = part_kv[:, :, D:].reshape(frame_part * batch_count, D)
    part_memory_grad = (
        project_back(part_flat_keys, back_cross_key)
        + project_back(part_flat_values, back_cross_value)
    ).reshape(frame_part, batch_count, D)
    grad_cross_key_weight = weight_grad(memory_part, part_flat_keys)
    grad_cross_value_weight = weight_grad(memory_part, part_flat_values)
    grad_cross_value_bias = column_sums(part_flat_values)
    grad_cross_query_weight = weight_grad(normed_cross_low, grad_cross_queries)
    grad_cross_query_bias = column_sums(grad_cross_queries)
    grad_normed_cross = project_back(grad_cross_queries, back_cross_query)
    grad_rows_cross, grad_cross_gain, grad_cross_shift = norm_backward(
        grad_normed_cross, scaled_cross, inverse_cross, full_cross_gain.astype(jnp.float32)
    )
    grad_middle = grad_after + grad_rows_cross
    back_query, back_key, back_value, back_self_out = (
        full_query,
        full_key,
        full_value,
        full_self_out,
    )
    grad_self_low = rounded(grad_middle)
    grad_attn_out_weight = weight_grad(attended_self_low, grad_self_low)
    grad_attn_out_bias = column_sums(grad_self_low)
    grad_attended_self = rounded(project_back(grad_self_low, back_self_out))
    head_grad = lax.all_to_all(to_pairs(grad_attended_self, seq_count), "seq", 0, 0).reshape(
        full_length, PAIR
    )
    head_grads = self_backward(
        head_queries, head_keys, head_values, labels, head_attended, head_log, head_grad
    )
    grad_triple = lax.all_to_all(
        jnp.stack(
            tuple(part.reshape(seq_count, local_len, PAIR) for part in head_grads), axis=1
        ),
        "seq",
        0,
        0,
    )
    grad_query_low, grad_key_low, grad_value_low = (
        from_pairs(grad_triple[:, slot]) for slot in range(3)
    )
    grad_query_weight = weight_grad(normed_self_low, grad_query_low)
    grad_query_bias = column_sums(grad_query_low)
    grad_key_weight = weight_grad(normed_self_low, grad_key_low)
    grad_value_weight = weight_grad(normed_self_low, grad_value_low)
    grad_value_bias = column_sums(grad_value_low)
    grad_normed_self = (
        project_back(grad_query_low, back_query)
        + project_back(grad_key_low, back_key)
        + project_back(grad_value_low, back_value)
    )
    grad_rows_self, grad_self_gain, grad_self_shift = norm_backward(
        grad_normed_self, scaled_self, inverse_self, full_self_gain.astype(jnp.float32)
    )
    token_grad = (grad_middle + grad_rows_self).reshape(local_len, batch_count, D)
    def owner_rows(matrix):
        return matrix.astype(jnp.bfloat16).reshape(owners, -1, D)

    late_vectors = jnp.concatenate(
        tuple(
            vector.reshape(owners, -1)
            for vector in (
                grad_self_gain,
                grad_self_shift,
                grad_query_bias,
                grad_value_bias,
                grad_attn_out_bias,
                grad_cross_gain,
                grad_cross_shift,
                grad_cross_query_bias,
                grad_cross_value_bias,
                grad_cross_out_bias,
                grad_mlp_gain,
                grad_mlp_shift,
                grad_fc_out_bias,
                grad_fc_in_bias,
            )
        ),
        axis=1,
    )
    late_block = jnp.pad(
        late_vectors.astype(jnp.bfloat16),
        ((0, 0), (0, vector_rows * D - late_vectors.shape[1])),
    ).reshape(owners, vector_rows, D)
    late_grads = jnp.concatenate(
        (
            owner_rows(grad_query_weight),
            owner_rows(grad_key_weight),
            owner_rows(grad_value_weight),
            owner_rows(grad_attn_out_weight),
            owner_rows(grad_cross_query_weight),
            owner_rows(grad_cross_key_weight),
            owner_rows(grad_cross_value_weight),
            owner_rows(grad_cross_out_weight),
            late_block,
        ),
        axis=1,
    )
    owned_late = lax.psum_scatter(
        late_grads, ("dp", "seq"), scatter_dimension=0, tiled=False
    ).astype(jnp.float32)
    memory_grad = lax.all_gather(
        part_memory_grad.astype(jnp.bfloat16), "seq", axis=0, tiled=True
    ).astype(jnp.float32)
    owned_vectors = owned_late[8 * shard_rows :].reshape(-1)

    def own_square(slot):
        return owned_late[slot * shard_rows : (slot + 1) * shard_rows]

    def own_vector(slot):
        return owned_vectors[slot * shard_rows : (slot + 1) * shard_rows]

    owned_fc_in_bias = owned_vectors[13 * shard_rows : 13 * shard_rows + fc_in_bias.shape[0]]
    return (
        output,
        token_grad,
        memory_grad,
        own_vector(0),
        own_vector(1),
        own_square(0),
        own_vector(2),
        own_square(1),
        own_square(2),
        own_vector(3),
        own_square(3),
        own_vector(4),
        own_vector(5),
        own_vector(6),
        own_square(4),
        own_vector(7),
        own_square(5),
        own_square(6),
        own_vector(8),
        own_square(7),
        own_vector(9),
        own_vector(10),
        own_vector(11),
        owned_fc_in,
        owned_fc_in_bias,
        owned_fc_out,
        own_vector(12),
    )


def local(
    tokens,
    memory,
    piece_starts,
    memory_lengths,
    self_gain,
    self_shift,
    query_weight,
    query_bias,
    key_weight,
    value_weight,
    value_bias,
    attn_out_weight,
    attn_out_bias,
    cross_gain,
    cross_shift,
    cross_query_weight,
    cross_query_bias,
    cross_key_weight,
    cross_value_weight,
    cross_value_bias,
    cross_out_weight,
    cross_out_bias,
    mlp_gain,
    mlp_shift,
    fc_in_weight,
    fc_in_bias,
    fc_out_weight,
    fc_out_bias,
    out_grad,
):
    local_len, batch_count, model_width = tokens.shape
    seq_count = lax.axis_size("seq")
    seq_index = lax.axis_index("seq")
    full_length = local_len * seq_count
    token_count = local_len * batch_count
    query_pos = seq_index * local_len + jnp.arange(local_len, dtype=jnp.int32)
    query_label = piece_labels(query_pos, piece_starts)
    input_rows = tokens.reshape(token_count, D).astype(jnp.float32)
    shard_rows = query_weight.shape[0]
    wide_parts = fc_in_weight.shape[1] // D
    vectors = jnp.concatenate(
        (
            self_gain,
            self_shift,
            query_bias,
            value_bias,
            attn_out_bias,
            cross_gain,
            cross_shift,
            cross_query_bias,
            cross_value_bias,
            cross_out_bias,
            mlp_gain,
            mlp_shift,
            fc_out_bias,
            fc_in_bias,
        )
    )
    vector_rows = 8
    vector_block = jnp.pad(vectors, (0, vector_rows * D - vectors.shape[0])).reshape(vector_rows, D)
    fc_in_blocks = jnp.transpose(
        fc_in_weight.reshape(shard_rows, wide_parts, D), (1, 0, 2)
    ).reshape(wide_parts * shard_rows, D)
    packed = jnp.concatenate(
        (
            query_weight,
            key_weight,
            value_weight,
            attn_out_weight,
            cross_query_weight,
            cross_key_weight,
            cross_value_weight,
            cross_out_weight,
            fc_in_blocks,
            fc_out_weight,
            vector_block,
        )
    )
    gathered = lax.all_gather(packed, ("dp", "seq"), axis=0, tiled=False)
    owners = gathered.shape[0]

    def square_at(slot):
        return gathered[:, slot * shard_rows : (slot + 1) * shard_rows, :].reshape(D, D)

    full_query, full_key, full_value, full_self_out = (square_at(slot) for slot in range(4))
    full_cross_query, full_cross_key, full_cross_value, full_cross_out = (
        square_at(slot) for slot in range(4, 8)
    )
    wide_start = 8 * shard_rows
    wide_stop = wide_start + wide_parts * shard_rows
    full_fc_in = jnp.transpose(
        gathered[:, wide_start:wide_stop, :].reshape(owners, wide_parts, shard_rows, D),
        (0, 2, 1, 3),
    ).reshape(D, wide_parts * D)
    out_stop = wide_stop + fc_out_weight.shape[0]
    full_fc_out = gathered[:, wide_stop:out_stop, :].reshape(wide_parts * D, D)
    full_vectors = gathered[:, out_stop:, :].reshape(owners, vector_rows * D)

    def vector_at(slot):
        return full_vectors[:, slot * shard_rows : (slot + 1) * shard_rows].reshape(D)

    (
        full_self_gain,
        full_self_shift,
        full_query_bias,
        full_value_bias,
        full_self_out_bias,
        full_cross_gain,
        full_cross_shift,
        full_cross_query_bias,
        full_cross_value_bias,
        full_cross_out_bias,
        full_mlp_gain,
        full_mlp_shift,
        full_fc_out_bias,
    ) = (vector_at(slot) for slot in range(13))
    full_fc_in_bias = full_vectors[
        :, 13 * shard_rows : 13 * shard_rows + fc_in_bias.shape[0]
    ].reshape(-1)
    normed_self, scaled_self, inverse_self = norm_forward(
        input_rows, full_self_gain.astype(jnp.float32), full_self_shift.astype(jnp.float32)
    )
    normed_self_low = rounded(normed_self)
    query_rows = rounded(project(normed_self_low, full_query) + full_query_bias.astype(jnp.float32))
    key_rows = rounded(project(normed_self_low, full_key)).reshape(local_len, batch_count, D)
    value_rows = rounded(
        project(normed_self_low, full_value) + full_value_bias.astype(jnp.float32)
    ).reshape(local_len, batch_count, D)
    query_heads = query_rows.reshape(local_len, batch_count, HEADS, HEAD)

    def key_block_scores(key_block, key_pos):
        key_heads = key_block.reshape(key_block.shape[0], batch_count, HEADS, HEAD)
        raw_scores = jnp.einsum(
            "qbhd,kbhd->qbhk", query_heads, key_heads, preferred_element_type=jnp.float32
        )
        allowed = visible(query_pos, query_label, key_pos, piece_labels(key_pos, piece_starts))
        return (raw_scores * 0.125, allowed)

    start_state = (
        jnp.full((local_len, batch_count, HEADS), neg_large, jnp.float32),
        jnp.zeros((local_len, batch_count, HEADS), jnp.float32),
        jnp.zeros((local_len, batch_count, HEADS, HEAD), jnp.float32),
    )
    running = start_state
    kv_piece = lax.all_gather(
        jnp.concatenate((key_rows, value_rows), axis=2), "seq", axis=0, tiled=True
    )
    key_piece = kv_piece[:, :, :D]
    value_piece = kv_piece[:, :, D:]
    block_rows = math.gcd(key_piece.shape[0], 512)

    def fold_block(inner_state, block_index):
        row_max, row_total, weighted_sum = inner_state
        block_start = block_index * block_rows
        key_block = lax.dynamic_slice_in_dim(key_piece, block_start, block_rows, 0)
        value_block = lax.dynamic_slice_in_dim(value_piece, block_start, block_rows, 0).reshape(
            block_rows, batch_count, HEADS, HEAD
        )
        key_pos = block_start + jnp.arange(block_rows, dtype=jnp.int32)
        scores, allowed = key_block_scores(key_block, key_pos)
        new_max = jnp.maximum(row_max, jnp.max(jnp.where(allowed, scores, neg_large), axis=-1))
        exp_terms = jnp.where(allowed, jnp.exp(scores - new_max[..., None]), 0.0)
        factor = jnp.exp(row_max - new_max)
        row_total = row_total * factor + jnp.sum(exp_terms, axis=-1)
        weighted_sum = weighted_sum * factor[..., None] + jnp.einsum(
            "qbhk,kbhd->qbhd", rounded(exp_terms), value_block, preferred_element_type=jnp.float32
        )
        return ((new_max, row_total, weighted_sum), None)

    running, unused = lax.scan(
        fold_block, running, jnp.arange(key_piece.shape[0] // block_rows, dtype=jnp.int32)
    )
    row_max, row_total, weighted_sum = running
    attended_self = weighted_sum / row_total[..., None]
    log_total = row_max + jnp.log(row_total)
    attended_self_low = rounded(attended_self.reshape(token_count, D))
    middle_rows = (
        input_rows
        + project(attended_self_low, full_self_out)
        + full_self_out_bias.astype(jnp.float32)
    )
    normed_cross, scaled_cross, inverse_cross = norm_forward(
        middle_rows, full_cross_gain.astype(jnp.float32), full_cross_shift.astype(jnp.float32)
    )
    normed_cross_low = rounded(normed_cross)
    cross_queries = rounded(
        project(normed_cross_low, full_cross_query) + full_cross_query_bias.astype(jnp.float32)
    ).reshape(local_len, batch_count, HEADS, HEAD)
    frame_count = memory.shape[0]
    frame_part = frame_count // seq_count
    frame_start = seq_index * frame_part
    memory_part = lax.dynamic_slice_in_dim(memory, frame_start, frame_part, 0).reshape(
        frame_part * batch_count, D
    )
    memory_flat = memory.reshape(frame_count * batch_count, D)
    memory_keys = rounded(project(memory_flat, full_cross_key)).reshape(frame_count, batch_count, D)
    memory_values = rounded(
        project(memory_flat, full_cross_value) + full_cross_value_bias.astype(jnp.float32)
    ).reshape(frame_count, batch_count, D)
    memory_key_heads = memory_keys.reshape(frame_count, batch_count, HEADS, HEAD)
    memory_value_heads = memory_values.reshape(frame_count, batch_count, HEADS, HEAD)
    frame_valid = (jnp.arange(frame_count, dtype=jnp.int32)[None, :] < memory_lengths[:, None])[
        None, :, None, :
    ]
    cross_scores = (
        jnp.einsum(
            "qbhd,kbhd->qbhk", cross_queries, memory_key_heads, preferred_element_type=jnp.float32
        )
        * 0.125
    )
    cross_max = jnp.max(jnp.where(frame_valid, cross_scores, neg_large), axis=-1, keepdims=True)
    cross_exp = jnp.where(frame_valid, jnp.exp(cross_scores - cross_max), 0.0)
    cross_probs = cross_exp / jnp.sum(cross_exp, axis=-1, keepdims=True)
    cross_probs_low = rounded(cross_probs)
    attended_cross = jnp.einsum(
        "qbhk,kbhd->qbhd", cross_probs_low, memory_value_heads, preferred_element_type=jnp.float32
    )
    attended_cross_low = rounded(attended_cross.reshape(token_count, D))
    after_rows = (
        middle_rows
        + project(attended_cross_low, full_cross_out)
        + full_cross_out_bias.astype(jnp.float32)
    )
    normed_mlp, scaled_mlp, inverse_mlp = norm_forward(
        after_rows, full_mlp_gain.astype(jnp.float32), full_mlp_shift.astype(jnp.float32)
    )
    normed_mlp_low = rounded(normed_mlp)
    hidden_pre = project(normed_mlp_low, full_fc_in) + full_fc_in_bias.astype(jnp.float32)
    activated, gelu_pull = jax.vjp(exact_gelu, hidden_pre)
    activated_low = rounded(activated)
    result_rows = (
        after_rows + project(activated_low, full_fc_out) + full_fc_out_bias.astype(jnp.float32)
    )
    output = rounded(result_rows).reshape(local_len, batch_count, D)
    back_fc_in, back_fc_out = full_fc_in, full_fc_out
    grad_result = out_grad.reshape(token_count, D)
    grad_mlp_low = rounded(grad_result)
    grad_fc_out_weight = weight_grad(activated_low, grad_mlp_low)
    grad_fc_out_bias = column_sums(grad_mlp_low)
    grad_activated = project_back(grad_mlp_low, back_fc_out)
    grad_hidden_low = rounded(gelu_pull(grad_activated)[0])
    grad_fc_in_weight = weight_grad(normed_mlp_low, grad_hidden_low)
    grad_fc_in_bias = column_sums(grad_hidden_low)
    grad_normed_mlp = project_back(grad_hidden_low, back_fc_in)
    grad_rows_mlp, grad_mlp_gain, grad_mlp_shift = norm_backward(
        grad_normed_mlp, scaled_mlp, inverse_mlp, full_mlp_gain.astype(jnp.float32)
    )
    early_grads = jnp.concatenate(
        (
            jnp.transpose(
                grad_fc_in_weight.astype(jnp.bfloat16).reshape(
                    owners, shard_rows, wide_parts, D
                ),
                (0, 2, 1, 3),
            ).reshape(owners, wide_parts * shard_rows, D),
            grad_fc_out_weight.astype(jnp.bfloat16).reshape(owners, -1, D),
        ),
        axis=1,
    )
    owned_early = lax.psum_scatter(
        early_grads, ("dp", "seq"), scatter_dimension=0, tiled=False
    ).astype(jnp.float32)
    wide_rows = wide_parts * shard_rows
    owned_fc_in = jnp.transpose(
        owned_early[:wide_rows].reshape(wide_parts, shard_rows, D), (1, 0, 2)
    ).reshape(shard_rows, wide_parts * D)
    owned_fc_out = owned_early[wide_rows:]
    grad_after = grad_result + grad_rows_mlp
    back_cross_query, back_cross_key, back_cross_value, back_cross_out = (
        full_cross_query,
        full_cross_key,
        full_cross_value,
        full_cross_out,
    )
    grad_cross_low = rounded(grad_after)
    grad_cross_out_weight = weight_grad(attended_cross_low, grad_cross_low)
    grad_cross_out_bias = column_sums(grad_cross_low)
    grad_attended_cross = rounded(project_back(grad_cross_low, back_cross_out)).reshape(
        local_len, batch_count, HEADS, HEAD
    )
    grad_cross_probs = jnp.einsum(
        "qbhd,kbhd->qbhk",
        grad_attended_cross,
        memory_value_heads,
        preferred_element_type=jnp.float32,
    )
    cross_delta = jnp.sum(cross_probs * grad_cross_probs, axis=-1, keepdims=True)
    grad_cross_scores = rounded(cross_probs * (grad_cross_probs - cross_delta) * 0.125)
    grad_cross_queries = rounded(
        jnp.einsum(
            "qbhk,kbhd->qbhd",
            grad_cross_scores,
            memory_key_heads,
            preferred_element_type=jnp.float32,
        ).reshape(token_count, D)
    )
    grad_memory_keys = jnp.einsum(
        "qbhk,qbhd->kbhd", grad_cross_scores, cross_queries, preferred_element_type=jnp.float32
    ).reshape(frame_count, batch_count, D)
    grad_memory_values = jnp.einsum(
        "qbhk,qbhd->kbhd", cross_probs_low, grad_attended_cross, preferred_element_type=jnp.float32
    ).reshape(frame_count, batch_count, D)
    grad_memory_kv = jnp.concatenate((grad_memory_keys, grad_memory_values), axis=2)
    grad_cross_query_weight = weight_grad(normed_cross_low, grad_cross_queries)
    grad_cross_query_bias = column_sums(grad_cross_queries)
    grad_normed_cross = project_back(grad_cross_queries, back_cross_query)
    grad_rows_cross, grad_cross_gain, grad_cross_shift = norm_backward(
        grad_normed_cross, scaled_cross, inverse_cross, full_cross_gain.astype(jnp.float32)
    )
    grad_middle = grad_after + grad_rows_cross
    back_query, back_key, back_value, back_self_out = (
        full_query,
        full_key,
        full_value,
        full_self_out,
    )
    grad_self_low = rounded(grad_middle)
    grad_attn_out_weight = weight_grad(attended_self_low, grad_self_low)
    grad_attn_out_bias = column_sums(grad_self_low)
    grad_attended_self = rounded(project_back(grad_self_low, back_self_out)).reshape(
        local_len, batch_count, HEADS, HEAD
    )
    self_delta = jnp.sum(grad_attended_self.astype(jnp.float32) * attended_self, axis=-1)

    def score_grads(key_block, value_block, key_pos):
        scores, allowed = key_block_scores(key_block, key_pos)
        attn_probs = jnp.where(allowed, jnp.exp(scores - log_total[..., None]), 0.0)
        grad_probs = jnp.einsum(
            "qbhd,kbhd->qbhk", grad_attended_self, value_block, preferred_element_type=jnp.float32
        )
        grad_scores = rounded(attn_probs * (grad_probs - self_delta[..., None]) * 0.125)
        return (grad_scores, attn_probs)

    zero_query_grad = jnp.zeros((local_len, batch_count, HEADS, HEAD), jnp.float32)
    back_state = (zero_query_grad, jnp.zeros((full_length, batch_count, 2 * D), jnp.float32))
    running = back_state
    self_key_piece = key_piece
    self_value_piece = value_piece
    self_block_rows = math.gcd(self_key_piece.shape[0], 512)

    def back_block(inner_state, block_index):
        grad_query_sum, kv_grads = inner_state
        block_start = block_index * self_block_rows
        key_block = lax.dynamic_slice_in_dim(self_key_piece, block_start, self_block_rows, 0)
        value_block = lax.dynamic_slice_in_dim(
            self_value_piece, block_start, self_block_rows, 0
        ).reshape(self_block_rows, batch_count, HEADS, HEAD)
        key_pos = block_start + jnp.arange(self_block_rows, dtype=jnp.int32)
        grad_scores, attn_probs = score_grads(key_block, value_block, key_pos)
        key_heads = key_block.reshape(self_block_rows, batch_count, HEADS, HEAD)
        grad_query_sum = grad_query_sum + jnp.einsum(
            "qbhk,kbhd->qbhd", grad_scores, key_heads, preferred_element_type=jnp.float32
        )
        grad_key_block = jnp.einsum(
            "qbhk,qbhd->kbhd", grad_scores, query_heads, preferred_element_type=jnp.float32
        ).reshape(self_block_rows, batch_count, D)
        grad_value_block = jnp.einsum(
            "qbhk,qbhd->kbhd",
            rounded(attn_probs),
            grad_attended_self,
            preferred_element_type=jnp.float32,
        ).reshape(self_block_rows, batch_count, D)
        kv_grads = lax.dynamic_update_slice_in_dim(
            kv_grads, jnp.concatenate((grad_key_block, grad_value_block), axis=2), block_start, 0
        )
        return ((grad_query_sum, kv_grads), None)

    running, unused = lax.scan(
        back_block, running, jnp.arange(self_key_piece.shape[0] // self_block_rows, dtype=jnp.int32)
    )
    grad_query_sum = running[0]
    joint_kv = jnp.concatenate(
        (
            running[1].astype(jnp.bfloat16).reshape(seq_count, local_len, batch_count, 2 * D),
            grad_memory_kv.astype(jnp.bfloat16).reshape(
                seq_count, frame_part, batch_count, 2 * D
            ),
        ),
        axis=1,
    )
    own_joint = lax.psum_scatter(joint_kv, "seq", scatter_dimension=0, tiled=False)
    own_kv = own_joint[:local_len]
    part_kv = own_joint[local_len:]
    grad_key_low = own_kv[:, :, :D].reshape(token_count, D)
    grad_value_low = own_kv[:, :, D:].reshape(token_count, D)
    part_flat_keys = part_kv[:, :, :D].reshape(frame_part * batch_count, D)
    part_flat_values = part_kv[:, :, D:].reshape(frame_part * batch_count, D)
    part_memory_grad = (
        project_back(part_flat_keys, back_cross_key)
        + project_back(part_flat_values, back_cross_value)
    ).reshape(frame_part, batch_count, D)
    grad_cross_key_weight = weight_grad(memory_part, part_flat_keys)
    grad_cross_value_weight = weight_grad(memory_part, part_flat_values)
    grad_cross_value_bias = column_sums(part_flat_values)
    grad_query_low = rounded(grad_query_sum.reshape(token_count, D))
    grad_query_weight = weight_grad(normed_self_low, grad_query_low)
    grad_query_bias = column_sums(grad_query_low)
    grad_key_weight = weight_grad(normed_self_low, grad_key_low)
    grad_value_weight = weight_grad(normed_self_low, grad_value_low)
    grad_value_bias = column_sums(grad_value_low)
    grad_normed_self = (
        project_back(grad_query_low, back_query)
        + project_back(grad_key_low, back_key)
        + project_back(grad_value_low, back_value)
    )
    grad_rows_self, grad_self_gain, grad_self_shift = norm_backward(
        grad_normed_self, scaled_self, inverse_self, full_self_gain.astype(jnp.float32)
    )
    token_grad = (grad_middle + grad_rows_self).reshape(local_len, batch_count, D)
    def owner_rows(matrix):
        return matrix.astype(jnp.bfloat16).reshape(owners, -1, D)

    late_vectors = jnp.concatenate(
        tuple(
            vector.reshape(owners, -1)
            for vector in (
                grad_self_gain,
                grad_self_shift,
                grad_query_bias,
                grad_value_bias,
                grad_attn_out_bias,
                grad_cross_gain,
                grad_cross_shift,
                grad_cross_query_bias,
                grad_cross_value_bias,
                grad_cross_out_bias,
                grad_mlp_gain,
                grad_mlp_shift,
                grad_fc_out_bias,
                grad_fc_in_bias,
            )
        ),
        axis=1,
    )
    late_block = jnp.pad(
        late_vectors.astype(jnp.bfloat16),
        ((0, 0), (0, vector_rows * D - late_vectors.shape[1])),
    ).reshape(owners, vector_rows, D)
    late_grads = jnp.concatenate(
        (
            owner_rows(grad_query_weight),
            owner_rows(grad_key_weight),
            owner_rows(grad_value_weight),
            owner_rows(grad_attn_out_weight),
            owner_rows(grad_cross_query_weight),
            owner_rows(grad_cross_key_weight),
            owner_rows(grad_cross_value_weight),
            owner_rows(grad_cross_out_weight),
            late_block,
        ),
        axis=1,
    )
    owned_late = lax.psum_scatter(
        late_grads, ("dp", "seq"), scatter_dimension=0, tiled=False
    ).astype(jnp.float32)
    memory_grad = lax.all_gather(
        part_memory_grad.astype(jnp.bfloat16), "seq", axis=0, tiled=True
    ).astype(jnp.float32)
    owned_vectors = owned_late[8 * shard_rows :].reshape(-1)

    def own_square(slot):
        return owned_late[slot * shard_rows : (slot + 1) * shard_rows]

    def own_vector(slot):
        return owned_vectors[slot * shard_rows : (slot + 1) * shard_rows]

    owned_fc_in_bias = owned_vectors[13 * shard_rows : 13 * shard_rows + fc_in_bias.shape[0]]
    return (
        output,
        token_grad,
        memory_grad,
        own_vector(0),
        own_vector(1),
        own_square(0),
        own_vector(2),
        own_square(1),
        own_square(2),
        own_vector(3),
        own_square(3),
        own_vector(4),
        own_vector(5),
        own_vector(6),
        own_square(4),
        own_vector(7),
        own_square(5),
        own_square(6),
        own_vector(8),
        own_square(7),
        own_vector(9),
        own_vector(10),
        own_vector(11),
        owned_fc_in,
        owned_fc_in_bias,
        owned_fc_out,
        own_vector(12),
    )


def solution(mesh):
    in_specs = (
        P("seq", "dp", None),
        P(None, "dp", None),
        P("dp", None),
        P("dp"),
        P(("dp", "seq")),
        P(("dp", "seq")),
        P(("dp", "seq"), None),
        P(("dp", "seq")),
        P(("dp", "seq"), None),
        P(("dp", "seq"), None),
        P(("dp", "seq")),
        P(("dp", "seq"), None),
        P(("dp", "seq")),
        P(("dp", "seq")),
        P(("dp", "seq")),
        P(("dp", "seq"), None),
        P(("dp", "seq")),
        P(("dp", "seq"), None),
        P(("dp", "seq"), None),
        P(("dp", "seq")),
        P(("dp", "seq"), None),
        P(("dp", "seq")),
        P(("dp", "seq")),
        P(("dp", "seq")),
        P(("dp", "seq"), None),
        P(("dp", "seq")),
        P(("dp", "seq"), None),
        P(("dp", "seq")),
        P("seq", "dp", None),
    )
    out_specs = (
        P("seq", "dp", None),
        P("seq", "dp", None),
        P(None, "dp", None),
        P(("dp", "seq")),
        P(("dp", "seq")),
        P(("dp", "seq"), None),
        P(("dp", "seq")),
        P(("dp", "seq"), None),
        P(("dp", "seq"), None),
        P(("dp", "seq")),
        P(("dp", "seq"), None),
        P(("dp", "seq")),
        P(("dp", "seq")),
        P(("dp", "seq")),
        P(("dp", "seq"), None),
        P(("dp", "seq")),
        P(("dp", "seq"), None),
        P(("dp", "seq"), None),
        P(("dp", "seq")),
        P(("dp", "seq"), None),
        P(("dp", "seq")),
        P(("dp", "seq")),
        P(("dp", "seq")),
        P(("dp", "seq"), None),
        P(("dp", "seq")),
        P(("dp", "seq"), None),
        P(("dp", "seq")),
    )
    by_heads = D // PAIR <= mesh.shape["seq"] <= 8
    return jax.shard_map(
        local_heads if by_heads else local,
        mesh=mesh, in_specs=in_specs, out_specs=out_specs, check_vma=False,
    )
```

```python
import math

import jax
import jax.numpy as jnp
from jax import lax
from jax.experimental import pallas as pl
from jax.experimental.pallas import tpu as pltpu
from jax.sharding import PartitionSpec as P


D = 768
HEADS = 12
HEAD = 64
PIECE = 256


norm_epsilon = 1e-05
neg_large = -1e30


def rounded(tensor):
    return tensor.astype(jnp.bfloat16)


def project(left_rows, matrix):
    return jnp.dot(left_rows, matrix, preferred_element_type=jnp.float32)


def project_back(left_rows, matrix):
    return lax.dot_general(
        left_rows, matrix, (((1,), (1,)), ((), ())), preferred_element_type=jnp.float32
    )


def weight_grad(inputs, grad_rows):
    return lax.dot_general(
        inputs, grad_rows, (((0,), (0,)), ((), ())), preferred_element_type=jnp.float32
    )


def column_sums(grad_rows):
    return jnp.sum(grad_rows.astype(jnp.float32), axis=0)


def exact_gelu(inputs):
    return jax.nn.gelu(inputs, approximate=False)


def norm_forward(token_rows, norm_gain, norm_shift):
    centre = token_rows - jnp.mean(token_rows, axis=-1, keepdims=True)
    inverse = lax.rsqrt(jnp.mean(centre * centre, axis=-1, keepdims=True) + norm_epsilon)
    scaled = centre * inverse
    return (scaled * norm_gain + norm_shift, scaled, inverse)


def norm_backward(grad_normed, scaled, inverse, norm_gain):
    grad_scaled = grad_normed * norm_gain
    mean_grad = jnp.mean(grad_scaled, axis=-1, keepdims=True)
    mean_cross = jnp.mean(grad_scaled * scaled, axis=-1, keepdims=True)
    grad_input = inverse * (grad_scaled - mean_grad - scaled * mean_cross)
    return (grad_input, jnp.sum(grad_normed * scaled, axis=0), jnp.sum(grad_normed, axis=0))


def piece_labels(positions, starts):
    inside = (positions[None, :, None] >= starts[:, None, :]) & (
        positions[None, :, None] < starts[:, None, :] + PIECE
    )
    numbers = jnp.arange(1, starts.shape[1] + 1, dtype=jnp.int32)
    return jnp.sum(jnp.where(inside, numbers, 0), axis=2)


def visible(query_pos, query_label, key_pos, key_label):
    causal = (key_pos[None, :] <= query_pos[:, None])[:, None, :]
    query_side = jnp.transpose(query_label)[:, :, None]
    same_piece = (query_side == key_label[None, :, :]) & (query_side > 0)
    return (causal | same_piece)[:, :, None, :]


PAIR = 2 * HEAD
QUERY_BLOCK = 256
KEY_BLOCK = 512


def to_pairs(rows, seq_count):
    blocks = jnp.transpose(rows.reshape(rows.shape[0], D // PAIR, PAIR), (1, 0, 2))
    return jnp.pad(blocks, ((0, seq_count - D // PAIR), (0, 0), (0, 0)))


def from_pairs(blocks):
    kept = blocks[: D // PAIR]
    return jnp.transpose(kept, (1, 0, 2)).reshape(kept.shape[1], D)


def dot_rows(left, right):
    return lax.dot_general(left, right, (((1,), (1,)), ((), ())), preferred_element_type=jnp.float32)


def dot_plain(left, right):
    return lax.dot_general(left, right, (((1,), (0,)), ((), ())), preferred_element_type=jnp.float32)


def dot_columns(left, right):
    return lax.dot_general(left, right, (((0,), (0,)), ((), ())), preferred_element_type=jnp.float32)


def split_pair(block):
    lanes = lax.broadcasted_iota(jnp.int32, block.shape, 1)
    zero = jnp.zeros_like(block)
    return (jnp.where(lanes < HEAD, block, zero), jnp.where(lanes < HEAD, zero, block))


def join_pair(first, second, shape):
    lanes = lax.broadcasted_iota(jnp.int32, shape, 1)
    return jnp.where(lanes < HEAD, first, second)


def stack_pair(block):
    return jnp.concatenate(split_pair(block), axis=0)


def join_stack(stacked):
    rows = stacked.shape[0] // 2
    return join_pair(stacked[:rows], stacked[rows:], (rows, stacked.shape[1]))


def block_allowed(query_pos, key_pos, query_label, key_label):
    same_piece = (query_label == key_label) & (query_label > 0)
    return (key_pos <= query_pos) | same_piece


def key_block_range(block, key_rows):
    full = block * QUERY_BLOCK // KEY_BLOCK
    last = ((block + 2) * QUERY_BLOCK + KEY_BLOCK - 1) // KEY_BLOCK
    return (full, jnp.minimum(last, key_rows // KEY_BLOCK))


def self_forward_body(query_ref, key_ref, value_ref, column_ref, row_ref, out_ref, log_ref):
    block = pl.program_id(0)
    queries = stack_pair(query_ref[...] * jnp.bfloat16(0.125))
    query_label = column_ref[...]

    def step(key_block, state, masked):
        start = pl.multiple_of(key_block * KEY_BLOCK, KEY_BLOCK)
        here = pl.ds(start, KEY_BLOCK)
        row_max, row_total, weighted = state
        scores = dot_rows(queries, key_ref[here, :])
        if masked:
            shape = (QUERY_BLOCK, KEY_BLOCK)
            allowed = block_allowed(
                block * QUERY_BLOCK + lax.broadcasted_iota(jnp.int32, shape, 0),
                start + lax.broadcasted_iota(jnp.int32, shape, 1),
                query_label,
                row_ref[:, here],
            )
            scores = jnp.concatenate(
                (
                    jnp.where(allowed, scores[:QUERY_BLOCK], neg_large),
                    jnp.where(allowed, scores[QUERY_BLOCK:], neg_large),
                ),
                axis=0,
            )
        new_max = jnp.maximum(row_max, jnp.max(scores, axis=1, keepdims=True))
        exp_terms = jnp.exp(scores - new_max)
        factor = jnp.exp(row_max - new_max)
        row_total = row_total * factor + jnp.sum(exp_terms, axis=1, keepdims=True)
        weighted = weighted * factor + dot_plain(rounded(exp_terms), value_ref[here, :])
        return (new_max, row_total, weighted)

    state = (
        jnp.full((2 * QUERY_BLOCK, 1), neg_large, jnp.float32),
        jnp.zeros((2 * QUERY_BLOCK, 1), jnp.float32),
        jnp.zeros((2 * QUERY_BLOCK, PAIR), jnp.float32),
    )
    full, last = key_block_range(block, key_ref.shape[0])
    state = lax.fori_loop(0, full, lambda index, state: step(index, state, False), state)
    state = lax.fori_loop(full, last, lambda index, state: step(index, state, True), state)
    row_max, row_total, weighted = state
    out_ref[...] = join_stack(weighted / row_total)
    log_ref[...] = join_stack(jnp.broadcast_to(row_max + jnp.log(row_total), weighted.shape))


def self_forward(queries, keys, values, labels):
    length = queries.shape[0]
    block_spec = pl.BlockSpec((QUERY_BLOCK, PAIR), lambda index: (index, 0))
    whole_spec = pl.BlockSpec((length, PAIR), lambda index: (0, 0))
    result = jax.ShapeDtypeStruct((length, PAIR), jnp.float32)
    return pl.pallas_call(
        self_forward_body,
        grid=(length // QUERY_BLOCK,),
        in_specs=[
            block_spec,
            whole_spec,
            whole_spec,
            pl.BlockSpec((QUERY_BLOCK, 1), lambda index: (index, 0)),
            pl.BlockSpec((1, length), lambda index: (0, 0)),
        ],
        out_specs=[block_spec, block_spec],
        out_shape=[result, result],
        name="self_forward",
    )(queries, keys, values, labels[:, None], labels[None, :])


def self_backward_body(
    query_ref,
    key_ref,
    value_ref,
    column_ref,
    row_ref,
    out_ref,
    log_ref,
    grad_ref,
    grad_query_ref,
    grad_key_ref,
    grad_value_ref,
    key_sum,
    value_sum,
):
    block = pl.program_id(0)
    block_count = pl.num_programs(0)

    @pl.when(block == 0)
    def clear():
        key_sum[...] = jnp.zeros_like(key_sum)
        value_sum[...] = jnp.zeros_like(value_sum)

    queries = stack_pair(query_ref[...] * jnp.bfloat16(0.125))
    query_label = row_ref[...]
    grad_rows = grad_ref[...]
    grads = stack_pair(grad_rows)
    products = stack_pair(grad_rows.astype(jnp.float32) * out_ref[...])
    delta = jnp.sum(jnp.transpose(products), axis=0, keepdims=True)
    log_columns = jnp.transpose(log_ref[...])
    logs = jnp.concatenate((log_columns[:1], log_columns[HEAD : HEAD + 1]), axis=1)

    def step(key_block, query_sum, masked):
        start = pl.multiple_of(key_block * KEY_BLOCK, KEY_BLOCK)
        here = pl.ds(start, KEY_BLOCK)
        keys = key_ref[here, :]
        scores = dot_rows(keys, queries)
        if masked:
            shape = (KEY_BLOCK, QUERY_BLOCK)
            allowed = block_allowed(
                block * QUERY_BLOCK + lax.broadcasted_iota(jnp.int32, shape, 1),
                start + lax.broadcasted_iota(jnp.int32, shape, 0),
                query_label,
                column_ref[here, :],
            )
            scores = jnp.concatenate(
                (
                    jnp.where(allowed, scores[:, :QUERY_BLOCK], neg_large),
                    jnp.where(allowed, scores[:, QUERY_BLOCK:], neg_large),
                ),
                axis=1,
            )
        probs = jnp.exp(scores - logs)
        grad_probs = dot_rows(value_ref[here, :], grads)
        grad_scores = rounded(probs * (grad_probs - delta))
        key_sum[here, :] = key_sum[here, :] + dot_plain(grad_scores, queries)
        value_sum[here, :] = value_sum[here, :] + dot_plain(rounded(probs), grads)
        return query_sum + dot_columns(grad_scores, keys)

    query_sum = jnp.zeros((2 * QUERY_BLOCK, PAIR), jnp.float32)
    full, last = key_block_range(block, key_ref.shape[0])
    query_sum = lax.fori_loop(0, full, lambda index, total: step(index, total, False), query_sum)
    query_sum = lax.fori_loop(full, last, lambda index, total: step(index, total, True), query_sum)
    grad_query_ref[...] = rounded(join_stack(query_sum) * 0.125)

    @pl.when(block == block_count - 1)
    def finish():
        grad_key_ref[...] = rounded(key_sum[...])
        grad_value_ref[...] = rounded(value_sum[...])


def self_backward(queries, keys, values, labels, attended, log_total, grad_attended):
    length = queries.shape[0]
    block_spec = pl.BlockSpec((QUERY_BLOCK, PAIR), lambda index: (index, 0))
    whole_spec = pl.BlockSpec((length, PAIR), lambda index: (0, 0))
    result = jax.ShapeDtypeStruct((length, PAIR), jnp.bfloat16)
    return pl.pallas_call(
        self_backward_body,
        grid=(length // QUERY_BLOCK,),
        in_specs=[
            block_spec,
            whole_spec,
            whole_spec,
            pl.BlockSpec((length, 1), lambda index: (0, 0)),
            pl.BlockSpec((1, QUERY_BLOCK), lambda index: (0, index)),
            block_spec,
            block_spec,
            block_spec,
        ],
        out_specs=[block_spec, whole_spec, whole_spec],
        out_shape=[result, result, result],
        scratch_shapes=[
            pltpu.VMEM((length, PAIR), jnp.float32),
            pltpu.VMEM((length, PAIR), jnp.float32),
        ],
        name="self_backward",
    )(queries, keys, values, labels[:, None], labels[None, :], attended, log_total, grad_attended)


def widen_body(frame_ref, out_ref):
    parts = D // 128
    for part in range(parts):
        out_ref[pl.ds(part, frame_ref.shape[0], stride=parts), :] = frame_ref[
            :, part * 128 : (part + 1) * 128
        ].astype(jnp.float32)


def widen_frames(frames):
    frame_count = frames.shape[0]
    parts = D // 128
    wide = pl.pallas_call(
        widen_body,
        grid=(6,),
        in_specs=[pl.BlockSpec((frame_count // 6, D), lambda index: (index, 0))],
        out_specs=pl.BlockSpec((frame_count // 6 * parts, 128), lambda index: (index, 0)),
        out_shape=jax.ShapeDtypeStruct((frame_count * parts, 128), jnp.float32),
        name="widen_frames",
    )(frames)
    return wide.reshape(frame_count, 1, D)


def place_rows(vectors, row_count):
    lead = vectors[0].shape[:-1]
    rows = lax.broadcasted_iota(jnp.int32, lead + (row_count, D), len(lead))
    block = jnp.zeros(rows.shape, jnp.bfloat16)
    for slot, vector in enumerate(vectors):
        padding = [(0, 0)] * len(lead) + [(0, D - vector.shape[-1])]
        wide = jnp.pad(vector.astype(jnp.bfloat16), padding)[..., None, :]
        block = jnp.where(rows == slot, wide, block)
    return block


def halve(buffer, axis, axis_name, flip, bit, kind=jnp.bfloat16):
    kept = lax.dynamic_index_in_dim(buffer, bit, axis, keepdims=False)
    sent = lax.dynamic_index_in_dim(buffer, 1 - bit, axis, keepdims=False)
    pairs = [(index, index ^ flip) for index in range(lax.axis_size(axis_name))]
    received = lax.ppermute(sent, axis_name, pairs)
    return (kept.astype(jnp.float32) + received.astype(jnp.float32)).astype(kind)


def frame_mask(length, shape):
    return lax.broadcasted_iota(jnp.int32, shape, 1) < length


def cross_forward_body(length_ref, query_ref, key_ref, value_ref, out_ref, log_ref):
    query_halves = split_pair(query_ref[...])
    value_halves = split_pair(value_ref[...])
    keys = key_ref[...]
    valid = frame_mask(length_ref[0], (query_ref.shape[0], keys.shape[0]))
    attended = jnp.zeros(query_ref.shape, jnp.float32)
    logs = []
    for half in range(2):
        scores = jnp.where(valid, dot_rows(query_halves[half], keys) * 0.125, neg_large)
        row_max = jnp.max(scores, axis=1, keepdims=True)
        exp_terms = jnp.exp(scores - row_max)
        total = jnp.sum(exp_terms, axis=1, keepdims=True)
        attended = attended + dot_plain(rounded(exp_terms), value_halves[half]) / total
        logs.append(row_max + jnp.log(total))
    out_ref[...] = rounded(attended)
    log_ref[...] = join_pair(logs[0], logs[1], log_ref.shape)


def cross_forward(lengths, queries, keys, values):
    query_spec = pl.BlockSpec((queries.shape[0], PAIR), lambda pair: (0, pair))
    frame_spec = pl.BlockSpec((keys.shape[0], PAIR), lambda pair: (0, pair))
    return pl.pallas_call(
        cross_forward_body,
        grid=(D // PAIR,),
        in_specs=[pl.BlockSpec(memory_space=pltpu.SMEM), query_spec, frame_spec, frame_spec],
        out_specs=[query_spec, query_spec],
        out_shape=[
            jax.ShapeDtypeStruct(queries.shape, jnp.bfloat16),
            jax.ShapeDtypeStruct(queries.shape, jnp.float32),
        ],
        name="cross_forward",
    )(lengths, queries, keys, values)


def cross_backward_body(
    length_ref, query_ref, key_ref, value_ref, log_ref, grad_ref, grad_query_ref, grad_frame_ref
):
    query_halves = split_pair(query_ref[...])
    grad_halves = split_pair(grad_ref[...])
    keys = key_ref[...]
    values = value_ref[...]
    key_halves = split_pair(keys)
    valid = frame_mask(length_ref[0], (query_ref.shape[0], keys.shape[0]))
    logs = (log_ref[:, :1], log_ref[:, HEAD : HEAD + 1])
    query_sum = jnp.zeros(query_ref.shape, jnp.float32)
    key_sum = jnp.zeros(keys.shape, jnp.float32)
    value_sum = jnp.zeros(keys.shape, jnp.float32)
    for half in range(2):
        scores = jnp.where(valid, dot_rows(query_halves[half], keys) * 0.125, neg_large)
        probs = jnp.exp(scores - logs[half])
        grad_probs = dot_rows(grad_halves[half], values)
        delta = jnp.sum(probs * grad_probs, axis=1, keepdims=True)
        grad_scores = rounded(probs * (grad_probs - delta) * 0.125)
        query_sum = query_sum + dot_plain(grad_scores, key_halves[half])
        key_sum = key_sum + dot_columns(grad_scores, query_halves[half])
        value_sum = value_sum + dot_columns(rounded(probs), grad_halves[half])
    grad_query_ref[...] = rounded(query_sum)
    grad_frame_ref[0] = rounded(key_sum)
    grad_frame_ref[1] = rounded(value_sum)


def cross_backward(lengths, queries, keys, values, log_total, grad_attended):
    query_spec = pl.BlockSpec((queries.shape[0], PAIR), lambda pair: (0, pair))
    frame_spec = pl.BlockSpec((keys.shape[0], PAIR), lambda pair: (0, pair))
    return pl.pallas_call(
        cross_backward_body,
        grid=(D // PAIR,),
        in_specs=[
            pl.BlockSpec(memory_space=pltpu.SMEM),
            query_spec,
            frame_spec,
            frame_spec,
            query_spec,
            query_spec,
        ],
        out_specs=[
            query_spec,
            pl.BlockSpec((2, keys.shape[0], PAIR), lambda pair: (0, 0, pair)),
        ],
        out_shape=[
            jax.ShapeDtypeStruct(queries.shape, jnp.bfloat16),
            jax.ShapeDtypeStruct((2,) + keys.shape, jnp.bfloat16),
        ],
        name="cross_backward",
    )(lengths, queries, keys, values, log_total, grad_attended)


def local_heads(
    tokens,
    memory,
    piece_starts,
    memory_lengths,
    self_gain,
    self_shift,
    query_weight,
    query_bias,
    key_weight,
    value_weight,
    value_bias,
    attn_out_weight,
    attn_out_bias,
    cross_gain,
    cross_shift,
    cross_query_weight,
    cross_query_bias,
    cross_key_weight,
    cross_value_weight,
    cross_value_bias,
    cross_out_weight,
    cross_out_bias,
    mlp_gain,
    mlp_shift,
    fc_in_weight,
    fc_in_bias,
    fc_out_weight,
    fc_out_bias,
    out_grad,
):
    local_len, batch_count, _ = tokens.shape
    seq_count = lax.axis_size("seq")
    seq_index = lax.axis_index("seq")
    full_length = local_len * seq_count
    token_count = local_len * batch_count
    query_pos = seq_index * local_len + jnp.arange(local_len, dtype=jnp.int32)
    labels = piece_labels(jnp.arange(full_length, dtype=jnp.int32), piece_starts).reshape(-1)
    input_rows = tokens.reshape(token_count, D).astype(jnp.float32)
    shard_rows = query_weight.shape[0]
    wide_parts = fc_in_weight.shape[1] // D
    vector_block = place_rows(
        (
            self_gain,
            self_shift,
            query_bias,
            value_bias,
            attn_out_bias,
            cross_gain,
            cross_shift,
            cross_query_bias,
            cross_value_bias,
            cross_out_bias,
            mlp_gain,
            mlp_shift,
            fc_out_bias,
            fc_in_bias,
        ),
        16,
    )
    fc_in_blocks = jnp.transpose(
        fc_in_weight.reshape(shard_rows, wide_parts, D), (1, 0, 2)
    ).reshape(wide_parts * shard_rows, D)
    first_packed = jnp.concatenate(
        (
            query_weight,
            key_weight,
            value_weight,
            cross_key_weight,
            cross_value_weight,
            vector_block,
        )
    )
    first = lax.all_gather(first_packed, ("dp", "seq"), axis=0, tiled=False)
    owners = first.shape[0]

    def owner_rows(matrix):
        return matrix.astype(jnp.bfloat16).reshape(owners, -1, D)

    def first_at(slot):
        return first[:, slot * shard_rows : (slot + 1) * shard_rows, :].reshape(D, D)

    full_query, full_key, full_value, full_cross_key, full_cross_value = (
        first_at(slot) for slot in range(5)
    )
    full_vectors = first[:, 5 * shard_rows :, :]
    packed = jnp.concatenate(
        (
            attn_out_weight,
            cross_query_weight,
            cross_out_weight,
            fc_in_blocks,
            fc_out_weight,
        )
    )
    packed, first = lax.optimization_barrier((packed, first))
    gathered = lax.all_gather(packed, ("dp", "seq"), axis=0, tiled=False)

    def square_at(slot):
        return gathered[:, slot * shard_rows : (slot + 1) * shard_rows, :].reshape(D, D)

    full_self_out, full_cross_query, full_cross_out = (square_at(slot) for slot in range(3))
    wide_start = 3 * shard_rows
    wide_stop = wide_start + wide_parts * shard_rows
    full_fc_in = jnp.transpose(
        gathered[:, wide_start:wide_stop, :].reshape(owners, wide_parts, shard_rows, D),
        (0, 2, 1, 3),
    ).reshape(D, wide_parts * D)
    out_stop = wide_stop + fc_out_weight.shape[0]
    full_fc_out = gathered[:, wide_stop:out_stop, :].reshape(wide_parts * D, D)

    def vector_at(slot):
        return full_vectors[:, slot, :shard_rows].reshape(D)

    (
        full_self_gain,
        full_self_shift,
        full_query_bias,
        full_value_bias,
        full_self_out_bias,
        full_cross_gain,
        full_cross_shift,
        full_cross_query_bias,
        full_cross_value_bias,
        full_cross_out_bias,
        full_mlp_gain,
        full_mlp_shift,
        full_fc_out_bias,
    ) = (vector_at(slot) for slot in range(13))
    full_fc_in_bias = full_vectors[:, 13, : fc_in_bias.shape[0]].reshape(-1)
    normed_self, scaled_self, inverse_self = norm_forward(
        input_rows, full_self_gain.astype(jnp.float32), full_self_shift.astype(jnp.float32)
    )
    normed_self_low = rounded(normed_self)
    query_rows = rounded(project(normed_self_low, full_query) + full_query_bias.astype(jnp.float32))
    key_rows = rounded(project(normed_self_low, full_key))
    value_rows = rounded(
        project(normed_self_low, full_value) + full_value_bias.astype(jnp.float32)
    )
    head_triple = lax.all_to_all(
        jnp.stack(
            tuple(to_pairs(rows, seq_count) for rows in (query_rows, key_rows, value_rows)), axis=1
        ),
        "seq",
        0,
        0,
    )
    head_queries, head_keys, head_values = (
        head_triple[:, slot].reshape(full_length, PAIR) for slot in range(3)
    )
    head_attended, head_log = self_forward(head_queries, head_keys, head_values, labels)
    attended_blocks = lax.all_to_all(
        rounded(head_attended).reshape(seq_count, local_len, PAIR), "seq", 0, 0
    )
    attended_self_low = from_pairs(attended_blocks)
    middle_rows = (
        input_rows
        + project(attended_self_low, full_self_out)
        + full_self_out_bias.astype(jnp.float32)
    )
    normed_cross, scaled_cross, inverse_cross = norm_forward(
        middle_rows, full_cross_gain.astype(jnp.float32), full_cross_shift.astype(jnp.float32)
    )
    normed_cross_low = rounded(normed_cross)
    cross_queries = rounded(
        project(normed_cross_low, full_cross_query) + full_cross_query_bias.astype(jnp.float32)
    )
    frame_count = memory.shape[0]
    frame_part = frame_count // seq_count
    frame_start = seq_index * frame_part
    memory_flat = memory.reshape(frame_count, D)
    memory_part = lax.dynamic_slice_in_dim(memory_flat, frame_start, frame_part, 0)
    memory_keys = rounded(project(memory_flat, full_cross_key))
    memory_values = rounded(
        project(memory_flat, full_cross_value) + full_cross_value_bias.astype(jnp.float32)
    )
    attended_cross_low, cross_log = cross_forward(
        memory_lengths, cross_queries, memory_keys, memory_values
    )
    after_rows = (
        middle_rows
        + project(attended_cross_low, full_cross_out)
        + full_cross_out_bias.astype(jnp.float32)
    )
    normed_mlp, scaled_mlp, inverse_mlp = norm_forward(
        after_rows, full_mlp_gain.astype(jnp.float32), full_mlp_shift.astype(jnp.float32)
    )
    normed_mlp_low = rounded(normed_mlp)
    hidden_pre = project(normed_mlp_low, full_fc_in) + full_fc_in_bias.astype(jnp.float32)
    activated, gelu_pull = jax.vjp(exact_gelu, hidden_pre)
    activated_low = rounded(activated)
    result_rows = (
        after_rows + project(activated_low, full_fc_out) + full_fc_out_bias.astype(jnp.float32)
    )
    output = rounded(result_rows).reshape(local_len, batch_count, D)
    back_fc_in, back_fc_out = full_fc_in, full_fc_out
    grad_result = out_grad.reshape(token_count, D)
    grad_mlp_low = rounded(grad_result)
    grad_fc_out_weight = weight_grad(activated_low, grad_mlp_low)
    grad_fc_out_bias = column_sums(grad_mlp_low)
    grad_activated = project_back(grad_mlp_low, back_fc_out)
    grad_hidden_low = rounded(gelu_pull(grad_activated)[0])
    grad_fc_in_blocks = tuple(
        weight_grad(normed_mlp_low, grad_hidden_low[:, part * D : (part + 1) * D])
        for part in range(wide_parts)
    )
    grad_fc_in_bias = column_sums(grad_hidden_low)
    grad_normed_mlp = project_back(grad_hidden_low, back_fc_in)
    grad_rows_mlp, grad_mlp_gain, grad_mlp_shift = norm_backward(
        grad_normed_mlp, scaled_mlp, inverse_mlp, full_mlp_gain.astype(jnp.float32)
    )
    grad_after = grad_result + grad_rows_mlp
    back_cross_query, back_cross_key, back_cross_value, back_cross_out = (
        full_cross_query,
        full_cross_key,
        full_cross_value,
        full_cross_out,
    )
    grad_cross_low = rounded(grad_after)
    grad_cross_out_weight = weight_grad(attended_cross_low, grad_cross_low)
    grad_cross_out_bias = column_sums(grad_cross_low)
    grad_attended_cross = rounded(project_back(grad_cross_low, back_cross_out))
    grad_cross_queries, grad_memory_kv = cross_backward(
        memory_lengths,
        cross_queries,
        memory_keys,
        memory_values,
        cross_log,
        grad_attended_cross,
    )
    dp_index = lax.axis_index("dp")
    core_bit, x_bit = dp_index % 2, dp_index // 2
    y_bit, low_bit, high_bit = seq_index % 2, (seq_index // 2) % 2, seq_index // 4
    memory_parts = grad_memory_kv.reshape(2, 2, 2, 2, frame_part, D)
    part_keys = halve(halve(memory_parts[0], 2, "seq", 1, y_bit), 1, "seq", 2, low_bit)
    part_values = halve(halve(memory_parts[1], 1, "seq", 2, low_bit), 1, "seq", 1, y_bit)
    part_flat_keys = halve(part_keys, 0, "seq", 4, high_bit)
    part_flat_values = halve(part_values, 0, "seq", 4, high_bit)
    part_memory_grad = (
        project_back(part_flat_keys, back_cross_key)
        + project_back(part_flat_values, back_cross_value)
    )
    grad_cross_key_weight = weight_grad(memory_part, part_flat_keys)
    grad_cross_value_weight = weight_grad(memory_part, part_flat_values)
    grad_cross_value_bias = column_sums(part_flat_values)
    grad_cross_query_weight = weight_grad(normed_cross_low, grad_cross_queries)
    grad_cross_query_bias = column_sums(grad_cross_queries)
    grad_normed_cross = project_back(grad_cross_queries, back_cross_query)
    grad_rows_cross, grad_cross_gain, grad_cross_shift = norm_backward(
        grad_normed_cross, scaled_cross, inverse_cross, full_cross_gain.astype(jnp.float32)
    )
    grad_middle = grad_after + grad_rows_cross
    back_query, back_key, back_value, back_self_out = (
        full_query,
        full_key,
        full_value,
        full_self_out,
    )
    grad_self_low = rounded(grad_middle)
    grad_attn_out_weight = weight_grad(attended_self_low, grad_self_low)
    grad_attn_out_bias = column_sums(grad_self_low)
    early_grads = jnp.concatenate(
        (
            *(owner_rows(block) for block in grad_fc_in_blocks),
            owner_rows(grad_fc_out_weight),
            owner_rows(grad_attn_out_weight),
            owner_rows(grad_cross_query_weight),
            owner_rows(grad_cross_out_weight),
        ),
        axis=1,
    )
    owned_early = lax.psum_scatter(
        early_grads, ("dp", "seq"), scatter_dimension=0, tiled=False
    )
    owned_early = owned_early.astype(jnp.float32)
    wide_rows = wide_parts * shard_rows
    owned_fc_in = jnp.transpose(
        owned_early[:wide_rows].reshape(wide_parts, shard_rows, D), (1, 0, 2)
    ).reshape(shard_rows, wide_parts * D)
    out_rows = wide_rows + fc_out_weight.shape[0]
    owned_fc_out = owned_early[wide_rows:out_rows]
    owned_middle = owned_early[out_rows:]
    grad_attended_self = rounded(project_back(grad_self_low, back_self_out))
    head_blocks = to_pairs(grad_attended_self, seq_count)
    head_grad = lax.all_to_all(head_blocks, "seq", 0, 0)
    head_grad = head_grad.reshape(full_length, PAIR)
    head_grads = self_backward(
        head_queries, head_keys, head_values, labels, head_attended, head_log, head_grad
    )
    grad_blocks = jnp.stack(
        tuple(part.reshape(seq_count, local_len, PAIR) for part in head_grads), axis=1
    )
    grad_triple = lax.all_to_all(grad_blocks, "seq", 0, 0)
    grad_query_low, grad_key_low, grad_value_low = (
        from_pairs(grad_triple[:, slot]) for slot in range(3)
    )
    grad_query_weight = weight_grad(normed_self_low, grad_query_low)
    grad_query_bias = column_sums(grad_query_low)
    grad_key_weight = weight_grad(normed_self_low, grad_key_low)
    grad_value_weight = weight_grad(normed_self_low, grad_value_low)
    grad_value_bias = column_sums(grad_value_low)
    grad_normed_self = (
        project_back(grad_query_low, back_query)
        + project_back(grad_key_low, back_key)
        + project_back(grad_value_low, back_value)
    )
    grad_rows_self, grad_self_gain, grad_self_shift = norm_backward(
        grad_normed_self, scaled_self, inverse_self, full_self_gain.astype(jnp.float32)
    )
    token_grad = (grad_middle + grad_rows_self).reshape(local_len, batch_count, D)
    late_block = place_rows(
        tuple(
            vector.reshape(owners, -1)
            for vector in (
                grad_self_gain,
                grad_self_shift,
                grad_query_bias,
                grad_value_bias,
                grad_attn_out_bias,
                grad_cross_gain,
                grad_cross_shift,
                grad_cross_query_bias,
                grad_cross_value_bias,
                grad_cross_out_bias,
                grad_mlp_gain,
                grad_mlp_shift,
                grad_fc_out_bias,
                grad_fc_in_bias,
            )
        ),
        16,
    )
    late_grads = jnp.concatenate(
        (
            owner_rows(grad_query_weight),
            owner_rows(grad_key_weight),
            owner_rows(grad_value_weight),
            owner_rows(grad_cross_key_weight),
            owner_rows(grad_cross_value_weight),
            late_block,
        ),
        axis=1,
    )
    late_rows = late_grads.shape[1]
    by_core = halve(late_grads.reshape(2, 2, 2, 2, 2, late_rows, D), 1, "dp", 1, core_bit)
    cut_row = late_rows // 16 * 8
    upper = by_core[:, :, :, :, :cut_row]
    lower = by_core[:, :, :, :, cut_row:]
    upper = halve(halve(upper, 0, "dp", 2, x_bit), 2, "seq", 1, y_bit)
    lower = halve(halve(lower, 3, "seq", 1, y_bit), 0, "dp", 2, x_bit)
    by_column = jnp.concatenate((upper, lower), axis=2)
    owned_late = halve(
        halve(by_column, 1, "seq", 2, low_bit), 0, "seq", 4, high_bit, jnp.float32
    )
    memory_grad = lax.all_gather(part_memory_grad.astype(jnp.bfloat16), "seq", axis=0, tiled=True)
    memory_grad = widen_frames(memory_grad)
    owned_vectors = owned_late[5 * shard_rows :]

    def own_square(slot):
        return owned_late[slot * shard_rows : (slot + 1) * shard_rows]

    def own_middle(slot):
        return owned_middle[slot * shard_rows : (slot + 1) * shard_rows]

    def own_vector(slot):
        return owned_vectors[slot, :shard_rows]

    owned_fc_in_bias = owned_vectors[13, : fc_in_bias.shape[0]]
    return (
        output,
        token_grad,
        memory_grad,
        own_vector(0),
        own_vector(1),
        own_square(0),
        own_vector(2),
        own_square(1),
        own_square(2),
        own_vector(3),
        own_middle(0),
        own_vector(4),
        own_vector(5),
        own_vector(6),
        own_middle(1),
        own_vector(7),
        own_square(3),
        own_square(4),
        own_vector(8),
        own_middle(2),
        own_vector(9),
        own_vector(10),
        own_vector(11),
        owned_fc_in,
        owned_fc_in_bias,
        owned_fc_out,
        own_vector(12),
    )


def local(
    tokens,
    memory,
    piece_starts,
    memory_lengths,
    self_gain,
    self_shift,
    query_weight,
    query_bias,
    key_weight,
    value_weight,
    value_bias,
    attn_out_weight,
    attn_out_bias,
    cross_gain,
    cross_shift,
    cross_query_weight,
    cross_query_bias,
    cross_key_weight,
    cross_value_weight,
    cross_value_bias,
    cross_out_weight,
    cross_out_bias,
    mlp_gain,
    mlp_shift,
    fc_in_weight,
    fc_in_bias,
    fc_out_weight,
    fc_out_bias,
    out_grad,
):
    local_len, batch_count, _ = tokens.shape
    seq_count = lax.axis_size("seq")
    seq_index = lax.axis_index("seq")
    full_length = local_len * seq_count
    token_count = local_len * batch_count
    query_pos = seq_index * local_len + jnp.arange(local_len, dtype=jnp.int32)
    query_label = piece_labels(query_pos, piece_starts)
    input_rows = tokens.reshape(token_count, D).astype(jnp.float32)
    shard_rows = query_weight.shape[0]
    wide_parts = fc_in_weight.shape[1] // D
    vectors = jnp.concatenate(
        (
            self_gain,
            self_shift,
            query_bias,
            value_bias,
            attn_out_bias,
            cross_gain,
            cross_shift,
            cross_query_bias,
            cross_value_bias,
            cross_out_bias,
            mlp_gain,
            mlp_shift,
            fc_out_bias,
            fc_in_bias,
        )
    )
    vector_rows = 8
    vector_block = jnp.pad(vectors, (0, vector_rows * D - vectors.shape[0])).reshape(vector_rows, D)
    fc_in_blocks = jnp.transpose(
        fc_in_weight.reshape(shard_rows, wide_parts, D), (1, 0, 2)
    ).reshape(wide_parts * shard_rows, D)
    packed = jnp.concatenate(
        (
            query_weight,
            key_weight,
            value_weight,
            attn_out_weight,
            cross_query_weight,
            cross_key_weight,
            cross_value_weight,
            cross_out_weight,
            fc_in_blocks,
            fc_out_weight,
            vector_block,
        )
    )
    gathered = lax.all_gather(packed, ("dp", "seq"), axis=0, tiled=False)
    owners = gathered.shape[0]

    def square_at(slot):
        return gathered[:, slot * shard_rows : (slot + 1) * shard_rows, :].reshape(D, D)

    full_query, full_key, full_value, full_self_out = (square_at(slot) for slot in range(4))
    full_cross_query, full_cross_key, full_cross_value, full_cross_out = (
        square_at(slot) for slot in range(4, 8)
    )
    wide_start = 8 * shard_rows
    wide_stop = wide_start + wide_parts * shard_rows
    full_fc_in = jnp.transpose(
        gathered[:, wide_start:wide_stop, :].reshape(owners, wide_parts, shard_rows, D),
        (0, 2, 1, 3),
    ).reshape(D, wide_parts * D)
    out_stop = wide_stop + fc_out_weight.shape[0]
    full_fc_out = gathered[:, wide_stop:out_stop, :].reshape(wide_parts * D, D)
    full_vectors = gathered[:, out_stop:, :].reshape(owners, vector_rows * D)

    def vector_at(slot):
        return full_vectors[:, slot * shard_rows : (slot + 1) * shard_rows].reshape(D)

    (
        full_self_gain,
        full_self_shift,
        full_query_bias,
        full_value_bias,
        full_self_out_bias,
        full_cross_gain,
        full_cross_shift,
        full_cross_query_bias,
        full_cross_value_bias,
        full_cross_out_bias,
        full_mlp_gain,
        full_mlp_shift,
        full_fc_out_bias,
    ) = (vector_at(slot) for slot in range(13))
    full_fc_in_bias = full_vectors[
        :, 13 * shard_rows : 13 * shard_rows + fc_in_bias.shape[0]
    ].reshape(-1)
    normed_self, scaled_self, inverse_self = norm_forward(
        input_rows, full_self_gain.astype(jnp.float32), full_self_shift.astype(jnp.float32)
    )
    normed_self_low = rounded(normed_self)
    query_rows = rounded(project(normed_self_low, full_query) + full_query_bias.astype(jnp.float32))
    key_rows = rounded(project(normed_self_low, full_key)).reshape(local_len, batch_count, D)
    value_rows = rounded(
        project(normed_self_low, full_value) + full_value_bias.astype(jnp.float32)
    ).reshape(local_len, batch_count, D)
    query_heads = query_rows.reshape(local_len, batch_count, HEADS, HEAD)

    def key_block_scores(key_block, key_pos):
        key_heads = key_block.reshape(key_block.shape[0], batch_count, HEADS, HEAD)
        raw_scores = jnp.einsum(
            "qbhd,kbhd->qbhk", query_heads, key_heads, preferred_element_type=jnp.float32
        )
        allowed = visible(query_pos, query_label, key_pos, piece_labels(key_pos, piece_starts))
        return (raw_scores * 0.125, allowed)

    start_state = (
        jnp.full((local_len, batch_count, HEADS), neg_large, jnp.float32),
        jnp.zeros((local_len, batch_count, HEADS), jnp.float32),
        jnp.zeros((local_len, batch_count, HEADS, HEAD), jnp.float32),
    )
    running = start_state
    kv_piece = lax.all_gather(
        jnp.concatenate((key_rows, value_rows), axis=2), "seq", axis=0, tiled=True
    )
    key_piece = kv_piece[:, :, :D]
    value_piece = kv_piece[:, :, D:]
    block_rows = math.gcd(key_piece.shape[0], 512)

    def fold_block(inner_state, block_index):
        row_max, row_total, weighted_sum = inner_state
        block_start = block_index * block_rows
        key_block = lax.dynamic_slice_in_dim(key_piece, block_start, block_rows, 0)
        value_block = lax.dynamic_slice_in_dim(value_piece, block_start, block_rows, 0).reshape(
            block_rows, batch_count, HEADS, HEAD
        )
        key_pos = block_start + jnp.arange(block_rows, dtype=jnp.int32)
        scores, allowed = key_block_scores(key_block, key_pos)
        new_max = jnp.maximum(row_max, jnp.max(jnp.where(allowed, scores, neg_large), axis=-1))
        exp_terms = jnp.where(allowed, jnp.exp(scores - new_max[..., None]), 0.0)
        factor = jnp.exp(row_max - new_max)
        row_total = row_total * factor + jnp.sum(exp_terms, axis=-1)
        weighted_sum = weighted_sum * factor[..., None] + jnp.einsum(
            "qbhk,kbhd->qbhd", rounded(exp_terms), value_block, preferred_element_type=jnp.float32
        )
        return ((new_max, row_total, weighted_sum), None)

    running, unused = lax.scan(
        fold_block, running, jnp.arange(key_piece.shape[0] // block_rows, dtype=jnp.int32)
    )
    row_max, row_total, weighted_sum = running
    attended_self = weighted_sum / row_total[..., None]
    log_total = row_max + jnp.log(row_total)
    attended_self_low = rounded(attended_self.reshape(token_count, D))
    middle_rows = (
        input_rows
        + project(attended_self_low, full_self_out)
        + full_self_out_bias.astype(jnp.float32)
    )
    normed_cross, scaled_cross, inverse_cross = norm_forward(
        middle_rows, full_cross_gain.astype(jnp.float32), full_cross_shift.astype(jnp.float32)
    )
    normed_cross_low = rounded(normed_cross)
    cross_queries = rounded(
        project(normed_cross_low, full_cross_query) + full_cross_query_bias.astype(jnp.float32)
    ).reshape(local_len, batch_count, HEADS, HEAD)
    frame_count = memory.shape[0]
    frame_part = frame_count // seq_count
    frame_start = seq_index * frame_part
    memory_part = lax.dynamic_slice_in_dim(memory, frame_start, frame_part, 0).reshape(
        frame_part * batch_count, D
    )
    memory_flat = memory.reshape(frame_count * batch_count, D)
    memory_keys = rounded(project(memory_flat, full_cross_key)).reshape(frame_count, batch_count, D)
    memory_values = rounded(
        project(memory_flat, full_cross_value) + full_cross_value_bias.astype(jnp.float32)
    ).reshape(frame_count, batch_count, D)
    memory_key_heads = memory_keys.reshape(frame_count, batch_count, HEADS, HEAD)
    memory_value_heads = memory_values.reshape(frame_count, batch_count, HEADS, HEAD)
    frame_valid = (jnp.arange(frame_count, dtype=jnp.int32)[None, :] < memory_lengths[:, None])[
        None, :, None, :
    ]
    cross_scores = (
        jnp.einsum(
            "qbhd,kbhd->qbhk", cross_queries, memory_key_heads, preferred_element_type=jnp.float32
        )
        * 0.125
    )
    cross_max = jnp.max(jnp.where(frame_valid, cross_scores, neg_large), axis=-1, keepdims=True)
    cross_exp = jnp.where(frame_valid, jnp.exp(cross_scores - cross_max), 0.0)
    cross_probs = cross_exp / jnp.sum(cross_exp, axis=-1, keepdims=True)
    cross_probs_low = rounded(cross_probs)
    attended_cross = jnp.einsum(
        "qbhk,kbhd->qbhd", cross_probs_low, memory_value_heads, preferred_element_type=jnp.float32
    )
    attended_cross_low = rounded(attended_cross.reshape(token_count, D))
    after_rows = (
        middle_rows
        + project(attended_cross_low, full_cross_out)
        + full_cross_out_bias.astype(jnp.float32)
    )
    normed_mlp, scaled_mlp, inverse_mlp = norm_forward(
        after_rows, full_mlp_gain.astype(jnp.float32), full_mlp_shift.astype(jnp.float32)
    )
    normed_mlp_low = rounded(normed_mlp)
    hidden_pre = project(normed_mlp_low, full_fc_in) + full_fc_in_bias.astype(jnp.float32)
    activated, gelu_pull = jax.vjp(exact_gelu, hidden_pre)
    activated_low = rounded(activated)
    result_rows = (
        after_rows + project(activated_low, full_fc_out) + full_fc_out_bias.astype(jnp.float32)
    )
    output = rounded(result_rows).reshape(local_len, batch_count, D)
    back_fc_in, back_fc_out = full_fc_in, full_fc_out
    grad_result = out_grad.reshape(token_count, D)
    grad_mlp_low = rounded(grad_result)
    grad_fc_out_weight = weight_grad(activated_low, grad_mlp_low)
    grad_fc_out_bias = column_sums(grad_mlp_low)
    grad_activated = project_back(grad_mlp_low, back_fc_out)
    grad_hidden_low = rounded(gelu_pull(grad_activated)[0])
    grad_fc_in_weight = weight_grad(normed_mlp_low, grad_hidden_low)
    grad_fc_in_bias = column_sums(grad_hidden_low)
    grad_normed_mlp = project_back(grad_hidden_low, back_fc_in)
    grad_rows_mlp, grad_mlp_gain, grad_mlp_shift = norm_backward(
        grad_normed_mlp, scaled_mlp, inverse_mlp, full_mlp_gain.astype(jnp.float32)
    )
    early_grads = jnp.concatenate(
        (
            jnp.transpose(
                grad_fc_in_weight.astype(jnp.bfloat16).reshape(
                    owners, shard_rows, wide_parts, D
                ),
                (0, 2, 1, 3),
            ).reshape(owners, wide_parts * shard_rows, D),
            grad_fc_out_weight.astype(jnp.bfloat16).reshape(owners, -1, D),
        ),
        axis=1,
    )
    owned_early = lax.psum_scatter(
        early_grads, ("dp", "seq"), scatter_dimension=0, tiled=False
    ).astype(jnp.float32)
    wide_rows = wide_parts * shard_rows
    owned_fc_in = jnp.transpose(
        owned_early[:wide_rows].reshape(wide_parts, shard_rows, D), (1, 0, 2)
    ).reshape(shard_rows, wide_parts * D)
    owned_fc_out = owned_early[wide_rows:]
    grad_after = grad_result + grad_rows_mlp
    back_cross_query, back_cross_key, back_cross_value, back_cross_out = (
        full_cross_query,
        full_cross_key,
        full_cross_value,
        full_cross_out,
    )
    grad_cross_low = rounded(grad_after)
    grad_cross_out_weight = weight_grad(attended_cross_low, grad_cross_low)
    grad_cross_out_bias = column_sums(grad_cross_low)
    grad_attended_cross = rounded(project_back(grad_cross_low, back_cross_out)).reshape(
        local_len, batch_count, HEADS, HEAD
    )
    grad_cross_probs = jnp.einsum(
        "qbhd,kbhd->qbhk",
        grad_attended_cross,
        memory_value_heads,
        preferred_element_type=jnp.float32,
    )
    cross_delta = jnp.sum(cross_probs * grad_cross_probs, axis=-1, keepdims=True)
    grad_cross_scores = rounded(cross_probs * (grad_cross_probs - cross_delta) * 0.125)
    grad_cross_queries = rounded(
        jnp.einsum(
            "qbhk,kbhd->qbhd",
            grad_cross_scores,
            memory_key_heads,
            preferred_element_type=jnp.float32,
        ).reshape(token_count, D)
    )
    grad_memory_keys = jnp.einsum(
        "qbhk,qbhd->kbhd", grad_cross_scores, cross_queries, preferred_element_type=jnp.float32
    ).reshape(frame_count, batch_count, D)
    grad_memory_values = jnp.einsum(
        "qbhk,qbhd->kbhd", cross_probs_low, grad_attended_cross, preferred_element_type=jnp.float32
    ).reshape(frame_count, batch_count, D)
    grad_memory_kv = jnp.concatenate((grad_memory_keys, grad_memory_values), axis=2)
    grad_cross_query_weight = weight_grad(normed_cross_low, grad_cross_queries)
    grad_cross_query_bias = column_sums(grad_cross_queries)
    grad_normed_cross = project_back(grad_cross_queries, back_cross_query)
    grad_rows_cross, grad_cross_gain, grad_cross_shift = norm_backward(
        grad_normed_cross, scaled_cross, inverse_cross, full_cross_gain.astype(jnp.float32)
    )
    grad_middle = grad_after + grad_rows_cross
    back_query, back_key, back_value, back_self_out = (
        full_query,
        full_key,
        full_value,
        full_self_out,
    )
    grad_self_low = rounded(grad_middle)
    grad_attn_out_weight = weight_grad(attended_self_low, grad_self_low)
    grad_attn_out_bias = column_sums(grad_self_low)
    grad_attended_self = rounded(project_back(grad_self_low, back_self_out)).reshape(
        local_len, batch_count, HEADS, HEAD
    )
    self_delta = jnp.sum(grad_attended_self.astype(jnp.float32) * attended_self, axis=-1)

    def score_grads(key_block, value_block, key_pos):
        scores, allowed = key_block_scores(key_block, key_pos)
        attn_probs = jnp.where(allowed, jnp.exp(scores - log_total[..., None]), 0.0)
        grad_probs = jnp.einsum(
            "qbhd,kbhd->qbhk", grad_attended_self, value_block, preferred_element_type=jnp.float32
        )
        grad_scores = rounded(attn_probs * (grad_probs - self_delta[..., None]) * 0.125)
        return (grad_scores, attn_probs)

    zero_query_grad = jnp.zeros((local_len, batch_count, HEADS, HEAD), jnp.float32)
    back_state = (zero_query_grad, jnp.zeros((full_length, batch_count, 2 * D), jnp.float32))
    running = back_state
    self_key_piece = key_piece
    self_value_piece = value_piece
    self_block_rows = math.gcd(self_key_piece.shape[0], 512)

    def back_block(inner_state, block_index):
        grad_query_sum, kv_grads = inner_state
        block_start = block_index * self_block_rows
        key_block = lax.dynamic_slice_in_dim(self_key_piece, block_start, self_block_rows, 0)
        value_block = lax.dynamic_slice_in_dim(
            self_value_piece, block_start, self_block_rows, 0
        ).reshape(self_block_rows, batch_count, HEADS, HEAD)
        key_pos = block_start + jnp.arange(self_block_rows, dtype=jnp.int32)
        grad_scores, attn_probs = score_grads(key_block, value_block, key_pos)
        key_heads = key_block.reshape(self_block_rows, batch_count, HEADS, HEAD)
        grad_query_sum = grad_query_sum + jnp.einsum(
            "qbhk,kbhd->qbhd", grad_scores, key_heads, preferred_element_type=jnp.float32
        )
        grad_key_block = jnp.einsum(
            "qbhk,qbhd->kbhd", grad_scores, query_heads, preferred_element_type=jnp.float32
        ).reshape(self_block_rows, batch_count, D)
        grad_value_block = jnp.einsum(
            "qbhk,qbhd->kbhd",
            rounded(attn_probs),
            grad_attended_self,
            preferred_element_type=jnp.float32,
        ).reshape(self_block_rows, batch_count, D)
        kv_grads = lax.dynamic_update_slice_in_dim(
            kv_grads, jnp.concatenate((grad_key_block, grad_value_block), axis=2), block_start, 0
        )
        return ((grad_query_sum, kv_grads), None)

    running, unused = lax.scan(
        back_block, running, jnp.arange(self_key_piece.shape[0] // self_block_rows, dtype=jnp.int32)
    )
    grad_query_sum = running[0]
    joint_kv = jnp.concatenate(
        (
            running[1].astype(jnp.bfloat16).reshape(seq_count, local_len, batch_count, 2 * D),
            grad_memory_kv.astype(jnp.bfloat16).reshape(
                seq_count, frame_part, batch_count, 2 * D
            ),
        ),
        axis=1,
    )
    own_joint = lax.psum_scatter(joint_kv, "seq", scatter_dimension=0, tiled=False)
    own_kv = own_joint[:local_len]
    part_kv = own_joint[local_len:]
    grad_key_low = own_kv[:, :, :D].reshape(token_count, D)
    grad_value_low = own_kv[:, :, D:].reshape(token_count, D)
    part_flat_keys = part_kv[:, :, :D].reshape(frame_part * batch_count, D)
    part_flat_values = part_kv[:, :, D:].reshape(frame_part * batch_count, D)
    part_memory_grad = (
        project_back(part_flat_keys, back_cross_key)
        + project_back(part_flat_values, back_cross_value)
    ).reshape(frame_part, batch_count, D)
    grad_cross_key_weight = weight_grad(memory_part, part_flat_keys)
    grad_cross_value_weight = weight_grad(memory_part, part_flat_values)
    grad_cross_value_bias = column_sums(part_flat_values)
    grad_query_low = rounded(grad_query_sum.reshape(token_count, D))
    grad_query_weight = weight_grad(normed_self_low, grad_query_low)
    grad_query_bias = column_sums(grad_query_low)
    grad_key_weight = weight_grad(normed_self_low, grad_key_low)
    grad_value_weight = weight_grad(normed_self_low, grad_value_low)
    grad_value_bias = column_sums(grad_value_low)
    grad_normed_self = (
        project_back(grad_query_low, back_query)
        + project_back(grad_key_low, back_key)
        + project_back(grad_value_low, back_value)
    )
    grad_rows_self, grad_self_gain, grad_self_shift = norm_backward(
        grad_normed_self, scaled_self, inverse_self, full_self_gain.astype(jnp.float32)
    )
    token_grad = (grad_middle + grad_rows_self).reshape(local_len, batch_count, D)

    def owner_rows(matrix):
        return matrix.astype(jnp.bfloat16).reshape(owners, -1, D)

    late_vectors = jnp.concatenate(
        tuple(
            vector.reshape(owners, -1)
            for vector in (
                grad_self_gain,
                grad_self_shift,
                grad_query_bias,
                grad_value_bias,
                grad_attn_out_bias,
                grad_cross_gain,
                grad_cross_shift,
                grad_cross_query_bias,
                grad_cross_value_bias,
                grad_cross_out_bias,
                grad_mlp_gain,
                grad_mlp_shift,
                grad_fc_out_bias,
                grad_fc_in_bias,
            )
        ),
        axis=1,
    )
    late_block = jnp.pad(
        late_vectors.astype(jnp.bfloat16),
        ((0, 0), (0, vector_rows * D - late_vectors.shape[1])),
    ).reshape(owners, vector_rows, D)
    late_grads = jnp.concatenate(
        (
            owner_rows(grad_query_weight),
            owner_rows(grad_key_weight),
            owner_rows(grad_value_weight),
            owner_rows(grad_attn_out_weight),
            owner_rows(grad_cross_query_weight),
            owner_rows(grad_cross_key_weight),
            owner_rows(grad_cross_value_weight),
            owner_rows(grad_cross_out_weight),
            late_block,
        ),
        axis=1,
    )
    owned_late = lax.psum_scatter(
        late_grads, ("dp", "seq"), scatter_dimension=0, tiled=False
    ).astype(jnp.float32)
    memory_grad = lax.all_gather(
        part_memory_grad.astype(jnp.bfloat16), "seq", axis=0, tiled=True
    ).astype(jnp.float32)
    owned_vectors = owned_late[8 * shard_rows :].reshape(-1)

    def own_square(slot):
        return owned_late[slot * shard_rows : (slot + 1) * shard_rows]

    def own_vector(slot):
        return owned_vectors[slot * shard_rows : (slot + 1) * shard_rows]

    owned_fc_in_bias = owned_vectors[13 * shard_rows : 13 * shard_rows + fc_in_bias.shape[0]]
    return (
        output,
        token_grad,
        memory_grad,
        own_vector(0),
        own_vector(1),
        own_square(0),
        own_vector(2),
        own_square(1),
        own_square(2),
        own_vector(3),
        own_square(3),
        own_vector(4),
        own_vector(5),
        own_vector(6),
        own_square(4),
        own_vector(7),
        own_square(5),
        own_square(6),
        own_vector(8),
        own_square(7),
        own_vector(9),
        own_vector(10),
        own_vector(11),
        owned_fc_in,
        owned_fc_in_bias,
        owned_fc_out,
        own_vector(12),
    )


def solution(mesh):
    in_specs = (
        P("seq", "dp", None),
        P(None, "dp", None),
        P("dp", None),
        P("dp"),
        P(("dp", "seq")),
        P(("dp", "seq")),
        P(("dp", "seq"), None),
        P(("dp", "seq")),
        P(("dp", "seq"), None),
        P(("dp", "seq"), None),
        P(("dp", "seq")),
        P(("dp", "seq"), None),
        P(("dp", "seq")),
        P(("dp", "seq")),
        P(("dp", "seq")),
        P(("dp", "seq"), None),
        P(("dp", "seq")),
        P(("dp", "seq"), None),
        P(("dp", "seq"), None),
        P(("dp", "seq")),
        P(("dp", "seq"), None),
        P(("dp", "seq")),
        P(("dp", "seq")),
        P(("dp", "seq")),
        P(("dp", "seq"), None),
        P(("dp", "seq")),
        P(("dp", "seq"), None),
        P(("dp", "seq")),
        P("seq", "dp", None),
    )
    out_specs = (
        P("seq", "dp", None),
        P("seq", "dp", None),
        P(None, "dp", None),
        P(("dp", "seq")),
        P(("dp", "seq")),
        P(("dp", "seq"), None),
        P(("dp", "seq")),
        P(("dp", "seq"), None),
        P(("dp", "seq"), None),
        P(("dp", "seq")),
        P(("dp", "seq"), None),
        P(("dp", "seq")),
        P(("dp", "seq")),
        P(("dp", "seq")),
        P(("dp", "seq"), None),
        P(("dp", "seq")),
        P(("dp", "seq"), None),
        P(("dp", "seq"), None),
        P(("dp", "seq")),
        P(("dp", "seq"), None),
        P(("dp", "seq")),
        P(("dp", "seq")),
        P(("dp", "seq")),
        P(("dp", "seq"), None),
        P(("dp", "seq")),
        P(("dp", "seq"), None),
        P(("dp", "seq")),
    )
    by_heads = mesh.shape["dp"] == 4 and mesh.shape["seq"] == 8

    def layer(*arrays):
        return local_heads(*arrays)

    return jax.shard_map(
        layer if by_heads else local,
        mesh=mesh,
        in_specs=in_specs,
        out_specs=out_specs,
        check_vma=False,
    )
```

```python
import math

import jax
import jax.numpy as jnp
from jax import lax
from jax.experimental import pallas as pl
from jax.experimental.pallas import tpu as pltpu
from jax.sharding import PartitionSpec as P


D = 768
HEADS = 12
HEAD = 64
PIECE = 256


norm_epsilon = 1e-05
neg_large = -1e30


def rounded(tensor):
    return tensor.astype(jnp.bfloat16)


def project(left_rows, matrix):
    return jnp.dot(left_rows, matrix, preferred_element_type=jnp.float32)


def project_back(left_rows, matrix):
    return lax.dot_general(
        left_rows, matrix, (((1,), (1,)), ((), ())), preferred_element_type=jnp.float32
    )


def weight_grad(inputs, grad_rows):
    return lax.dot_general(
        inputs, grad_rows, (((0,), (0,)), ((), ())), preferred_element_type=jnp.float32
    )


def column_sums(grad_rows):
    return jnp.sum(grad_rows.astype(jnp.float32), axis=0)


def row_sums(grad_rows):
    return jnp.sum(grad_rows.astype(jnp.float32), axis=0, keepdims=True)


def exact_gelu(inputs):
    return jax.nn.gelu(inputs, approximate=False)


def norm_forward(token_rows, norm_gain, norm_shift):
    centre = token_rows - jnp.mean(token_rows, axis=-1, keepdims=True)
    inverse = lax.rsqrt(jnp.mean(centre * centre, axis=-1, keepdims=True) + norm_epsilon)
    scaled = centre * inverse
    return (scaled * norm_gain + norm_shift, scaled, inverse)


def norm_backward(grad_normed, scaled, inverse, norm_gain):
    grad_scaled = grad_normed * norm_gain
    mean_grad = jnp.mean(grad_scaled, axis=-1, keepdims=True)
    mean_cross = jnp.mean(grad_scaled * scaled, axis=-1, keepdims=True)
    grad_input = inverse * (grad_scaled - mean_grad - scaled * mean_cross)
    return (grad_input, jnp.sum(grad_normed * scaled, axis=0), jnp.sum(grad_normed, axis=0))


def piece_labels(positions, starts):
    inside = (positions[None, :, None] >= starts[:, None, :]) & (
        positions[None, :, None] < starts[:, None, :] + PIECE
    )
    numbers = jnp.arange(1, starts.shape[1] + 1, dtype=jnp.int32)
    return jnp.sum(jnp.where(inside, numbers, 0), axis=2)


def visible(query_pos, query_label, key_pos, key_label):
    causal = (key_pos[None, :] <= query_pos[:, None])[:, None, :]
    query_side = jnp.transpose(query_label)[:, :, None]
    same_piece = (query_side == key_label[None, :, :]) & (query_side > 0)
    return (causal | same_piece)[:, :, None, :]


PAIR = 2 * HEAD
QUERY_BLOCK = 256
KEY_BLOCK = 512


def to_pairs(rows, seq_count):
    blocks = jnp.transpose(rows.reshape(rows.shape[0], D // PAIR, PAIR), (1, 0, 2))
    return jnp.pad(blocks, ((0, seq_count - D // PAIR), (0, 0), (0, 0)))


def from_pairs(blocks):
    kept = blocks[: D // PAIR]
    return jnp.transpose(kept, (1, 0, 2)).reshape(kept.shape[1], D)


def dot_rows(left, right):
    return lax.dot_general(left, right, (((1,), (1,)), ((), ())), preferred_element_type=jnp.float32)


def dot_plain(left, right):
    return lax.dot_general(left, right, (((1,), (0,)), ((), ())), preferred_element_type=jnp.float32)


def dot_columns(left, right):
    return lax.dot_general(left, right, (((0,), (0,)), ((), ())), preferred_element_type=jnp.float32)


def split_pair(block):
    lanes = lax.broadcasted_iota(jnp.int32, block.shape, 1)
    zero = jnp.zeros_like(block)
    return (jnp.where(lanes < HEAD, block, zero), jnp.where(lanes < HEAD, zero, block))


def join_pair(first, second, shape):
    lanes = lax.broadcasted_iota(jnp.int32, shape, 1)
    return jnp.where(lanes < HEAD, first, second)


def stack_pair(block):
    return jnp.concatenate(split_pair(block), axis=0)


def join_stack(stacked):
    rows = stacked.shape[0] // 2
    return join_pair(stacked[:rows], stacked[rows:], (rows, stacked.shape[1]))


def block_allowed(query_pos, key_pos, query_label, key_label):
    same_piece = (query_label == key_label) & (query_label > 0)
    return (key_pos <= query_pos) | same_piece


def key_rows_at(ref, key_block):
    parts = KEY_BLOCK // QUERY_BLOCK
    return ref[pl.ds(key_block * parts, parts), 0].reshape(KEY_BLOCK, PAIR)


def exchange_specs(owners):
    return [
        pl.BlockSpec((1, 1, QUERY_BLOCK, PAIR), lambda index: (index, 0, 0, 0)),
        pl.BlockSpec((owners, 1, QUERY_BLOCK, PAIR), lambda index: (0, 1, 0, 0)),
        pl.BlockSpec((owners, 1, QUERY_BLOCK, PAIR), lambda index: (0, 2, 0, 0)),
    ]


def key_block_range(block, key_rows):
    full = block * QUERY_BLOCK // KEY_BLOCK
    last = ((block + 2) * QUERY_BLOCK + KEY_BLOCK - 1) // KEY_BLOCK
    return (full, jnp.minimum(last, key_rows // KEY_BLOCK))


def self_forward_body(
    query_ref, key_ref, value_ref, column_ref, row_ref, out_ref, log_ref, low_ref
):
    block = pl.program_id(0)
    queries = stack_pair(query_ref[0, 0] * jnp.bfloat16(0.125))
    query_label = column_ref[...]

    def step(key_block, state, masked):
        start = pl.multiple_of(key_block * KEY_BLOCK, KEY_BLOCK)
        here = pl.ds(start, KEY_BLOCK)
        row_max, row_total, weighted = state
        scores = dot_rows(queries, key_rows_at(key_ref, key_block))
        if masked:
            shape = (QUERY_BLOCK, KEY_BLOCK)
            allowed = block_allowed(
                block * QUERY_BLOCK + lax.broadcasted_iota(jnp.int32, shape, 0),
                start + lax.broadcasted_iota(jnp.int32, shape, 1),
                query_label,
                row_ref[:, here],
            )
            scores = jnp.concatenate(
                (
                    jnp.where(allowed, scores[:QUERY_BLOCK], neg_large),
                    jnp.where(allowed, scores[QUERY_BLOCK:], neg_large),
                ),
                axis=0,
            )
        new_max = jnp.maximum(row_max, jnp.max(scores, axis=1, keepdims=True))
        exp_terms = jnp.exp(scores - new_max)
        factor = jnp.exp(row_max - new_max)
        row_total = row_total * factor + jnp.sum(exp_terms, axis=1, keepdims=True)
        weighted = weighted * factor + dot_plain(
            rounded(exp_terms), key_rows_at(value_ref, key_block)
        )
        return (new_max, row_total, weighted)

    state = (
        jnp.full((2 * QUERY_BLOCK, 1), neg_large, jnp.float32),
        jnp.zeros((2 * QUERY_BLOCK, 1), jnp.float32),
        jnp.zeros((2 * QUERY_BLOCK, PAIR), jnp.float32),
    )
    full, last = key_block_range(block, key_ref.shape[0] * QUERY_BLOCK)
    state = lax.fori_loop(0, full, lambda index, state: step(index, state, False), state)
    state = lax.fori_loop(full, last, lambda index, state: step(index, state, True), state)
    row_max, row_total, weighted = state
    attended = join_stack(weighted / row_total)
    out_ref[...] = attended
    low_ref[0] = rounded(attended)
    log_ref[...] = join_stack(jnp.broadcast_to(row_max + jnp.log(row_total), weighted.shape))


def self_forward(triple, labels):
    owners = triple.shape[0]
    length = owners * QUERY_BLOCK
    block_spec = pl.BlockSpec((QUERY_BLOCK, PAIR), lambda index: (index, 0))
    result = jax.ShapeDtypeStruct((length, PAIR), jnp.float32)
    return pl.pallas_call(
        self_forward_body,
        grid=(owners,),
        in_specs=exchange_specs(owners)
        + [
            pl.BlockSpec((QUERY_BLOCK, 1), lambda index: (index, 0)),
            pl.BlockSpec((1, length), lambda index: (0, 0)),
        ],
        out_specs=[
            block_spec,
            block_spec,
            pl.BlockSpec((1, QUERY_BLOCK, PAIR), lambda index: (index, 0, 0)),
        ],
        out_shape=[
            result,
            result,
            jax.ShapeDtypeStruct((owners, QUERY_BLOCK, PAIR), jnp.bfloat16),
        ],
        name="self_forward",
    )(triple, triple, triple, labels[:, None], labels[None, :])


def self_backward_body(
    query_ref,
    key_ref,
    value_ref,
    column_ref,
    row_ref,
    out_ref,
    log_ref,
    grad_ref,
    triple_ref,
    key_sum,
    value_sum,
):
    block = pl.program_id(0)
    block_count = pl.num_programs(0)

    @pl.when(block == 0)
    def clear():
        key_sum[...] = jnp.zeros_like(key_sum)
        value_sum[...] = jnp.zeros_like(value_sum)

    queries = stack_pair(query_ref[0, 0] * jnp.bfloat16(0.125))
    query_label = row_ref[...]
    grad_rows = grad_ref[0]
    grads = stack_pair(grad_rows)
    products = stack_pair(grad_rows.astype(jnp.float32) * out_ref[...])
    delta = jnp.sum(jnp.transpose(products), axis=0, keepdims=True)
    log_columns = jnp.transpose(log_ref[...])
    logs = jnp.concatenate((log_columns[:1], log_columns[HEAD : HEAD + 1]), axis=1)

    def step(key_block, query_sum, masked):
        start = pl.multiple_of(key_block * KEY_BLOCK, KEY_BLOCK)
        here = pl.ds(start, KEY_BLOCK)
        keys = key_rows_at(key_ref, key_block)
        scores = dot_rows(keys, queries)
        if masked:
            shape = (KEY_BLOCK, QUERY_BLOCK)
            allowed = block_allowed(
                block * QUERY_BLOCK + lax.broadcasted_iota(jnp.int32, shape, 1),
                start + lax.broadcasted_iota(jnp.int32, shape, 0),
                query_label,
                column_ref[here, :],
            )
            scores = jnp.concatenate(
                (
                    jnp.where(allowed, scores[:, :QUERY_BLOCK], neg_large),
                    jnp.where(allowed, scores[:, QUERY_BLOCK:], neg_large),
                ),
                axis=1,
            )
        probs = jnp.exp(scores - logs)
        grad_probs = dot_rows(key_rows_at(value_ref, key_block), grads)
        grad_scores = rounded(probs * (grad_probs - delta))
        key_sum[here, :] = key_sum[here, :] + dot_plain(grad_scores, queries)
        value_sum[here, :] = value_sum[here, :] + dot_plain(rounded(probs), grads)
        return query_sum + dot_columns(grad_scores, keys)

    query_sum = jnp.zeros((2 * QUERY_BLOCK, PAIR), jnp.float32)
    full, last = key_block_range(block, key_ref.shape[0] * QUERY_BLOCK)
    query_sum = lax.fori_loop(0, full, lambda index, total: step(index, total, False), query_sum)
    query_sum = lax.fori_loop(full, last, lambda index, total: step(index, total, True), query_sum)
    triple_ref[block, 0] = rounded(join_stack(query_sum) * 0.125)

    @pl.when(block == block_count - 1)
    def finish():
        for owner in range(triple_ref.shape[0]):
            rows = slice(owner * QUERY_BLOCK, (owner + 1) * QUERY_BLOCK)
            triple_ref[owner, 1] = rounded(key_sum[rows, :])
            triple_ref[owner, 2] = rounded(value_sum[rows, :])


def self_backward(triple, labels, attended, log_total, grad_attended):
    owners = triple.shape[0]
    length = owners * QUERY_BLOCK
    block_spec = pl.BlockSpec((QUERY_BLOCK, PAIR), lambda index: (index, 0))
    return pl.pallas_call(
        self_backward_body,
        grid=(owners,),
        in_specs=exchange_specs(owners)
        + [
            pl.BlockSpec((length, 1), lambda index: (0, 0)),
            pl.BlockSpec((1, QUERY_BLOCK), lambda index: (0, index)),
            block_spec,
            block_spec,
            pl.BlockSpec((1, QUERY_BLOCK, PAIR), lambda index: (index, 0, 0)),
        ],
        out_specs=pl.BlockSpec(triple.shape, lambda index: (0, 0, 0, 0)),
        out_shape=jax.ShapeDtypeStruct(triple.shape, jnp.bfloat16),
        scratch_shapes=[
            pltpu.VMEM((length, PAIR), jnp.float32),
            pltpu.VMEM((length, PAIR), jnp.float32),
        ],
        name="self_backward",
    )(
        triple,
        triple,
        triple,
        labels[:, None],
        labels[None, :],
        attended,
        log_total,
        grad_attended,
    )


def pack_body(*refs):
    row_refs, wide_ref, out_ref, stacked = refs[:-3], refs[-3], refs[-2], refs[-1]
    stacked[...] = jnp.zeros_like(stacked)
    for slot, ref in enumerate(row_refs):
        stacked[slot : slot + 1, :] = ref[...]
    rows = stacked[...]
    wide = jnp.broadcast_to(wide_ref[...], (16, wide_ref.shape[1]))
    owners = out_ref.shape[0]
    narrow, long = rows.shape[1] // owners, wide.shape[1] // owners
    lanes = lax.broadcasted_iota(jnp.int32, (16, 128), 1)
    slots = lax.broadcasted_iota(jnp.int32, (16, 128), 0)
    out_ref[...] = jnp.zeros_like(out_ref)

    def window(source, start, width):
        base = min(start // 128 * 128, source.shape[1] - 256)
        offset = start - base
        moved = source[:, base : base + 256]
        if offset:
            moved = pltpu.roll(moved, 256 - offset, 1)
        return jnp.where(lanes < width, moved[:, :128], 0.0)

    for owner in range(owners):
        block = window(rows, owner * narrow, narrow)
        long_block = window(wide, owner * long, long)
        block = jnp.where(slots == len(row_refs), long_block, block)
        out_ref[owner, :, :128] = rounded(block)


def pack_vectors(vectors, wide, owners):
    rows = tuple(vector.reshape(1, -1) for vector in vectors)
    return pl.pallas_call(
        pack_body,
        out_shape=jax.ShapeDtypeStruct((owners, 16, D), jnp.bfloat16),
        scratch_shapes=[pltpu.VMEM((16, D), jnp.float32)],
        name="pack_vectors",
    )(*rows, wide.reshape(1, -1))


def widen_body(frame_ref, out_ref):
    parts = D // 128
    for part in range(parts):
        out_ref[pl.ds(part, frame_ref.shape[0], stride=parts), :] = frame_ref[
            :, part * 128 : (part + 1) * 128
        ].astype(jnp.float32)


def widen_frames(frames):
    frame_count = frames.shape[0]
    parts = D // 128
    wide = pl.pallas_call(
        widen_body,
        grid=(6,),
        in_specs=[pl.BlockSpec((frame_count // 6, D), lambda index: (index, 0))],
        out_specs=pl.BlockSpec((frame_count // 6 * parts, 128), lambda index: (index, 0)),
        out_shape=jax.ShapeDtypeStruct((frame_count * parts, 128), jnp.float32),
        name="widen_frames",
    )(frames)
    return wide.reshape(frame_count, 1, D)


def place_rows(vectors, row_count):
    lead = vectors[0].shape[:-1]
    rows = lax.broadcasted_iota(jnp.int32, lead + (row_count, D), len(lead))
    block = jnp.zeros(rows.shape, jnp.bfloat16)
    for slot, vector in enumerate(vectors):
        padding = [(0, 0)] * len(lead) + [(0, D - vector.shape[-1])]
        wide = jnp.pad(vector.astype(jnp.bfloat16), padding)[..., None, :]
        block = jnp.where(rows == slot, wide, block)
    return block


def halve(buffer, axis, axis_name, flip, bit, kind=jnp.bfloat16):
    kept = lax.dynamic_index_in_dim(buffer, bit, axis, keepdims=False)
    sent = lax.dynamic_index_in_dim(buffer, 1 - bit, axis, keepdims=False)
    pairs = [(index, index ^ flip) for index in range(lax.axis_size(axis_name))]
    received = lax.ppermute(sent, axis_name, pairs)
    return (kept.astype(jnp.float32) + received.astype(jnp.float32)).astype(kind)


def frame_mask(length, shape):
    return lax.broadcasted_iota(jnp.int32, shape, 1) < length


def cross_forward_body(length_ref, query_ref, key_ref, value_ref, out_ref, log_ref):
    query_halves = split_pair(query_ref[...])
    value_halves = split_pair(value_ref[...])
    keys = key_ref[...]
    valid = frame_mask(length_ref[0], (query_ref.shape[0], keys.shape[0]))
    attended = jnp.zeros(query_ref.shape, jnp.float32)
    logs = []
    for half in range(2):
        scores = jnp.where(valid, dot_rows(query_halves[half], keys) * 0.125, neg_large)
        row_max = jnp.max(scores, axis=1, keepdims=True)
        exp_terms = jnp.exp(scores - row_max)
        total = jnp.sum(exp_terms, axis=1, keepdims=True)
        attended = attended + dot_plain(rounded(exp_terms), value_halves[half]) / total
        logs.append(row_max + jnp.log(total))
    out_ref[...] = rounded(attended)
    log_ref[...] = join_pair(logs[0], logs[1], log_ref.shape)


def cross_forward(lengths, queries, keys, values):
    query_spec = pl.BlockSpec((queries.shape[0], PAIR), lambda pair: (0, pair))
    frame_spec = pl.BlockSpec((keys.shape[0], PAIR), lambda pair: (0, pair))
    return pl.pallas_call(
        cross_forward_body,
        grid=(D // PAIR,),
        in_specs=[pl.BlockSpec(memory_space=pltpu.SMEM), query_spec, frame_spec, frame_spec],
        out_specs=[query_spec, query_spec],
        out_shape=[
            jax.ShapeDtypeStruct(queries.shape, jnp.bfloat16),
            jax.ShapeDtypeStruct(queries.shape, jnp.float32),
        ],
        name="cross_forward",
    )(lengths, queries, keys, values)


def cross_backward_body(
    length_ref, query_ref, key_ref, value_ref, log_ref, grad_ref, grad_query_ref, grad_frame_ref
):
    query_halves = split_pair(query_ref[...])
    grad_halves = split_pair(grad_ref[...])
    keys = key_ref[...]
    values = value_ref[...]
    key_halves = split_pair(keys)
    valid = frame_mask(length_ref[0], (query_ref.shape[0], keys.shape[0]))
    logs = (log_ref[:, :1], log_ref[:, HEAD : HEAD + 1])
    query_sum = jnp.zeros(query_ref.shape, jnp.float32)
    key_sum = jnp.zeros(keys.shape, jnp.float32)
    value_sum = jnp.zeros(keys.shape, jnp.float32)
    for half in range(2):
        scores = jnp.where(valid, dot_rows(query_halves[half], keys) * 0.125, neg_large)
        probs = jnp.exp(scores - logs[half])
        grad_probs = dot_rows(grad_halves[half], values)
        delta = jnp.sum(probs * grad_probs, axis=1, keepdims=True)
        grad_scores = rounded(probs * (grad_probs - delta) * 0.125)
        query_sum = query_sum + dot_plain(grad_scores, key_halves[half])
        key_sum = key_sum + dot_columns(grad_scores, query_halves[half])
        value_sum = value_sum + dot_columns(rounded(probs), grad_halves[half])
    grad_query_ref[...] = rounded(query_sum)
    grad_frame_ref[0] = rounded(key_sum)
    grad_frame_ref[1] = rounded(value_sum)


def cross_backward(lengths, queries, keys, values, log_total, grad_attended):
    query_spec = pl.BlockSpec((queries.shape[0], PAIR), lambda pair: (0, pair))
    frame_spec = pl.BlockSpec((keys.shape[0], PAIR), lambda pair: (0, pair))
    return pl.pallas_call(
        cross_backward_body,
        grid=(D // PAIR,),
        in_specs=[
            pl.BlockSpec(memory_space=pltpu.SMEM),
            query_spec,
            frame_spec,
            frame_spec,
            query_spec,
            query_spec,
        ],
        out_specs=[
            query_spec,
            pl.BlockSpec((2, keys.shape[0], PAIR), lambda pair: (0, 0, pair)),
        ],
        out_shape=[
            jax.ShapeDtypeStruct(queries.shape, jnp.bfloat16),
            jax.ShapeDtypeStruct((2,) + keys.shape, jnp.bfloat16),
        ],
        name="cross_backward",
    )(lengths, queries, keys, values, log_total, grad_attended)


def local_heads(
    tokens,
    memory,
    piece_starts,
    memory_lengths,
    self_gain,
    self_shift,
    query_weight,
    query_bias,
    key_weight,
    value_weight,
    value_bias,
    attn_out_weight,
    attn_out_bias,
    cross_gain,
    cross_shift,
    cross_query_weight,
    cross_query_bias,
    cross_key_weight,
    cross_value_weight,
    cross_value_bias,
    cross_out_weight,
    cross_out_bias,
    mlp_gain,
    mlp_shift,
    fc_in_weight,
    fc_in_bias,
    fc_out_weight,
    fc_out_bias,
    out_grad,
):
    local_len, batch_count, _ = tokens.shape
    seq_count = lax.axis_size("seq")
    seq_index = lax.axis_index("seq")
    full_length = local_len * seq_count
    token_count = local_len * batch_count
    query_pos = seq_index * local_len + jnp.arange(local_len, dtype=jnp.int32)
    labels = piece_labels(jnp.arange(full_length, dtype=jnp.int32), piece_starts).reshape(-1)
    input_rows = tokens.reshape(token_count, D).astype(jnp.float32)
    shard_rows = query_weight.shape[0]
    wide_parts = fc_in_weight.shape[1] // D
    vector_block = place_rows(
        (
            self_gain,
            self_shift,
            query_bias,
            value_bias,
            attn_out_bias,
            cross_gain,
            cross_shift,
            cross_query_bias,
            cross_value_bias,
            cross_out_bias,
            mlp_gain,
            mlp_shift,
            fc_out_bias,
            fc_in_bias,
        ),
        16,
    )
    fc_in_blocks = jnp.transpose(
        fc_in_weight.reshape(shard_rows, wide_parts, D), (1, 0, 2)
    ).reshape(wide_parts * shard_rows, D)
    first_packed = jnp.concatenate(
        (
            query_weight,
            key_weight,
            value_weight,
            cross_key_weight,
            cross_value_weight,
            vector_block,
        )
    )
    first = lax.all_gather(first_packed, ("dp", "seq"), axis=0, tiled=False)
    owners = first.shape[0]

    def owner_rows(matrix):
        return matrix.astype(jnp.bfloat16).reshape(owners, -1, D)

    def first_at(slot):
        return first[:, slot * shard_rows : (slot + 1) * shard_rows, :].reshape(D, D)

    full_query, full_key, full_value, full_cross_key, full_cross_value = (
        first_at(slot) for slot in range(5)
    )
    full_vectors = first[:, 5 * shard_rows :, :]
    packed = jnp.concatenate(
        (
            attn_out_weight,
            cross_query_weight,
            cross_out_weight,
            fc_in_blocks,
            fc_out_weight,
        )
    )
    packed, first = lax.optimization_barrier((packed, first))
    gathered = lax.all_gather(packed, ("dp", "seq"), axis=0, tiled=False)

    def square_at(slot):
        return gathered[:, slot * shard_rows : (slot + 1) * shard_rows, :].reshape(D, D)

    full_self_out, full_cross_query, full_cross_out = (square_at(slot) for slot in range(3))
    wide_start = 3 * shard_rows
    wide_stop = wide_start + wide_parts * shard_rows
    full_fc_in = jnp.transpose(
        gathered[:, wide_start:wide_stop, :].reshape(owners, wide_parts, shard_rows, D),
        (0, 2, 1, 3),
    ).reshape(D, wide_parts * D)
    out_stop = wide_stop + fc_out_weight.shape[0]
    full_fc_out = gathered[:, wide_stop:out_stop, :].reshape(wide_parts * D, D)

    def vector_at(slot):
        return full_vectors[:, slot, :shard_rows].reshape(D)

    (
        full_self_gain,
        full_self_shift,
        full_query_bias,
        full_value_bias,
        full_self_out_bias,
        full_cross_gain,
        full_cross_shift,
        full_cross_query_bias,
        full_cross_value_bias,
        full_cross_out_bias,
        full_mlp_gain,
        full_mlp_shift,
        full_fc_out_bias,
    ) = (vector_at(slot) for slot in range(13))
    full_fc_in_bias = full_vectors[:, 13, : fc_in_bias.shape[0]].reshape(-1)
    normed_self, scaled_self, inverse_self = norm_forward(
        input_rows, full_self_gain.astype(jnp.float32), full_self_shift.astype(jnp.float32)
    )
    normed_self_low = rounded(normed_self)
    query_rows = rounded(project(normed_self_low, full_query) + full_query_bias.astype(jnp.float32))
    key_rows = rounded(project(normed_self_low, full_key))
    value_rows = rounded(
        project(normed_self_low, full_value) + full_value_bias.astype(jnp.float32)
    )
    head_triple = lax.all_to_all(
        jnp.stack(
            tuple(to_pairs(rows, seq_count) for rows in (query_rows, key_rows, value_rows)), axis=1
        ),
        "seq",
        0,
        0,
    )
    head_attended, head_log, head_low = self_forward(head_triple, labels)
    attended_blocks = lax.all_to_all(head_low, "seq", 0, 0)
    attended_self_low = from_pairs(attended_blocks)
    middle_rows = (
        input_rows
        + project(attended_self_low, full_self_out)
        + full_self_out_bias.astype(jnp.float32)
    )
    normed_cross, scaled_cross, inverse_cross = norm_forward(
        middle_rows, full_cross_gain.astype(jnp.float32), full_cross_shift.astype(jnp.float32)
    )
    normed_cross_low = rounded(normed_cross)
    cross_queries = rounded(
        project(normed_cross_low, full_cross_query) + full_cross_query_bias.astype(jnp.float32)
    )
    frame_count = memory.shape[0]
    frame_part = frame_count // seq_count
    frame_start = seq_index * frame_part
    memory_flat = memory.reshape(frame_count, D)
    memory_part = lax.dynamic_slice_in_dim(memory_flat, frame_start, frame_part, 0)
    memory_keys = rounded(project(memory_flat, full_cross_key))
    memory_values = rounded(
        project(memory_flat, full_cross_value) + full_cross_value_bias.astype(jnp.float32)
    )
    attended_cross_low, cross_log = cross_forward(
        memory_lengths, cross_queries, memory_keys, memory_values
    )
    after_rows = (
        middle_rows
        + project(attended_cross_low, full_cross_out)
        + full_cross_out_bias.astype(jnp.float32)
    )
    normed_mlp, scaled_mlp, inverse_mlp = norm_forward(
        after_rows, full_mlp_gain.astype(jnp.float32), full_mlp_shift.astype(jnp.float32)
    )
    normed_mlp_low = rounded(normed_mlp)
    hidden_pre = project(normed_mlp_low, full_fc_in) + full_fc_in_bias.astype(jnp.float32)
    activated, gelu_pull = jax.vjp(exact_gelu, hidden_pre)
    activated_low = rounded(activated)
    result_rows = (
        after_rows + project(activated_low, full_fc_out) + full_fc_out_bias.astype(jnp.float32)
    )
    output = rounded(result_rows).reshape(local_len, batch_count, D)
    back_fc_in, back_fc_out = full_fc_in, full_fc_out
    grad_result = out_grad.reshape(token_count, D)
    grad_mlp_low = rounded(grad_result)
    grad_fc_out_weight = weight_grad(activated_low, grad_mlp_low)
    grad_fc_out_bias = row_sums(grad_mlp_low)
    grad_activated = project_back(grad_mlp_low, back_fc_out)
    grad_hidden_low = rounded(gelu_pull(grad_activated)[0])
    grad_fc_in_blocks = tuple(
        weight_grad(normed_mlp_low, grad_hidden_low[:, part * D : (part + 1) * D])
        for part in range(wide_parts)
    )
    grad_fc_in_bias = row_sums(grad_hidden_low)
    grad_normed_mlp = project_back(grad_hidden_low, back_fc_in)
    grad_rows_mlp, grad_mlp_gain, grad_mlp_shift = norm_backward(
        grad_normed_mlp, scaled_mlp, inverse_mlp, full_mlp_gain.astype(jnp.float32)
    )
    grad_after = grad_result + grad_rows_mlp
    back_cross_query, back_cross_key, back_cross_value, back_cross_out = (
        full_cross_query,
        full_cross_key,
        full_cross_value,
        full_cross_out,
    )
    grad_cross_low = rounded(grad_after)
    grad_cross_out_weight = weight_grad(attended_cross_low, grad_cross_low)
    grad_cross_out_bias = row_sums(grad_cross_low)
    grad_attended_cross = rounded(project_back(grad_cross_low, back_cross_out))
    grad_cross_queries, grad_memory_kv = cross_backward(
        memory_lengths,
        cross_queries,
        memory_keys,
        memory_values,
        cross_log,
        grad_attended_cross,
    )
    dp_index = lax.axis_index("dp")
    core_bit, x_bit = dp_index % 2, dp_index // 2
    y_bit, low_bit, high_bit = seq_index % 2, (seq_index // 2) % 2, seq_index // 4
    memory_parts = grad_memory_kv.reshape(2, 2, 2, 2, frame_part, D)
    part_keys = halve(halve(memory_parts[0], 2, "seq", 1, y_bit), 1, "seq", 2, low_bit)
    part_values = halve(halve(memory_parts[1], 1, "seq", 2, low_bit), 1, "seq", 1, y_bit)
    part_flat_keys = halve(part_keys, 0, "seq", 4, high_bit)
    part_flat_values = halve(part_values, 0, "seq", 4, high_bit)
    part_memory_grad = (
        project_back(part_flat_keys, back_cross_key)
        + project_back(part_flat_values, back_cross_value)
    )
    grad_cross_key_weight = weight_grad(memory_part, part_flat_keys)
    grad_cross_value_weight = weight_grad(memory_part, part_flat_values)
    grad_cross_value_bias = row_sums(part_flat_values)
    grad_cross_query_weight = weight_grad(normed_cross_low, grad_cross_queries)
    grad_cross_query_bias = row_sums(grad_cross_queries)
    grad_normed_cross = project_back(grad_cross_queries, back_cross_query)
    grad_rows_cross, grad_cross_gain, grad_cross_shift = norm_backward(
        grad_normed_cross, scaled_cross, inverse_cross, full_cross_gain.astype(jnp.float32)
    )
    grad_middle = grad_after + grad_rows_cross
    back_query, back_key, back_value, back_self_out = (
        full_query,
        full_key,
        full_value,
        full_self_out,
    )
    grad_self_low = rounded(grad_middle)
    grad_attn_out_weight = weight_grad(attended_self_low, grad_self_low)
    grad_attn_out_bias = row_sums(grad_self_low)
    early_grads = jnp.concatenate(
        (
            *(owner_rows(block) for block in grad_fc_in_blocks),
            owner_rows(grad_fc_out_weight),
            owner_rows(grad_attn_out_weight),
            owner_rows(grad_cross_query_weight),
            owner_rows(grad_cross_out_weight),
        ),
        axis=1,
    )
    owned_early = lax.psum_scatter(
        early_grads, ("dp", "seq"), scatter_dimension=0, tiled=False
    )
    owned_early = owned_early.astype(jnp.float32)
    wide_rows = wide_parts * shard_rows
    owned_fc_in = jnp.transpose(
        owned_early[:wide_rows].reshape(wide_parts, shard_rows, D), (1, 0, 2)
    ).reshape(shard_rows, wide_parts * D)
    out_rows = wide_rows + fc_out_weight.shape[0]
    owned_fc_out = owned_early[wide_rows:out_rows]
    owned_middle = owned_early[out_rows:]
    grad_attended_self = rounded(project_back(grad_self_low, back_self_out))
    head_blocks = to_pairs(grad_attended_self, seq_count)
    head_grad = lax.all_to_all(head_blocks, "seq", 0, 0)
    grad_blocks = self_backward(head_triple, labels, head_attended, head_log, head_grad)
    grad_triple = lax.all_to_all(grad_blocks, "seq", 0, 0)
    grad_query_low, grad_key_low, grad_value_low = (
        from_pairs(grad_triple[:, slot]) for slot in range(3)
    )
    grad_query_weight = weight_grad(normed_self_low, grad_query_low)
    grad_query_bias = row_sums(grad_query_low)
    grad_key_weight = weight_grad(normed_self_low, grad_key_low)
    grad_value_weight = weight_grad(normed_self_low, grad_value_low)
    grad_value_bias = row_sums(grad_value_low)
    grad_normed_self = (
        project_back(grad_query_low, back_query)
        + project_back(grad_key_low, back_key)
        + project_back(grad_value_low, back_value)
    )
    grad_rows_self, grad_self_gain, grad_self_shift = norm_backward(
        grad_normed_self, scaled_self, inverse_self, full_self_gain.astype(jnp.float32)
    )
    token_grad = (grad_middle + grad_rows_self).reshape(local_len, batch_count, D)
    late_block = pack_vectors(
        (
            grad_self_gain,
            grad_self_shift,
            grad_query_bias,
            grad_value_bias,
            grad_attn_out_bias,
            grad_cross_gain,
            grad_cross_shift,
            grad_cross_query_bias,
            grad_cross_value_bias,
            grad_cross_out_bias,
            grad_mlp_gain,
            grad_mlp_shift,
            grad_fc_out_bias,
        ),
        grad_fc_in_bias,
        owners,
    )
    late_grads = jnp.concatenate(
        (
            owner_rows(grad_query_weight),
            owner_rows(grad_key_weight),
            owner_rows(grad_value_weight),
            owner_rows(grad_cross_key_weight),
            owner_rows(grad_cross_value_weight),
            late_block,
        ),
        axis=1,
    )
    late_rows = late_grads.shape[1]
    by_core = halve(late_grads.reshape(2, 2, 2, 2, 2, late_rows, D), 1, "dp", 1, core_bit)
    cut_row = late_rows // 16 * 8
    upper = by_core[:, :, :, :, :cut_row]
    lower = by_core[:, :, :, :, cut_row:]
    upper = halve(halve(upper, 0, "dp", 2, x_bit), 2, "seq", 1, y_bit)
    lower = halve(halve(lower, 3, "seq", 1, y_bit), 0, "dp", 2, x_bit)
    by_column = jnp.concatenate((upper, lower), axis=2)
    owned_late = halve(
        halve(by_column, 1, "seq", 2, low_bit), 0, "seq", 4, high_bit, jnp.float32
    )
    memory_grad = lax.all_gather(part_memory_grad.astype(jnp.bfloat16), "seq", axis=0, tiled=True)
    memory_grad = widen_frames(memory_grad)
    owned_vectors = owned_late[5 * shard_rows :]

    def own_square(slot):
        return owned_late[slot * shard_rows : (slot + 1) * shard_rows]

    def own_middle(slot):
        return owned_middle[slot * shard_rows : (slot + 1) * shard_rows]

    def own_vector(slot):
        return owned_vectors[slot, :shard_rows]

    owned_fc_in_bias = owned_vectors[13, : fc_in_bias.shape[0]]
    return (
        output,
        token_grad,
        memory_grad,
        own_vector(0),
        own_vector(1),
        own_square(0),
        own_vector(2),
        own_square(1),
        own_square(2),
        own_vector(3),
        own_middle(0),
        own_vector(4),
        own_vector(5),
        own_vector(6),
        own_middle(1),
        own_vector(7),
        own_square(3),
        own_square(4),
        own_vector(8),
        own_middle(2),
        own_vector(9),
        own_vector(10),
        own_vector(11),
        owned_fc_in,
        owned_fc_in_bias,
        owned_fc_out,
        own_vector(12),
    )


def local(
    tokens,
    memory,
    piece_starts,
    memory_lengths,
    self_gain,
    self_shift,
    query_weight,
    query_bias,
    key_weight,
    value_weight,
    value_bias,
    attn_out_weight,
    attn_out_bias,
    cross_gain,
    cross_shift,
    cross_query_weight,
    cross_query_bias,
    cross_key_weight,
    cross_value_weight,
    cross_value_bias,
    cross_out_weight,
    cross_out_bias,
    mlp_gain,
    mlp_shift,
    fc_in_weight,
    fc_in_bias,
    fc_out_weight,
    fc_out_bias,
    out_grad,
):
    local_len, batch_count, _ = tokens.shape
    seq_count = lax.axis_size("seq")
    seq_index = lax.axis_index("seq")
    full_length = local_len * seq_count
    token_count = local_len * batch_count
    query_pos = seq_index * local_len + jnp.arange(local_len, dtype=jnp.int32)
    query_label = piece_labels(query_pos, piece_starts)
    input_rows = tokens.reshape(token_count, D).astype(jnp.float32)
    shard_rows = query_weight.shape[0]
    wide_parts = fc_in_weight.shape[1] // D
    vectors = jnp.concatenate(
        (
            self_gain,
            self_shift,
            query_bias,
            value_bias,
            attn_out_bias,
            cross_gain,
            cross_shift,
            cross_query_bias,
            cross_value_bias,
            cross_out_bias,
            mlp_gain,
            mlp_shift,
            fc_out_bias,
            fc_in_bias,
        )
    )
    vector_rows = 8
    vector_block = jnp.pad(vectors, (0, vector_rows * D - vectors.shape[0])).reshape(vector_rows, D)
    fc_in_blocks = jnp.transpose(
        fc_in_weight.reshape(shard_rows, wide_parts, D), (1, 0, 2)
    ).reshape(wide_parts * shard_rows, D)
    packed = jnp.concatenate(
        (
            query_weight,
            key_weight,
            value_weight,
            attn_out_weight,
            cross_query_weight,
            cross_key_weight,
            cross_value_weight,
            cross_out_weight,
            fc_in_blocks,
            fc_out_weight,
            vector_block,
        )
    )
    gathered = lax.all_gather(packed, ("dp", "seq"), axis=0, tiled=False)
    owners = gathered.shape[0]

    def square_at(slot):
        return gathered[:, slot * shard_rows : (slot + 1) * shard_rows, :].reshape(D, D)

    full_query, full_key, full_value, full_self_out = (square_at(slot) for slot in range(4))
    full_cross_query, full_cross_key, full_cross_value, full_cross_out = (
        square_at(slot) for slot in range(4, 8)
    )
    wide_start = 8 * shard_rows
    wide_stop = wide_start + wide_parts * shard_rows
    full_fc_in = jnp.transpose(
        gathered[:, wide_start:wide_stop, :].reshape(owners, wide_parts, shard_rows, D),
        (0, 2, 1, 3),
    ).reshape(D, wide_parts * D)
    out_stop = wide_stop + fc_out_weight.shape[0]
    full_fc_out = gathered[:, wide_stop:out_stop, :].reshape(wide_parts * D, D)
    full_vectors = gathered[:, out_stop:, :].reshape(owners, vector_rows * D)

    def vector_at(slot):
        return full_vectors[:, slot * shard_rows : (slot + 1) * shard_rows].reshape(D)

    (
        full_self_gain,
        full_self_shift,
        full_query_bias,
        full_value_bias,
        full_self_out_bias,
        full_cross_gain,
        full_cross_shift,
        full_cross_query_bias,
        full_cross_value_bias,
        full_cross_out_bias,
        full_mlp_gain,
        full_mlp_shift,
        full_fc_out_bias,
    ) = (vector_at(slot) for slot in range(13))
    full_fc_in_bias = full_vectors[
        :, 13 * shard_rows : 13 * shard_rows + fc_in_bias.shape[0]
    ].reshape(-1)
    normed_self, scaled_self, inverse_self = norm_forward(
        input_rows, full_self_gain.astype(jnp.float32), full_self_shift.astype(jnp.float32)
    )
    normed_self_low = rounded(normed_self)
    query_rows = rounded(project(normed_self_low, full_query) + full_query_bias.astype(jnp.float32))
    key_rows = rounded(project(normed_self_low, full_key)).reshape(local_len, batch_count, D)
    value_rows = rounded(
        project(normed_self_low, full_value) + full_value_bias.astype(jnp.float32)
    ).reshape(local_len, batch_count, D)
    query_heads = query_rows.reshape(local_len, batch_count, HEADS, HEAD)

    def key_block_scores(key_block, key_pos):
        key_heads = key_block.reshape(key_block.shape[0], batch_count, HEADS, HEAD)
        raw_scores = jnp.einsum(
            "qbhd,kbhd->qbhk", query_heads, key_heads, preferred_element_type=jnp.float32
        )
        allowed = visible(query_pos, query_label, key_pos, piece_labels(key_pos, piece_starts))
        return (raw_scores * 0.125, allowed)

    start_state = (
        jnp.full((local_len, batch_count, HEADS), neg_large, jnp.float32),
        jnp.zeros((local_len, batch_count, HEADS), jnp.float32),
        jnp.zeros((local_len, batch_count, HEADS, HEAD), jnp.float32),
    )
    running = start_state
    kv_piece = lax.all_gather(
        jnp.concatenate((key_rows, value_rows), axis=2), "seq", axis=0, tiled=True
    )
    key_piece = kv_piece[:, :, :D]
    value_piece = kv_piece[:, :, D:]
    block_rows = math.gcd(key_piece.shape[0], 512)

    def fold_block(inner_state, block_index):
        row_max, row_total, weighted_sum = inner_state
        block_start = block_index * block_rows
        key_block = lax.dynamic_slice_in_dim(key_piece, block_start, block_rows, 0)
        value_block = lax.dynamic_slice_in_dim(value_piece, block_start, block_rows, 0).reshape(
            block_rows, batch_count, HEADS, HEAD
        )
        key_pos = block_start + jnp.arange(block_rows, dtype=jnp.int32)
        scores, allowed = key_block_scores(key_block, key_pos)
        new_max = jnp.maximum(row_max, jnp.max(jnp.where(allowed, scores, neg_large), axis=-1))
        exp_terms = jnp.where(allowed, jnp.exp(scores - new_max[..., None]), 0.0)
        factor = jnp.exp(row_max - new_max)
        row_total = row_total * factor + jnp.sum(exp_terms, axis=-1)
        weighted_sum = weighted_sum * factor[..., None] + jnp.einsum(
            "qbhk,kbhd->qbhd", rounded(exp_terms), value_block, preferred_element_type=jnp.float32
        )
        return ((new_max, row_total, weighted_sum), None)

    running, unused = lax.scan(
        fold_block, running, jnp.arange(key_piece.shape[0] // block_rows, dtype=jnp.int32)
    )
    row_max, row_total, weighted_sum = running
    attended_self = weighted_sum / row_total[..., None]
    log_total = row_max + jnp.log(row_total)
    attended_self_low = rounded(attended_self.reshape(token_count, D))
    middle_rows = (
        input_rows
        + project(attended_self_low, full_self_out)
        + full_self_out_bias.astype(jnp.float32)
    )
    normed_cross, scaled_cross, inverse_cross = norm_forward(
        middle_rows, full_cross_gain.astype(jnp.float32), full_cross_shift.astype(jnp.float32)
    )
    normed_cross_low = rounded(normed_cross)
    cross_queries = rounded(
        project(normed_cross_low, full_cross_query) + full_cross_query_bias.astype(jnp.float32)
    ).reshape(local_len, batch_count, HEADS, HEAD)
    frame_count = memory.shape[0]
    frame_part = frame_count // seq_count
    frame_start = seq_index * frame_part
    memory_part = lax.dynamic_slice_in_dim(memory, frame_start, frame_part, 0).reshape(
        frame_part * batch_count, D
    )
    memory_flat = memory.reshape(frame_count * batch_count, D)
    memory_keys = rounded(project(memory_flat, full_cross_key)).reshape(frame_count, batch_count, D)
    memory_values = rounded(
        project(memory_flat, full_cross_value) + full_cross_value_bias.astype(jnp.float32)
    ).reshape(frame_count, batch_count, D)
    memory_key_heads = memory_keys.reshape(frame_count, batch_count, HEADS, HEAD)
    memory_value_heads = memory_values.reshape(frame_count, batch_count, HEADS, HEAD)
    frame_valid = (jnp.arange(frame_count, dtype=jnp.int32)[None, :] < memory_lengths[:, None])[
        None, :, None, :
    ]
    cross_scores = (
        jnp.einsum(
            "qbhd,kbhd->qbhk", cross_queries, memory_key_heads, preferred_element_type=jnp.float32
        )
        * 0.125
    )
    cross_max = jnp.max(jnp.where(frame_valid, cross_scores, neg_large), axis=-1, keepdims=True)
    cross_exp = jnp.where(frame_valid, jnp.exp(cross_scores - cross_max), 0.0)
    cross_probs = cross_exp / jnp.sum(cross_exp, axis=-1, keepdims=True)
    cross_probs_low = rounded(cross_probs)
    attended_cross = jnp.einsum(
        "qbhk,kbhd->qbhd", cross_probs_low, memory_value_heads, preferred_element_type=jnp.float32
    )
    attended_cross_low = rounded(attended_cross.reshape(token_count, D))
    after_rows = (
        middle_rows
        + project(attended_cross_low, full_cross_out)
        + full_cross_out_bias.astype(jnp.float32)
    )
    normed_mlp, scaled_mlp, inverse_mlp = norm_forward(
        after_rows, full_mlp_gain.astype(jnp.float32), full_mlp_shift.astype(jnp.float32)
    )
    normed_mlp_low = rounded(normed_mlp)
    hidden_pre = project(normed_mlp_low, full_fc_in) + full_fc_in_bias.astype(jnp.float32)
    activated, gelu_pull = jax.vjp(exact_gelu, hidden_pre)
    activated_low = rounded(activated)
    result_rows = (
        after_rows + project(activated_low, full_fc_out) + full_fc_out_bias.astype(jnp.float32)
    )
    output = rounded(result_rows).reshape(local_len, batch_count, D)
    back_fc_in, back_fc_out = full_fc_in, full_fc_out
    grad_result = out_grad.reshape(token_count, D)
    grad_mlp_low = rounded(grad_result)
    grad_fc_out_weight = weight_grad(activated_low, grad_mlp_low)
    grad_fc_out_bias = column_sums(grad_mlp_low)
    grad_activated = project_back(grad_mlp_low, back_fc_out)
    grad_hidden_low = rounded(gelu_pull(grad_activated)[0])
    grad_fc_in_weight = weight_grad(normed_mlp_low, grad_hidden_low)
    grad_fc_in_bias = column_sums(grad_hidden_low)
    grad_normed_mlp = project_back(grad_hidden_low, back_fc_in)
    grad_rows_mlp, grad_mlp_gain, grad_mlp_shift = norm_backward(
        grad_normed_mlp, scaled_mlp, inverse_mlp, full_mlp_gain.astype(jnp.float32)
    )
    early_grads = jnp.concatenate(
        (
            jnp.transpose(
                grad_fc_in_weight.astype(jnp.bfloat16).reshape(
                    owners, shard_rows, wide_parts, D
                ),
                (0, 2, 1, 3),
            ).reshape(owners, wide_parts * shard_rows, D),
            grad_fc_out_weight.astype(jnp.bfloat16).reshape(owners, -1, D),
        ),
        axis=1,
    )
    owned_early = lax.psum_scatter(
        early_grads, ("dp", "seq"), scatter_dimension=0, tiled=False
    ).astype(jnp.float32)
    wide_rows = wide_parts * shard_rows
    owned_fc_in = jnp.transpose(
        owned_early[:wide_rows].reshape(wide_parts, shard_rows, D), (1, 0, 2)
    ).reshape(shard_rows, wide_parts * D)
    owned_fc_out = owned_early[wide_rows:]
    grad_after = grad_result + grad_rows_mlp
    back_cross_query, back_cross_key, back_cross_value, back_cross_out = (
        full_cross_query,
        full_cross_key,
        full_cross_value,
        full_cross_out,
    )
    grad_cross_low = rounded(grad_after)
    grad_cross_out_weight = weight_grad(attended_cross_low, grad_cross_low)
    grad_cross_out_bias = column_sums(grad_cross_low)
    grad_attended_cross = rounded(project_back(grad_cross_low, back_cross_out)).reshape(
        local_len, batch_count, HEADS, HEAD
    )
    grad_cross_probs = jnp.einsum(
        "qbhd,kbhd->qbhk",
        grad_attended_cross,
        memory_value_heads,
        preferred_element_type=jnp.float32,
    )
    cross_delta = jnp.sum(cross_probs * grad_cross_probs, axis=-1, keepdims=True)
    grad_cross_scores = rounded(cross_probs * (grad_cross_probs - cross_delta) * 0.125)
    grad_cross_queries = rounded(
        jnp.einsum(
            "qbhk,kbhd->qbhd",
            grad_cross_scores,
            memory_key_heads,
            preferred_element_type=jnp.float32,
        ).reshape(token_count, D)
    )
    grad_memory_keys = jnp.einsum(
        "qbhk,qbhd->kbhd", grad_cross_scores, cross_queries, preferred_element_type=jnp.float32
    ).reshape(frame_count, batch_count, D)
    grad_memory_values = jnp.einsum(
        "qbhk,qbhd->kbhd", cross_probs_low, grad_attended_cross, preferred_element_type=jnp.float32
    ).reshape(frame_count, batch_count, D)
    grad_memory_kv = jnp.concatenate((grad_memory_keys, grad_memory_values), axis=2)
    grad_cross_query_weight = weight_grad(normed_cross_low, grad_cross_queries)
    grad_cross_query_bias = column_sums(grad_cross_queries)
    grad_normed_cross = project_back(grad_cross_queries, back_cross_query)
    grad_rows_cross, grad_cross_gain, grad_cross_shift = norm_backward(
        grad_normed_cross, scaled_cross, inverse_cross, full_cross_gain.astype(jnp.float32)
    )
    grad_middle = grad_after + grad_rows_cross
    back_query, back_key, back_value, back_self_out = (
        full_query,
        full_key,
        full_value,
        full_self_out,
    )
    grad_self_low = rounded(grad_middle)
    grad_attn_out_weight = weight_grad(attended_self_low, grad_self_low)
    grad_attn_out_bias = column_sums(grad_self_low)
    grad_attended_self = rounded(project_back(grad_self_low, back_self_out)).reshape(
        local_len, batch_count, HEADS, HEAD
    )
    self_delta = jnp.sum(grad_attended_self.astype(jnp.float32) * attended_self, axis=-1)

    def score_grads(key_block, value_block, key_pos):
        scores, allowed = key_block_scores(key_block, key_pos)
        attn_probs = jnp.where(allowed, jnp.exp(scores - log_total[..., None]), 0.0)
        grad_probs = jnp.einsum(
            "qbhd,kbhd->qbhk", grad_attended_self, value_block, preferred_element_type=jnp.float32
        )
        grad_scores = rounded(attn_probs * (grad_probs - self_delta[..., None]) * 0.125)
        return (grad_scores, attn_probs)

    zero_query_grad = jnp.zeros((local_len, batch_count, HEADS, HEAD), jnp.float32)
    back_state = (zero_query_grad, jnp.zeros((full_length, batch_count, 2 * D), jnp.float32))
    running = back_state
    self_key_piece = key_piece
    self_value_piece = value_piece
    self_block_rows = math.gcd(self_key_piece.shape[0], 512)

    def back_block(inner_state, block_index):
        grad_query_sum, kv_grads = inner_state
        block_start = block_index * self_block_rows
        key_block = lax.dynamic_slice_in_dim(self_key_piece, block_start, self_block_rows, 0)
        value_block = lax.dynamic_slice_in_dim(
            self_value_piece, block_start, self_block_rows, 0
        ).reshape(self_block_rows, batch_count, HEADS, HEAD)
        key_pos = block_start + jnp.arange(self_block_rows, dtype=jnp.int32)
        grad_scores, attn_probs = score_grads(key_block, value_block, key_pos)
        key_heads = key_block.reshape(self_block_rows, batch_count, HEADS, HEAD)
        grad_query_sum = grad_query_sum + jnp.einsum(
            "qbhk,kbhd->qbhd", grad_scores, key_heads, preferred_element_type=jnp.float32
        )
        grad_key_block = jnp.einsum(
            "qbhk,qbhd->kbhd", grad_scores, query_heads, preferred_element_type=jnp.float32
        ).reshape(self_block_rows, batch_count, D)
        grad_value_block = jnp.einsum(
            "qbhk,qbhd->kbhd",
            rounded(attn_probs),
            grad_attended_self,
            preferred_element_type=jnp.float32,
        ).reshape(self_block_rows, batch_count, D)
        kv_grads = lax.dynamic_update_slice_in_dim(
            kv_grads, jnp.concatenate((grad_key_block, grad_value_block), axis=2), block_start, 0
        )
        return ((grad_query_sum, kv_grads), None)

    running, unused = lax.scan(
        back_block, running, jnp.arange(self_key_piece.shape[0] // self_block_rows, dtype=jnp.int32)
    )
    grad_query_sum = running[0]
    joint_kv = jnp.concatenate(
        (
            running[1].astype(jnp.bfloat16).reshape(seq_count, local_len, batch_count, 2 * D),
            grad_memory_kv.astype(jnp.bfloat16).reshape(
                seq_count, frame_part, batch_count, 2 * D
            ),
        ),
        axis=1,
    )
    own_joint = lax.psum_scatter(joint_kv, "seq", scatter_dimension=0, tiled=False)
    own_kv = own_joint[:local_len]
    part_kv = own_joint[local_len:]
    grad_key_low = own_kv[:, :, :D].reshape(token_count, D)
    grad_value_low = own_kv[:, :, D:].reshape(token_count, D)
    part_flat_keys = part_kv[:, :, :D].reshape(frame_part * batch_count, D)
    part_flat_values = part_kv[:, :, D:].reshape(frame_part * batch_count, D)
    part_memory_grad = (
        project_back(part_flat_keys, back_cross_key)
        + project_back(part_flat_values, back_cross_value)
    ).reshape(frame_part, batch_count, D)
    grad_cross_key_weight = weight_grad(memory_part, part_flat_keys)
    grad_cross_value_weight = weight_grad(memory_part, part_flat_values)
    grad_cross_value_bias = column_sums(part_flat_values)
    grad_query_low = rounded(grad_query_sum.reshape(token_count, D))
    grad_query_weight = weight_grad(normed_self_low, grad_query_low)
    grad_query_bias = column_sums(grad_query_low)
    grad_key_weight = weight_grad(normed_self_low, grad_key_low)
    grad_value_weight = weight_grad(normed_self_low, grad_value_low)
    grad_value_bias = column_sums(grad_value_low)
    grad_normed_self = (
        project_back(grad_query_low, back_query)
        + project_back(grad_key_low, back_key)
        + project_back(grad_value_low, back_value)
    )
    grad_rows_self, grad_self_gain, grad_self_shift = norm_backward(
        grad_normed_self, scaled_self, inverse_self, full_self_gain.astype(jnp.float32)
    )
    token_grad = (grad_middle + grad_rows_self).reshape(local_len, batch_count, D)

    def owner_rows(matrix):
        return matrix.astype(jnp.bfloat16).reshape(owners, -1, D)

    late_vectors = jnp.concatenate(
        tuple(
            vector.reshape(owners, -1)
            for vector in (
                grad_self_gain,
                grad_self_shift,
                grad_query_bias,
                grad_value_bias,
                grad_attn_out_bias,
                grad_cross_gain,
                grad_cross_shift,
                grad_cross_query_bias,
                grad_cross_value_bias,
                grad_cross_out_bias,
                grad_mlp_gain,
                grad_mlp_shift,
                grad_fc_out_bias,
                grad_fc_in_bias,
            )
        ),
        axis=1,
    )
    late_block = jnp.pad(
        late_vectors.astype(jnp.bfloat16),
        ((0, 0), (0, vector_rows * D - late_vectors.shape[1])),
    ).reshape(owners, vector_rows, D)
    late_grads = jnp.concatenate(
        (
            owner_rows(grad_query_weight),
            owner_rows(grad_key_weight),
            owner_rows(grad_value_weight),
            owner_rows(grad_attn_out_weight),
            owner_rows(grad_cross_query_weight),
            owner_rows(grad_cross_key_weight),
            owner_rows(grad_cross_value_weight),
            owner_rows(grad_cross_out_weight),
            late_block,
        ),
        axis=1,
    )
    owned_late = lax.psum_scatter(
        late_grads, ("dp", "seq"), scatter_dimension=0, tiled=False
    ).astype(jnp.float32)
    memory_grad = lax.all_gather(
        part_memory_grad.astype(jnp.bfloat16), "seq", axis=0, tiled=True
    ).astype(jnp.float32)
    owned_vectors = owned_late[8 * shard_rows :].reshape(-1)

    def own_square(slot):
        return owned_late[slot * shard_rows : (slot + 1) * shard_rows]

    def own_vector(slot):
        return owned_vectors[slot * shard_rows : (slot + 1) * shard_rows]

    owned_fc_in_bias = owned_vectors[13 * shard_rows : 13 * shard_rows + fc_in_bias.shape[0]]
    return (
        output,
        token_grad,
        memory_grad,
        own_vector(0),
        own_vector(1),
        own_square(0),
        own_vector(2),
        own_square(1),
        own_square(2),
        own_vector(3),
        own_square(3),
        own_vector(4),
        own_vector(5),
        own_vector(6),
        own_square(4),
        own_vector(7),
        own_square(5),
        own_square(6),
        own_vector(8),
        own_square(7),
        own_vector(9),
        own_vector(10),
        own_vector(11),
        owned_fc_in,
        owned_fc_in_bias,
        owned_fc_out,
        own_vector(12),
    )


def solution(mesh):
    in_specs = (
        P("seq", "dp", None),
        P(None, "dp", None),
        P("dp", None),
        P("dp"),
        P(("dp", "seq")),
        P(("dp", "seq")),
        P(("dp", "seq"), None),
        P(("dp", "seq")),
        P(("dp", "seq"), None),
        P(("dp", "seq"), None),
        P(("dp", "seq")),
        P(("dp", "seq"), None),
        P(("dp", "seq")),
        P(("dp", "seq")),
        P(("dp", "seq")),
        P(("dp", "seq"), None),
        P(("dp", "seq")),
        P(("dp", "seq"), None),
        P(("dp", "seq"), None),
        P(("dp", "seq")),
        P(("dp", "seq"), None),
        P(("dp", "seq")),
        P(("dp", "seq")),
        P(("dp", "seq")),
        P(("dp", "seq"), None),
        P(("dp", "seq")),
        P(("dp", "seq"), None),
        P(("dp", "seq")),
        P("seq", "dp", None),
    )
    out_specs = (
        P("seq", "dp", None),
        P("seq", "dp", None),
        P(None, "dp", None),
        P(("dp", "seq")),
        P(("dp", "seq")),
        P(("dp", "seq"), None),
        P(("dp", "seq")),
        P(("dp", "seq"), None),
        P(("dp", "seq"), None),
        P(("dp", "seq")),
        P(("dp", "seq"), None),
        P(("dp", "seq")),
        P(("dp", "seq")),
        P(("dp", "seq")),
        P(("dp", "seq"), None),
        P(("dp", "seq")),
        P(("dp", "seq"), None),
        P(("dp", "seq"), None),
        P(("dp", "seq")),
        P(("dp", "seq"), None),
        P(("dp", "seq")),
        P(("dp", "seq")),
        P(("dp", "seq")),
        P(("dp", "seq"), None),
        P(("dp", "seq")),
        P(("dp", "seq"), None),
        P(("dp", "seq")),
    )
    by_heads = mesh.shape["dp"] == 4 and mesh.shape["seq"] == 8

    def layer(*arrays):
        return local_heads(*arrays)

    return jax.shard_map(
        layer if by_heads else local,
        mesh=mesh,
        in_specs=in_specs,
        out_specs=out_specs,
        check_vma=False,
    )
```

```python
import math

import jax
import jax.numpy as jnp
from jax import lax
from jax.experimental import pallas as pl
from jax.experimental.pallas import tpu as pltpu
from jax.sharding import PartitionSpec as P


D = 768
HEADS = 12
HEAD = 64
PIECE = 256


norm_epsilon = 1e-05
neg_large = -1e30


def rounded(tensor):
    return tensor.astype(jnp.bfloat16)


def project(left_rows, matrix):
    return jnp.dot(left_rows, matrix, preferred_element_type=jnp.float32)


def project_back(left_rows, matrix):
    return lax.dot_general(
        left_rows, matrix, (((1,), (1,)), ((), ())), preferred_element_type=jnp.float32
    )


def weight_grad(inputs, grad_rows):
    return lax.dot_general(
        inputs, grad_rows, (((0,), (0,)), ((), ())), preferred_element_type=jnp.float32
    )


def column_sums(grad_rows):
    return jnp.sum(grad_rows.astype(jnp.float32), axis=0)


def row_sums(grad_rows):
    return jnp.sum(grad_rows.astype(jnp.float32), axis=0, keepdims=True)


def exact_gelu(inputs):
    return jax.nn.gelu(inputs, approximate=False)


def norm_forward(token_rows, norm_gain, norm_shift):
    centre = token_rows - jnp.mean(token_rows, axis=-1, keepdims=True)
    inverse = lax.rsqrt(jnp.mean(centre * centre, axis=-1, keepdims=True) + norm_epsilon)
    scaled = centre * inverse
    return (scaled * norm_gain + norm_shift, scaled, inverse)


def norm_backward(grad_normed, scaled, inverse, norm_gain):
    grad_scaled = grad_normed * norm_gain
    mean_grad = jnp.mean(grad_scaled, axis=-1, keepdims=True)
    mean_cross = jnp.mean(grad_scaled * scaled, axis=-1, keepdims=True)
    grad_input = inverse * (grad_scaled - mean_grad - scaled * mean_cross)
    return (grad_input, jnp.sum(grad_normed * scaled, axis=0), jnp.sum(grad_normed, axis=0))


def piece_labels(positions, starts):
    inside = (positions[None, :, None] >= starts[:, None, :]) & (
        positions[None, :, None] < starts[:, None, :] + PIECE
    )
    numbers = jnp.arange(1, starts.shape[1] + 1, dtype=jnp.int32)
    return jnp.sum(jnp.where(inside, numbers, 0), axis=2)


def visible(query_pos, query_label, key_pos, key_label):
    causal = (key_pos[None, :] <= query_pos[:, None])[:, None, :]
    query_side = jnp.transpose(query_label)[:, :, None]
    same_piece = (query_side == key_label[None, :, :]) & (query_side > 0)
    return (causal | same_piece)[:, :, None, :]


PAIR = 2 * HEAD
QUERY_BLOCK = 256
KEY_BLOCK = 512


def to_pairs(rows, seq_count):
    blocks = jnp.transpose(rows.reshape(rows.shape[0], D // PAIR, PAIR), (1, 0, 2))
    return jnp.pad(blocks, ((0, seq_count - D // PAIR), (0, 0), (0, 0)))


def from_pairs(blocks):
    kept = blocks[: D // PAIR]
    return jnp.transpose(kept, (1, 0, 2)).reshape(kept.shape[1], D)


def dot_rows(left, right):
    return lax.dot_general(left, right, (((1,), (1,)), ((), ())), preferred_element_type=jnp.float32)


def dot_plain(left, right):
    return lax.dot_general(left, right, (((1,), (0,)), ((), ())), preferred_element_type=jnp.float32)


def dot_columns(left, right):
    return lax.dot_general(left, right, (((0,), (0,)), ((), ())), preferred_element_type=jnp.float32)


def split_pair(block):
    lanes = lax.broadcasted_iota(jnp.int32, block.shape, 1)
    zero = jnp.zeros_like(block)
    return (jnp.where(lanes < HEAD, block, zero), jnp.where(lanes < HEAD, zero, block))


def join_pair(first, second, shape):
    lanes = lax.broadcasted_iota(jnp.int32, shape, 1)
    return jnp.where(lanes < HEAD, first, second)


def stack_pair(block):
    return jnp.concatenate(split_pair(block), axis=0)


def join_stack(stacked):
    rows = stacked.shape[0] // 2
    return join_pair(stacked[:rows], stacked[rows:], (rows, stacked.shape[1]))


def block_allowed(query_pos, key_pos, query_label, key_label):
    same_piece = (query_label == key_label) & (query_label > 0)
    return (key_pos <= query_pos) | same_piece


def key_rows_at(ref, key_block):
    parts = KEY_BLOCK // QUERY_BLOCK
    return ref[pl.ds(key_block * parts, parts), 0].reshape(KEY_BLOCK, PAIR)


def exchange_specs(owners):
    return [
        pl.BlockSpec((1, 1, QUERY_BLOCK, PAIR), lambda index: (index, 0, 0, 0)),
        pl.BlockSpec((owners, 1, QUERY_BLOCK, PAIR), lambda index: (0, 1, 0, 0)),
        pl.BlockSpec((owners, 1, QUERY_BLOCK, PAIR), lambda index: (0, 2, 0, 0)),
    ]


def key_block_range(block, key_rows):
    full = block * QUERY_BLOCK // KEY_BLOCK
    last = ((block + 2) * QUERY_BLOCK + KEY_BLOCK - 1) // KEY_BLOCK
    return (full, jnp.minimum(last, key_rows // KEY_BLOCK))


def self_forward_body(
    query_ref, key_ref, value_ref, column_ref, row_ref, out_ref, log_ref, low_ref
):
    block = pl.program_id(0)
    queries = stack_pair(query_ref[0, 0] * jnp.bfloat16(0.125))
    query_label = column_ref[...]

    def step(key_block, state, masked):
        start = pl.multiple_of(key_block * KEY_BLOCK, KEY_BLOCK)
        here = pl.ds(start, KEY_BLOCK)
        row_max, row_total, weighted = state
        scores = dot_rows(queries, key_rows_at(key_ref, key_block))
        if masked:
            shape = (QUERY_BLOCK, KEY_BLOCK)
            allowed = block_allowed(
                block * QUERY_BLOCK + lax.broadcasted_iota(jnp.int32, shape, 0),
                start + lax.broadcasted_iota(jnp.int32, shape, 1),
                query_label,
                row_ref[:, here],
            )
            scores = jnp.concatenate(
                (
                    jnp.where(allowed, scores[:QUERY_BLOCK], neg_large),
                    jnp.where(allowed, scores[QUERY_BLOCK:], neg_large),
                ),
                axis=0,
            )
        new_max = jnp.maximum(row_max, jnp.max(scores, axis=1, keepdims=True))
        exp_terms = jnp.exp(scores - new_max)
        factor = jnp.exp(row_max - new_max)
        row_total = row_total * factor + jnp.sum(exp_terms, axis=1, keepdims=True)
        weighted = weighted * factor + dot_plain(
            rounded(exp_terms), key_rows_at(value_ref, key_block)
        )
        return (new_max, row_total, weighted)

    state = (
        jnp.full((2 * QUERY_BLOCK, 1), neg_large, jnp.float32),
        jnp.zeros((2 * QUERY_BLOCK, 1), jnp.float32),
        jnp.zeros((2 * QUERY_BLOCK, PAIR), jnp.float32),
    )
    full, last = key_block_range(block, key_ref.shape[0] * QUERY_BLOCK)
    state = lax.fori_loop(0, full, lambda index, state: step(index, state, False), state)
    state = lax.fori_loop(full, last, lambda index, state: step(index, state, True), state)
    row_max, row_total, weighted = state
    attended = join_stack(weighted / row_total)
    out_ref[...] = attended
    low_ref[0] = rounded(attended)
    log_ref[...] = join_stack(jnp.broadcast_to(row_max + jnp.log(row_total), weighted.shape))


def self_forward(triple, labels):
    owners = triple.shape[0]
    length = owners * QUERY_BLOCK
    block_spec = pl.BlockSpec((QUERY_BLOCK, PAIR), lambda index: (index, 0))
    result = jax.ShapeDtypeStruct((length, PAIR), jnp.float32)
    return pl.pallas_call(
        self_forward_body,
        grid=(owners,),
        in_specs=exchange_specs(owners)
        + [
            pl.BlockSpec((QUERY_BLOCK, 1), lambda index: (index, 0)),
            pl.BlockSpec((1, length), lambda index: (0, 0)),
        ],
        out_specs=[
            block_spec,
            block_spec,
            pl.BlockSpec((1, QUERY_BLOCK, PAIR), lambda index: (index, 0, 0)),
        ],
        out_shape=[
            result,
            result,
            jax.ShapeDtypeStruct((owners, QUERY_BLOCK, PAIR), jnp.bfloat16),
        ],
        name="self_forward",
    )(triple, triple, triple, labels[:, None], labels[None, :])


def self_backward_body(
    query_ref,
    key_ref,
    value_ref,
    column_ref,
    row_ref,
    out_ref,
    log_ref,
    grad_ref,
    triple_ref,
    key_sum,
    value_sum,
):
    block = pl.program_id(0)
    block_count = pl.num_programs(0)

    @pl.when(block == 0)
    def clear():
        key_sum[...] = jnp.zeros_like(key_sum)
        value_sum[...] = jnp.zeros_like(value_sum)

    queries = stack_pair(query_ref[0, 0] * jnp.bfloat16(0.125))
    query_label = row_ref[...]
    grad_rows = grad_ref[0]
    grads = stack_pair(grad_rows)
    products = stack_pair(grad_rows.astype(jnp.float32) * out_ref[...])
    delta = jnp.sum(jnp.transpose(products), axis=0, keepdims=True)
    log_columns = jnp.transpose(log_ref[...])
    logs = jnp.concatenate((log_columns[:1], log_columns[HEAD : HEAD + 1]), axis=1)

    def step(key_block, query_sum, masked):
        start = pl.multiple_of(key_block * KEY_BLOCK, KEY_BLOCK)
        here = pl.ds(start, KEY_BLOCK)
        keys = key_rows_at(key_ref, key_block)
        scores = dot_rows(keys, queries)
        if masked:
            shape = (KEY_BLOCK, QUERY_BLOCK)
            allowed = block_allowed(
                block * QUERY_BLOCK + lax.broadcasted_iota(jnp.int32, shape, 1),
                start + lax.broadcasted_iota(jnp.int32, shape, 0),
                query_label,
                column_ref[here, :],
            )
            scores = jnp.concatenate(
                (
                    jnp.where(allowed, scores[:, :QUERY_BLOCK], neg_large),
                    jnp.where(allowed, scores[:, QUERY_BLOCK:], neg_large),
                ),
                axis=1,
            )
        probs = jnp.exp(scores - logs)
        grad_probs = dot_rows(key_rows_at(value_ref, key_block), grads)
        grad_scores = rounded(probs * (grad_probs - delta))
        key_sum[here, :] = key_sum[here, :] + dot_plain(grad_scores, queries)
        value_sum[here, :] = value_sum[here, :] + dot_plain(rounded(probs), grads)
        return query_sum + dot_columns(grad_scores, keys)

    query_sum = jnp.zeros((2 * QUERY_BLOCK, PAIR), jnp.float32)
    full, last = key_block_range(block, key_ref.shape[0] * QUERY_BLOCK)
    query_sum = lax.fori_loop(0, full, lambda index, total: step(index, total, False), query_sum)
    query_sum = lax.fori_loop(full, last, lambda index, total: step(index, total, True), query_sum)
    triple_ref[block, 0] = rounded(join_stack(query_sum) * 0.125)

    @pl.when(block == block_count - 1)
    def finish():
        for owner in range(triple_ref.shape[0]):
            rows = slice(owner * QUERY_BLOCK, (owner + 1) * QUERY_BLOCK)
            triple_ref[owner, 1] = rounded(key_sum[rows, :])
            triple_ref[owner, 2] = rounded(value_sum[rows, :])


def self_backward(triple, labels, attended, log_total, grad_attended):
    owners = triple.shape[0]
    length = owners * QUERY_BLOCK
    block_spec = pl.BlockSpec((QUERY_BLOCK, PAIR), lambda index: (index, 0))
    return pl.pallas_call(
        self_backward_body,
        grid=(owners,),
        in_specs=exchange_specs(owners)
        + [
            pl.BlockSpec((length, 1), lambda index: (0, 0)),
            pl.BlockSpec((1, QUERY_BLOCK), lambda index: (0, index)),
            block_spec,
            block_spec,
            pl.BlockSpec((1, QUERY_BLOCK, PAIR), lambda index: (index, 0, 0)),
        ],
        out_specs=pl.BlockSpec(triple.shape, lambda index: (0, 0, 0, 0)),
        out_shape=jax.ShapeDtypeStruct(triple.shape, jnp.bfloat16),
        scratch_shapes=[
            pltpu.VMEM((length, PAIR), jnp.float32),
            pltpu.VMEM((length, PAIR), jnp.float32),
        ],
        name="self_backward",
    )(
        triple,
        triple,
        triple,
        labels[:, None],
        labels[None, :],
        attended,
        log_total,
        grad_attended,
    )


def pack_body(*refs):
    row_refs, wide_ref, out_ref, stacked = refs[:-3], refs[-3], refs[-2], refs[-1]
    stacked[...] = jnp.zeros_like(stacked)
    for slot, ref in enumerate(row_refs):
        stacked[slot : slot + 1, :] = ref[...]
    rows = stacked[...]
    wide = jnp.broadcast_to(wide_ref[...], (16, wide_ref.shape[1]))
    owners = out_ref.shape[0]
    narrow, long = rows.shape[1] // owners, wide.shape[1] // owners
    lanes = lax.broadcasted_iota(jnp.int32, (16, 128), 1)
    slots = lax.broadcasted_iota(jnp.int32, (16, 128), 0)
    out_ref[...] = jnp.zeros_like(out_ref)

    def window(source, start, width):
        base = min(start // 128 * 128, source.shape[1] - 256)
        offset = start - base
        moved = source[:, base : base + 256]
        if offset:
            moved = pltpu.roll(moved, 256 - offset, 1)
        return jnp.where(lanes < width, moved[:, :128], 0.0)

    for owner in range(owners):
        block = window(rows, owner * narrow, narrow)
        long_block = window(wide, owner * long, long)
        block = jnp.where(slots == len(row_refs), long_block, block)
        out_ref[owner, :, :128] = rounded(block)


def pack_vectors(vectors, wide, owners):
    rows = tuple(vector.reshape(1, -1) for vector in vectors)
    return pl.pallas_call(
        pack_body,
        out_shape=jax.ShapeDtypeStruct((owners, 16, D), jnp.bfloat16),
        scratch_shapes=[pltpu.VMEM((16, D), jnp.float32)],
        name="pack_vectors",
    )(*rows, wide.reshape(1, -1))


def widen_body(frame_ref, out_ref):
    parts = D // 128
    for part in range(parts):
        out_ref[pl.ds(part, frame_ref.shape[0], stride=parts), :] = frame_ref[
            :, part * 128 : (part + 1) * 128
        ].astype(jnp.float32)


def widen_frames(frames):
    frame_count = frames.shape[0]
    parts = D // 128
    wide = pl.pallas_call(
        widen_body,
        grid=(6,),
        in_specs=[pl.BlockSpec((frame_count // 6, D), lambda index: (index, 0))],
        out_specs=pl.BlockSpec((frame_count // 6 * parts, 128), lambda index: (index, 0)),
        out_shape=jax.ShapeDtypeStruct((frame_count * parts, 128), jnp.float32),
        name="widen_frames",
    )(frames)
    return wide.reshape(frame_count, 1, D)


def place_rows(vectors, row_count):
    lead = vectors[0].shape[:-1]
    rows = lax.broadcasted_iota(jnp.int32, lead + (row_count, D), len(lead))
    block = jnp.zeros(rows.shape, jnp.bfloat16)
    for slot, vector in enumerate(vectors):
        padding = [(0, 0)] * len(lead) + [(0, D - vector.shape[-1])]
        wide = jnp.pad(vector.astype(jnp.bfloat16), padding)[..., None, :]
        block = jnp.where(rows == slot, wide, block)
    return block


def halve(buffer, axis, axis_name, flip, bit, kind=jnp.bfloat16):
    kept = lax.dynamic_index_in_dim(buffer, bit, axis, keepdims=False)
    sent = lax.dynamic_index_in_dim(buffer, 1 - bit, axis, keepdims=False)
    pairs = [(index, index ^ flip) for index in range(lax.axis_size(axis_name))]
    received = lax.ppermute(sent, axis_name, pairs)
    return (kept.astype(jnp.float32) + received.astype(jnp.float32)).astype(kind)


def frame_mask(length, shape):
    return lax.broadcasted_iota(jnp.int32, shape, 1) < length


def cross_forward_body(length_ref, query_ref, key_ref, value_ref, out_ref, log_ref):
    query_halves = split_pair(query_ref[...])
    value_halves = split_pair(value_ref[...])
    keys = key_ref[...]
    valid = frame_mask(length_ref[0], (query_ref.shape[0], keys.shape[0]))
    attended = jnp.zeros(query_ref.shape, jnp.float32)
    logs = []
    for half in range(2):
        scores = jnp.where(valid, dot_rows(query_halves[half], keys) * 0.125, neg_large)
        row_max = jnp.max(scores, axis=1, keepdims=True)
        exp_terms = jnp.exp(scores - row_max)
        total = jnp.sum(exp_terms, axis=1, keepdims=True)
        attended = attended + dot_plain(rounded(exp_terms), value_halves[half]) / total
        logs.append(row_max + jnp.log(total))
    out_ref[...] = rounded(attended)
    log_ref[...] = join_pair(logs[0], logs[1], log_ref.shape)


def cross_forward(lengths, queries, keys, values):
    query_spec = pl.BlockSpec((queries.shape[0], PAIR), lambda pair: (0, pair))
    frame_spec = pl.BlockSpec((keys.shape[0], PAIR), lambda pair: (0, pair))
    return pl.pallas_call(
        cross_forward_body,
        grid=(D // PAIR,),
        in_specs=[pl.BlockSpec(memory_space=pltpu.SMEM), query_spec, frame_spec, frame_spec],
        out_specs=[query_spec, query_spec],
        out_shape=[
            jax.ShapeDtypeStruct(queries.shape, jnp.bfloat16),
            jax.ShapeDtypeStruct(queries.shape, jnp.float32),
        ],
        name="cross_forward",
    )(lengths, queries, keys, values)


def cross_backward_body(
    length_ref, query_ref, key_ref, value_ref, log_ref, grad_ref, grad_query_ref, grad_frame_ref
):
    query_halves = split_pair(query_ref[...])
    grad_halves = split_pair(grad_ref[...])
    keys = key_ref[...]
    values = value_ref[...]
    key_halves = split_pair(keys)
    valid = frame_mask(length_ref[0], (query_ref.shape[0], keys.shape[0]))
    logs = (log_ref[:, :1], log_ref[:, HEAD : HEAD + 1])
    query_sum = jnp.zeros(query_ref.shape, jnp.float32)
    key_sum = jnp.zeros(keys.shape, jnp.float32)
    value_sum = jnp.zeros(keys.shape, jnp.float32)
    for half in range(2):
        scores = jnp.where(valid, dot_rows(query_halves[half], keys) * 0.125, neg_large)
        probs = jnp.exp(scores - logs[half])
        grad_probs = dot_rows(grad_halves[half], values)
        delta = jnp.sum(probs * grad_probs, axis=1, keepdims=True)
        grad_scores = rounded(probs * (grad_probs - delta) * 0.125)
        query_sum = query_sum + dot_plain(grad_scores, key_halves[half])
        key_sum = key_sum + dot_columns(grad_scores, query_halves[half])
        value_sum = value_sum + dot_columns(rounded(probs), grad_halves[half])
    grad_query_ref[...] = rounded(query_sum)
    grad_frame_ref[0] = rounded(key_sum)
    grad_frame_ref[1] = rounded(value_sum)


def cross_backward(lengths, queries, keys, values, log_total, grad_attended):
    query_spec = pl.BlockSpec((queries.shape[0], PAIR), lambda pair: (0, pair))
    frame_spec = pl.BlockSpec((keys.shape[0], PAIR), lambda pair: (0, pair))
    return pl.pallas_call(
        cross_backward_body,
        grid=(D // PAIR,),
        in_specs=[
            pl.BlockSpec(memory_space=pltpu.SMEM),
            query_spec,
            frame_spec,
            frame_spec,
            query_spec,
            query_spec,
        ],
        out_specs=[
            query_spec,
            pl.BlockSpec((2, keys.shape[0], PAIR), lambda pair: (0, 0, pair)),
        ],
        out_shape=[
            jax.ShapeDtypeStruct(queries.shape, jnp.bfloat16),
            jax.ShapeDtypeStruct((2,) + keys.shape, jnp.bfloat16),
        ],
        name="cross_backward",
    )(lengths, queries, keys, values, log_total, grad_attended)


def local_heads(
    tokens,
    memory,
    piece_starts,
    memory_lengths,
    self_gain,
    self_shift,
    query_weight,
    query_bias,
    key_weight,
    value_weight,
    value_bias,
    attn_out_weight,
    attn_out_bias,
    cross_gain,
    cross_shift,
    cross_query_weight,
    cross_query_bias,
    cross_key_weight,
    cross_value_weight,
    cross_value_bias,
    cross_out_weight,
    cross_out_bias,
    mlp_gain,
    mlp_shift,
    fc_in_weight,
    fc_in_bias,
    fc_out_weight,
    fc_out_bias,
    out_grad,
):
    local_len, batch_count, _ = tokens.shape
    seq_count = lax.axis_size("seq")
    seq_index = lax.axis_index("seq")
    full_length = local_len * seq_count
    token_count = local_len * batch_count
    query_pos = seq_index * local_len + jnp.arange(local_len, dtype=jnp.int32)
    labels = piece_labels(jnp.arange(full_length, dtype=jnp.int32), piece_starts).reshape(-1)
    input_rows = tokens.reshape(token_count, D).astype(jnp.float32)
    shard_rows = query_weight.shape[0]
    wide_parts = fc_in_weight.shape[1] // D
    vector_block = place_rows(
        (
            self_gain,
            self_shift,
            query_bias,
            value_bias,
            attn_out_bias,
            cross_gain,
            cross_shift,
            cross_query_bias,
            cross_value_bias,
            cross_out_bias,
            mlp_gain,
            mlp_shift,
            fc_out_bias,
            fc_in_bias,
        ),
        16,
    )
    fc_in_blocks = jnp.transpose(
        fc_in_weight.reshape(shard_rows, wide_parts, D), (1, 0, 2)
    ).reshape(wide_parts * shard_rows, D)
    first_packed = jnp.concatenate(
        (
            query_weight,
            key_weight,
            value_weight,
            cross_key_weight,
            cross_value_weight,
            vector_block,
        )
    )
    first = lax.all_gather(first_packed, ("dp", "seq"), axis=0, tiled=False)
    owners = first.shape[0]

    def owner_rows(matrix):
        return matrix.astype(jnp.bfloat16).reshape(owners, -1, D)

    def first_at(slot):
        return first[:, slot * shard_rows : (slot + 1) * shard_rows, :].reshape(D, D)

    full_query, full_key, full_value, full_cross_key, full_cross_value = (
        first_at(slot) for slot in range(5)
    )
    full_vectors = first[:, 5 * shard_rows :, :]
    packed = jnp.concatenate(
        (
            attn_out_weight,
            cross_query_weight,
            cross_out_weight,
            fc_in_blocks,
            fc_out_weight,
        )
    )
    packed, first = lax.optimization_barrier((packed, first))
    gathered = lax.all_gather(packed, ("dp", "seq"), axis=0, tiled=False)

    def square_at(slot):
        return gathered[:, slot * shard_rows : (slot + 1) * shard_rows, :].reshape(D, D)

    full_self_out, full_cross_query, full_cross_out = (square_at(slot) for slot in range(3))
    wide_start = 3 * shard_rows
    wide_stop = wide_start + wide_parts * shard_rows
    full_fc_in = jnp.transpose(
        gathered[:, wide_start:wide_stop, :].reshape(owners, wide_parts, shard_rows, D),
        (0, 2, 1, 3),
    ).reshape(D, wide_parts * D)
    out_stop = wide_stop + fc_out_weight.shape[0]
    full_fc_out = gathered[:, wide_stop:out_stop, :].reshape(wide_parts * D, D)

    def vector_at(slot):
        return full_vectors[:, slot, :shard_rows].reshape(D)

    (
        full_self_gain,
        full_self_shift,
        full_query_bias,
        full_value_bias,
        full_self_out_bias,
        full_cross_gain,
        full_cross_shift,
        full_cross_query_bias,
        full_cross_value_bias,
        full_cross_out_bias,
        full_mlp_gain,
        full_mlp_shift,
        full_fc_out_bias,
    ) = (vector_at(slot) for slot in range(13))
    full_fc_in_bias = full_vectors[:, 13, : fc_in_bias.shape[0]].reshape(-1)
    normed_self, scaled_self, inverse_self = norm_forward(
        input_rows, full_self_gain.astype(jnp.float32), full_self_shift.astype(jnp.float32)
    )
    normed_self_low = rounded(normed_self)
    query_rows = rounded(project(normed_self_low, full_query) + full_query_bias.astype(jnp.float32))
    key_rows = rounded(project(normed_self_low, full_key))
    value_rows = rounded(
        project(normed_self_low, full_value) + full_value_bias.astype(jnp.float32)
    )
    head_triple = lax.all_to_all(
        jnp.stack(
            tuple(to_pairs(rows, seq_count) for rows in (query_rows, key_rows, value_rows)), axis=1
        ),
        "seq",
        0,
        0,
    )
    head_attended, head_log, head_low = self_forward(head_triple, labels)
    attended_blocks = lax.all_to_all(head_low, "seq", 0, 0)
    attended_self_low = from_pairs(attended_blocks)
    middle_rows = (
        input_rows
        + project(attended_self_low, full_self_out)
        + full_self_out_bias.astype(jnp.float32)
    )
    normed_cross, scaled_cross, inverse_cross = norm_forward(
        middle_rows, full_cross_gain.astype(jnp.float32), full_cross_shift.astype(jnp.float32)
    )
    normed_cross_low = rounded(normed_cross)
    cross_queries = rounded(
        project(normed_cross_low, full_cross_query) + full_cross_query_bias.astype(jnp.float32)
    )
    frame_count = memory.shape[0]
    frame_part = frame_count // seq_count
    frame_start = seq_index * frame_part
    memory_flat = memory.reshape(frame_count, D)
    memory_part = lax.dynamic_slice_in_dim(memory_flat, frame_start, frame_part, 0)
    memory_keys = rounded(project(memory_flat, full_cross_key))
    memory_values = rounded(
        project(memory_flat, full_cross_value) + full_cross_value_bias.astype(jnp.float32)
    )
    attended_cross_low, cross_log = cross_forward(
        memory_lengths, cross_queries, memory_keys, memory_values
    )
    after_rows = (
        middle_rows
        + project(attended_cross_low, full_cross_out)
        + full_cross_out_bias.astype(jnp.float32)
    )
    normed_mlp, scaled_mlp, inverse_mlp = norm_forward(
        after_rows, full_mlp_gain.astype(jnp.float32), full_mlp_shift.astype(jnp.float32)
    )
    normed_mlp_low = rounded(normed_mlp)
    hidden_pre = project(normed_mlp_low, full_fc_in) + full_fc_in_bias.astype(jnp.float32)
    activated, gelu_pull = jax.vjp(exact_gelu, hidden_pre)
    activated_low = rounded(activated)
    result_rows = (
        after_rows + project(activated_low, full_fc_out) + full_fc_out_bias.astype(jnp.float32)
    )
    output = rounded(result_rows).reshape(local_len, batch_count, D)
    back_fc_in, back_fc_out = full_fc_in, full_fc_out
    grad_result = out_grad.reshape(token_count, D)
    grad_mlp_low = rounded(grad_result)
    grad_fc_out_weight = weight_grad(activated_low, grad_mlp_low)
    grad_fc_out_bias = row_sums(grad_mlp_low)
    grad_activated = project_back(grad_mlp_low, back_fc_out)
    grad_hidden_low = rounded(gelu_pull(grad_activated)[0])
    grad_fc_in_blocks = tuple(
        weight_grad(normed_mlp_low, grad_hidden_low[:, part * D : (part + 1) * D])
        for part in range(wide_parts)
    )
    grad_fc_in_bias = row_sums(grad_hidden_low)
    grad_normed_mlp = project_back(grad_hidden_low, back_fc_in)
    grad_rows_mlp, grad_mlp_gain, grad_mlp_shift = norm_backward(
        grad_normed_mlp, scaled_mlp, inverse_mlp, full_mlp_gain.astype(jnp.float32)
    )
    grad_after = grad_result + grad_rows_mlp
    back_cross_query, back_cross_key, back_cross_value, back_cross_out = (
        full_cross_query,
        full_cross_key,
        full_cross_value,
        full_cross_out,
    )
    grad_cross_low = rounded(grad_after)
    grad_cross_out_weight = weight_grad(attended_cross_low, grad_cross_low)
    grad_cross_out_bias = row_sums(grad_cross_low)
    grad_attended_cross = rounded(project_back(grad_cross_low, back_cross_out))
    grad_cross_queries, grad_memory_kv = cross_backward(
        memory_lengths,
        cross_queries,
        memory_keys,
        memory_values,
        cross_log,
        grad_attended_cross,
    )
    dp_index = lax.axis_index("dp")
    core_bit, x_bit = dp_index % 2, dp_index // 2
    y_bit, low_bit, high_bit = seq_index % 2, (seq_index // 2) % 2, seq_index // 4
    memory_parts = grad_memory_kv.reshape(2, 2, 2, 2, frame_part, D)
    key_columns = halve(memory_parts[0], 2, "seq", 1, y_bit)
    value_columns = halve(memory_parts[1], 1, "seq", 2, low_bit)
    part_keys = halve(key_columns, 1, "seq", 2, low_bit)
    part_values = halve(value_columns, 1, "seq", 1, y_bit)
    part_flat_keys = halve(part_keys, 0, "seq", 4, high_bit)
    part_flat_values = halve(part_values, 0, "seq", 4, high_bit)
    part_memory_grad = (
        project_back(part_flat_keys, back_cross_key)
        + project_back(part_flat_values, back_cross_value)
    )
    grad_cross_key_weight = weight_grad(memory_part, part_flat_keys)
    grad_cross_value_weight = weight_grad(memory_part, part_flat_values)
    grad_cross_value_bias = row_sums(part_flat_values)
    grad_cross_query_weight = weight_grad(normed_cross_low, grad_cross_queries)
    grad_cross_query_bias = row_sums(grad_cross_queries)
    grad_normed_cross = project_back(grad_cross_queries, back_cross_query)
    grad_rows_cross, grad_cross_gain, grad_cross_shift = norm_backward(
        grad_normed_cross, scaled_cross, inverse_cross, full_cross_gain.astype(jnp.float32)
    )
    grad_middle = grad_after + grad_rows_cross
    back_query, back_key, back_value, back_self_out = (
        full_query,
        full_key,
        full_value,
        full_self_out,
    )
    grad_self_low = rounded(grad_middle)
    grad_attn_out_weight = weight_grad(attended_self_low, grad_self_low)
    grad_attn_out_bias = row_sums(grad_self_low)
    early_grads = jnp.concatenate(
        (
            *(owner_rows(block) for block in grad_fc_in_blocks),
            owner_rows(grad_fc_out_weight),
            owner_rows(grad_attn_out_weight),
            owner_rows(grad_cross_query_weight),
            owner_rows(grad_cross_out_weight),
        ),
        axis=1,
    )
    owned_early = lax.psum_scatter(
        early_grads, ("dp", "seq"), scatter_dimension=0, tiled=False
    )
    owned_early = owned_early.astype(jnp.float32)
    wide_rows = wide_parts * shard_rows
    owned_fc_in = jnp.transpose(
        owned_early[:wide_rows].reshape(wide_parts, shard_rows, D), (1, 0, 2)
    ).reshape(shard_rows, wide_parts * D)
    out_rows = wide_rows + fc_out_weight.shape[0]
    owned_fc_out = owned_early[wide_rows:out_rows]
    owned_middle = owned_early[out_rows:]
    grad_attended_self = rounded(project_back(grad_self_low, back_self_out))
    head_blocks = to_pairs(grad_attended_self, seq_count)
    head_grad = lax.all_to_all(head_blocks, "seq", 0, 0)
    grad_blocks = self_backward(head_triple, labels, head_attended, head_log, head_grad)
    grad_triple = lax.all_to_all(grad_blocks, "seq", 0, 0)
    grad_query_low, grad_key_low, grad_value_low = (
        from_pairs(grad_triple[:, slot]) for slot in range(3)
    )
    grad_query_weight = weight_grad(normed_self_low, grad_query_low)
    grad_query_bias = row_sums(grad_query_low)
    grad_key_weight = weight_grad(normed_self_low, grad_key_low)
    grad_value_weight = weight_grad(normed_self_low, grad_value_low)
    grad_value_bias = row_sums(grad_value_low)
    grad_normed_self = (
        project_back(grad_query_low, back_query)
        + project_back(grad_key_low, back_key)
        + project_back(grad_value_low, back_value)
    )
    grad_rows_self, grad_self_gain, grad_self_shift = norm_backward(
        grad_normed_self, scaled_self, inverse_self, full_self_gain.astype(jnp.float32)
    )
    token_grad = (grad_middle + grad_rows_self).reshape(local_len, batch_count, D)
    late_block = pack_vectors(
        (
            grad_self_gain,
            grad_self_shift,
            grad_query_bias,
            grad_value_bias,
            grad_attn_out_bias,
            grad_cross_gain,
            grad_cross_shift,
            grad_cross_query_bias,
            grad_cross_value_bias,
            grad_cross_out_bias,
            grad_mlp_gain,
            grad_mlp_shift,
            grad_fc_out_bias,
        ),
        grad_fc_in_bias,
        owners,
    )
    late_grads = jnp.concatenate(
        (
            owner_rows(grad_query_weight),
            owner_rows(grad_key_weight),
            owner_rows(grad_value_weight),
            owner_rows(grad_cross_key_weight),
            owner_rows(grad_cross_value_weight),
            late_block,
        ),
        axis=1,
    )
    late_rows = late_grads.shape[1]
    by_core = halve(late_grads.reshape(2, 2, 2, 2, 2, late_rows, D), 1, "dp", 1, core_bit)
    cut_row = late_rows // 16 * 8
    upper = by_core[:, :, :, :, :cut_row]
    lower = by_core[:, :, :, :, cut_row:]
    upper = halve(halve(upper, 0, "dp", 2, x_bit), 2, "seq", 1, y_bit)
    lower = halve(halve(lower, 3, "seq", 1, y_bit), 0, "dp", 2, x_bit)
    by_column = jnp.concatenate((upper, lower), axis=2)
    owned_late = halve(
        halve(by_column, 1, "seq", 2, low_bit), 0, "seq", 4, high_bit, jnp.float32
    )
    memory_grad = lax.all_gather(part_memory_grad.astype(jnp.bfloat16), "seq", axis=0, tiled=True)
    memory_grad = widen_frames(memory_grad)
    owned_vectors = owned_late[5 * shard_rows :]

    def own_square(slot):
        return owned_late[slot * shard_rows : (slot + 1) * shard_rows]

    def own_middle(slot):
        return owned_middle[slot * shard_rows : (slot + 1) * shard_rows]

    def own_vector(slot):
        return owned_vectors[slot, :shard_rows]

    owned_fc_in_bias = owned_vectors[13, : fc_in_bias.shape[0]]
    return (
        output,
        token_grad,
        memory_grad,
        own_vector(0),
        own_vector(1),
        own_square(0),
        own_vector(2),
        own_square(1),
        own_square(2),
        own_vector(3),
        own_middle(0),
        own_vector(4),
        own_vector(5),
        own_vector(6),
        own_middle(1),
        own_vector(7),
        own_square(3),
        own_square(4),
        own_vector(8),
        own_middle(2),
        own_vector(9),
        own_vector(10),
        own_vector(11),
        owned_fc_in,
        owned_fc_in_bias,
        owned_fc_out,
        own_vector(12),
    )


def local(
    tokens,
    memory,
    piece_starts,
    memory_lengths,
    self_gain,
    self_shift,
    query_weight,
    query_bias,
    key_weight,
    value_weight,
    value_bias,
    attn_out_weight,
    attn_out_bias,
    cross_gain,
    cross_shift,
    cross_query_weight,
    cross_query_bias,
    cross_key_weight,
    cross_value_weight,
    cross_value_bias,
    cross_out_weight,
    cross_out_bias,
    mlp_gain,
    mlp_shift,
    fc_in_weight,
    fc_in_bias,
    fc_out_weight,
    fc_out_bias,
    out_grad,
):
    local_len, batch_count, _ = tokens.shape
    seq_count = lax.axis_size("seq")
    seq_index = lax.axis_index("seq")
    full_length = local_len * seq_count
    token_count = local_len * batch_count
    query_pos = seq_index * local_len + jnp.arange(local_len, dtype=jnp.int32)
    query_label = piece_labels(query_pos, piece_starts)
    input_rows = tokens.reshape(token_count, D).astype(jnp.float32)
    shard_rows = query_weight.shape[0]
    wide_parts = fc_in_weight.shape[1] // D
    vectors = jnp.concatenate(
        (
            self_gain,
            self_shift,
            query_bias,
            value_bias,
            attn_out_bias,
            cross_gain,
            cross_shift,
            cross_query_bias,
            cross_value_bias,
            cross_out_bias,
            mlp_gain,
            mlp_shift,
            fc_out_bias,
            fc_in_bias,
        )
    )
    vector_rows = 8
    vector_block = jnp.pad(vectors, (0, vector_rows * D - vectors.shape[0])).reshape(vector_rows, D)
    fc_in_blocks = jnp.transpose(
        fc_in_weight.reshape(shard_rows, wide_parts, D), (1, 0, 2)
    ).reshape(wide_parts * shard_rows, D)
    packed = jnp.concatenate(
        (
            query_weight,
            key_weight,
            value_weight,
            attn_out_weight,
            cross_query_weight,
            cross_key_weight,
            cross_value_weight,
            cross_out_weight,
            fc_in_blocks,
            fc_out_weight,
            vector_block,
        )
    )
    gathered = lax.all_gather(packed, ("dp", "seq"), axis=0, tiled=False)
    owners = gathered.shape[0]

    def square_at(slot):
        return gathered[:, slot * shard_rows : (slot + 1) * shard_rows, :].reshape(D, D)

    full_query, full_key, full_value, full_self_out = (square_at(slot) for slot in range(4))
    full_cross_query, full_cross_key, full_cross_value, full_cross_out = (
        square_at(slot) for slot in range(4, 8)
    )
    wide_start = 8 * shard_rows
    wide_stop = wide_start + wide_parts * shard_rows
    full_fc_in = jnp.transpose(
        gathered[:, wide_start:wide_stop, :].reshape(owners, wide_parts, shard_rows, D),
        (0, 2, 1, 3),
    ).reshape(D, wide_parts * D)
    out_stop = wide_stop + fc_out_weight.shape[0]
    full_fc_out = gathered[:, wide_stop:out_stop, :].reshape(wide_parts * D, D)
    full_vectors = gathered[:, out_stop:, :].reshape(owners, vector_rows * D)

    def vector_at(slot):
        return full_vectors[:, slot * shard_rows : (slot + 1) * shard_rows].reshape(D)

    (
        full_self_gain,
        full_self_shift,
        full_query_bias,
        full_value_bias,
        full_self_out_bias,
        full_cross_gain,
        full_cross_shift,
        full_cross_query_bias,
        full_cross_value_bias,
        full_cross_out_bias,
        full_mlp_gain,
        full_mlp_shift,
        full_fc_out_bias,
    ) = (vector_at(slot) for slot in range(13))
    full_fc_in_bias = full_vectors[
        :, 13 * shard_rows : 13 * shard_rows + fc_in_bias.shape[0]
    ].reshape(-1)
    normed_self, scaled_self, inverse_self = norm_forward(
        input_rows, full_self_gain.astype(jnp.float32), full_self_shift.astype(jnp.float32)
    )
    normed_self_low = rounded(normed_self)
    query_rows = rounded(project(normed_self_low, full_query) + full_query_bias.astype(jnp.float32))
    key_rows = rounded(project(normed_self_low, full_key)).reshape(local_len, batch_count, D)
    value_rows = rounded(
        project(normed_self_low, full_value) + full_value_bias.astype(jnp.float32)
    ).reshape(local_len, batch_count, D)
    query_heads = query_rows.reshape(local_len, batch_count, HEADS, HEAD)

    def key_block_scores(key_block, key_pos):
        key_heads = key_block.reshape(key_block.shape[0], batch_count, HEADS, HEAD)
        raw_scores = jnp.einsum(
            "qbhd,kbhd->qbhk", query_heads, key_heads, preferred_element_type=jnp.float32
        )
        allowed = visible(query_pos, query_label, key_pos, piece_labels(key_pos, piece_starts))
        return (raw_scores * 0.125, allowed)

    start_state = (
        jnp.full((local_len, batch_count, HEADS), neg_large, jnp.float32),
        jnp.zeros((local_len, batch_count, HEADS), jnp.float32),
        jnp.zeros((local_len, batch_count, HEADS, HEAD), jnp.float32),
    )
    running = start_state
    kv_piece = lax.all_gather(
        jnp.concatenate((key_rows, value_rows), axis=2), "seq", axis=0, tiled=True
    )
    key_piece = kv_piece[:, :, :D]
    value_piece = kv_piece[:, :, D:]
    block_rows = math.gcd(key_piece.shape[0], 512)

    def fold_block(inner_state, block_index):
        row_max, row_total, weighted_sum = inner_state
        block_start = block_index * block_rows
        key_block = lax.dynamic_slice_in_dim(key_piece, block_start, block_rows, 0)
        value_block = lax.dynamic_slice_in_dim(value_piece, block_start, block_rows, 0).reshape(
            block_rows, batch_count, HEADS, HEAD
        )
        key_pos = block_start + jnp.arange(block_rows, dtype=jnp.int32)
        scores, allowed = key_block_scores(key_block, key_pos)
        new_max = jnp.maximum(row_max, jnp.max(jnp.where(allowed, scores, neg_large), axis=-1))
        exp_terms = jnp.where(allowed, jnp.exp(scores - new_max[..., None]), 0.0)
        factor = jnp.exp(row_max - new_max)
        row_total = row_total * factor + jnp.sum(exp_terms, axis=-1)
        weighted_sum = weighted_sum * factor[..., None] + jnp.einsum(
            "qbhk,kbhd->qbhd", rounded(exp_terms), value_block, preferred_element_type=jnp.float32
        )
        return ((new_max, row_total, weighted_sum), None)

    running, unused = lax.scan(
        fold_block, running, jnp.arange(key_piece.shape[0] // block_rows, dtype=jnp.int32)
    )
    row_max, row_total, weighted_sum = running
    attended_self = weighted_sum / row_total[..., None]
    log_total = row_max + jnp.log(row_total)
    attended_self_low = rounded(attended_self.reshape(token_count, D))
    middle_rows = (
        input_rows
        + project(attended_self_low, full_self_out)
        + full_self_out_bias.astype(jnp.float32)
    )
    normed_cross, scaled_cross, inverse_cross = norm_forward(
        middle_rows, full_cross_gain.astype(jnp.float32), full_cross_shift.astype(jnp.float32)
    )
    normed_cross_low = rounded(normed_cross)
    cross_queries = rounded(
        project(normed_cross_low, full_cross_query) + full_cross_query_bias.astype(jnp.float32)
    ).reshape(local_len, batch_count, HEADS, HEAD)
    frame_count = memory.shape[0]
    frame_part = frame_count // seq_count
    frame_start = seq_index * frame_part
    memory_part = lax.dynamic_slice_in_dim(memory, frame_start, frame_part, 0).reshape(
        frame_part * batch_count, D
    )
    memory_flat = memory.reshape(frame_count * batch_count, D)
    memory_keys = rounded(project(memory_flat, full_cross_key)).reshape(frame_count, batch_count, D)
    memory_values = rounded(
        project(memory_flat, full_cross_value) + full_cross_value_bias.astype(jnp.float32)
    ).reshape(frame_count, batch_count, D)
    memory_key_heads = memory_keys.reshape(frame_count, batch_count, HEADS, HEAD)
    memory_value_heads = memory_values.reshape(frame_count, batch_count, HEADS, HEAD)
    frame_valid = (jnp.arange(frame_count, dtype=jnp.int32)[None, :] < memory_lengths[:, None])[
        None, :, None, :
    ]
    cross_scores = (
        jnp.einsum(
            "qbhd,kbhd->qbhk", cross_queries, memory_key_heads, preferred_element_type=jnp.float32
        )
        * 0.125
    )
    cross_max = jnp.max(jnp.where(frame_valid, cross_scores, neg_large), axis=-1, keepdims=True)
    cross_exp = jnp.where(frame_valid, jnp.exp(cross_scores - cross_max), 0.0)
    cross_probs = cross_exp / jnp.sum(cross_exp, axis=-1, keepdims=True)
    cross_probs_low = rounded(cross_probs)
    attended_cross = jnp.einsum(
        "qbhk,kbhd->qbhd", cross_probs_low, memory_value_heads, preferred_element_type=jnp.float32
    )
    attended_cross_low = rounded(attended_cross.reshape(token_count, D))
    after_rows = (
        middle_rows
        + project(attended_cross_low, full_cross_out)
        + full_cross_out_bias.astype(jnp.float32)
    )
    normed_mlp, scaled_mlp, inverse_mlp = norm_forward(
        after_rows, full_mlp_gain.astype(jnp.float32), full_mlp_shift.astype(jnp.float32)
    )
    normed_mlp_low = rounded(normed_mlp)
    hidden_pre = project(normed_mlp_low, full_fc_in) + full_fc_in_bias.astype(jnp.float32)
    activated, gelu_pull = jax.vjp(exact_gelu, hidden_pre)
    activated_low = rounded(activated)
    result_rows = (
        after_rows + project(activated_low, full_fc_out) + full_fc_out_bias.astype(jnp.float32)
    )
    output = rounded(result_rows).reshape(local_len, batch_count, D)
    back_fc_in, back_fc_out = full_fc_in, full_fc_out
    grad_result = out_grad.reshape(token_count, D)
    grad_mlp_low = rounded(grad_result)
    grad_fc_out_weight = weight_grad(activated_low, grad_mlp_low)
    grad_fc_out_bias = column_sums(grad_mlp_low)
    grad_activated = project_back(grad_mlp_low, back_fc_out)
    grad_hidden_low = rounded(gelu_pull(grad_activated)[0])
    grad_fc_in_weight = weight_grad(normed_mlp_low, grad_hidden_low)
    grad_fc_in_bias = column_sums(grad_hidden_low)
    grad_normed_mlp = project_back(grad_hidden_low, back_fc_in)
    grad_rows_mlp, grad_mlp_gain, grad_mlp_shift = norm_backward(
        grad_normed_mlp, scaled_mlp, inverse_mlp, full_mlp_gain.astype(jnp.float32)
    )
    early_grads = jnp.concatenate(
        (
            jnp.transpose(
                grad_fc_in_weight.astype(jnp.bfloat16).reshape(
                    owners, shard_rows, wide_parts, D
                ),
                (0, 2, 1, 3),
            ).reshape(owners, wide_parts * shard_rows, D),
            grad_fc_out_weight.astype(jnp.bfloat16).reshape(owners, -1, D),
        ),
        axis=1,
    )
    owned_early = lax.psum_scatter(
        early_grads, ("dp", "seq"), scatter_dimension=0, tiled=False
    ).astype(jnp.float32)
    wide_rows = wide_parts * shard_rows
    owned_fc_in = jnp.transpose(
        owned_early[:wide_rows].reshape(wide_parts, shard_rows, D), (1, 0, 2)
    ).reshape(shard_rows, wide_parts * D)
    owned_fc_out = owned_early[wide_rows:]
    grad_after = grad_result + grad_rows_mlp
    back_cross_query, back_cross_key, back_cross_value, back_cross_out = (
        full_cross_query,
        full_cross_key,
        full_cross_value,
        full_cross_out,
    )
    grad_cross_low = rounded(grad_after)
    grad_cross_out_weight = weight_grad(attended_cross_low, grad_cross_low)
    grad_cross_out_bias = column_sums(grad_cross_low)
    grad_attended_cross = rounded(project_back(grad_cross_low, back_cross_out)).reshape(
        local_len, batch_count, HEADS, HEAD
    )
    grad_cross_probs = jnp.einsum(
        "qbhd,kbhd->qbhk",
        grad_attended_cross,
        memory_value_heads,
        preferred_element_type=jnp.float32,
    )
    cross_delta = jnp.sum(cross_probs * grad_cross_probs, axis=-1, keepdims=True)
    grad_cross_scores = rounded(cross_probs * (grad_cross_probs - cross_delta) * 0.125)
    grad_cross_queries = rounded(
        jnp.einsum(
            "qbhk,kbhd->qbhd",
            grad_cross_scores,
            memory_key_heads,
            preferred_element_type=jnp.float32,
        ).reshape(token_count, D)
    )
    grad_memory_keys = jnp.einsum(
        "qbhk,qbhd->kbhd", grad_cross_scores, cross_queries, preferred_element_type=jnp.float32
    ).reshape(frame_count, batch_count, D)
    grad_memory_values = jnp.einsum(
        "qbhk,qbhd->kbhd", cross_probs_low, grad_attended_cross, preferred_element_type=jnp.float32
    ).reshape(frame_count, batch_count, D)
    grad_memory_kv = jnp.concatenate((grad_memory_keys, grad_memory_values), axis=2)
    grad_cross_query_weight = weight_grad(normed_cross_low, grad_cross_queries)
    grad_cross_query_bias = column_sums(grad_cross_queries)
    grad_normed_cross = project_back(grad_cross_queries, back_cross_query)
    grad_rows_cross, grad_cross_gain, grad_cross_shift = norm_backward(
        grad_normed_cross, scaled_cross, inverse_cross, full_cross_gain.astype(jnp.float32)
    )
    grad_middle = grad_after + grad_rows_cross
    back_query, back_key, back_value, back_self_out = (
        full_query,
        full_key,
        full_value,
        full_self_out,
    )
    grad_self_low = rounded(grad_middle)
    grad_attn_out_weight = weight_grad(attended_self_low, grad_self_low)
    grad_attn_out_bias = column_sums(grad_self_low)
    grad_attended_self = rounded(project_back(grad_self_low, back_self_out)).reshape(
        local_len, batch_count, HEADS, HEAD
    )
    self_delta = jnp.sum(grad_attended_self.astype(jnp.float32) * attended_self, axis=-1)

    def score_grads(key_block, value_block, key_pos):
        scores, allowed = key_block_scores(key_block, key_pos)
        attn_probs = jnp.where(allowed, jnp.exp(scores - log_total[..., None]), 0.0)
        grad_probs = jnp.einsum(
            "qbhd,kbhd->qbhk", grad_attended_self, value_block, preferred_element_type=jnp.float32
        )
        grad_scores = rounded(attn_probs * (grad_probs - self_delta[..., None]) * 0.125)
        return (grad_scores, attn_probs)

    zero_query_grad = jnp.zeros((local_len, batch_count, HEADS, HEAD), jnp.float32)
    back_state = (zero_query_grad, jnp.zeros((full_length, batch_count, 2 * D), jnp.float32))
    running = back_state
    self_key_piece = key_piece
    self_value_piece = value_piece
    self_block_rows = math.gcd(self_key_piece.shape[0], 512)

    def back_block(inner_state, block_index):
        grad_query_sum, kv_grads = inner_state
        block_start = block_index * self_block_rows
        key_block = lax.dynamic_slice_in_dim(self_key_piece, block_start, self_block_rows, 0)
        value_block = lax.dynamic_slice_in_dim(
            self_value_piece, block_start, self_block_rows, 0
        ).reshape(self_block_rows, batch_count, HEADS, HEAD)
        key_pos = block_start + jnp.arange(self_block_rows, dtype=jnp.int32)
        grad_scores, attn_probs = score_grads(key_block, value_block, key_pos)
        key_heads = key_block.reshape(self_block_rows, batch_count, HEADS, HEAD)
        grad_query_sum = grad_query_sum + jnp.einsum(
            "qbhk,kbhd->qbhd", grad_scores, key_heads, preferred_element_type=jnp.float32
        )
        grad_key_block = jnp.einsum(
            "qbhk,qbhd->kbhd", grad_scores, query_heads, preferred_element_type=jnp.float32
        ).reshape(self_block_rows, batch_count, D)
        grad_value_block = jnp.einsum(
            "qbhk,qbhd->kbhd",
            rounded(attn_probs),
            grad_attended_self,
            preferred_element_type=jnp.float32,
        ).reshape(self_block_rows, batch_count, D)
        kv_grads = lax.dynamic_update_slice_in_dim(
            kv_grads, jnp.concatenate((grad_key_block, grad_value_block), axis=2), block_start, 0
        )
        return ((grad_query_sum, kv_grads), None)

    running, unused = lax.scan(
        back_block, running, jnp.arange(self_key_piece.shape[0] // self_block_rows, dtype=jnp.int32)
    )
    grad_query_sum = running[0]
    joint_kv = jnp.concatenate(
        (
            running[1].astype(jnp.bfloat16).reshape(seq_count, local_len, batch_count, 2 * D),
            grad_memory_kv.astype(jnp.bfloat16).reshape(
                seq_count, frame_part, batch_count, 2 * D
            ),
        ),
        axis=1,
    )
    own_joint = lax.psum_scatter(joint_kv, "seq", scatter_dimension=0, tiled=False)
    own_kv = own_joint[:local_len]
    part_kv = own_joint[local_len:]
    grad_key_low = own_kv[:, :, :D].reshape(token_count, D)
    grad_value_low = own_kv[:, :, D:].reshape(token_count, D)
    part_flat_keys = part_kv[:, :, :D].reshape(frame_part * batch_count, D)
    part_flat_values = part_kv[:, :, D:].reshape(frame_part * batch_count, D)
    part_memory_grad = (
        project_back(part_flat_keys, back_cross_key)
        + project_back(part_flat_values, back_cross_value)
    ).reshape(frame_part, batch_count, D)
    grad_cross_key_weight = weight_grad(memory_part, part_flat_keys)
    grad_cross_value_weight = weight_grad(memory_part, part_flat_values)
    grad_cross_value_bias = column_sums(part_flat_values)
    grad_query_low = rounded(grad_query_sum.reshape(token_count, D))
    grad_query_weight = weight_grad(normed_self_low, grad_query_low)
    grad_query_bias = column_sums(grad_query_low)
    grad_key_weight = weight_grad(normed_self_low, grad_key_low)
    grad_value_weight = weight_grad(normed_self_low, grad_value_low)
    grad_value_bias = column_sums(grad_value_low)
    grad_normed_self = (
        project_back(grad_query_low, back_query)
        + project_back(grad_key_low, back_key)
        + project_back(grad_value_low, back_value)
    )
    grad_rows_self, grad_self_gain, grad_self_shift = norm_backward(
        grad_normed_self, scaled_self, inverse_self, full_self_gain.astype(jnp.float32)
    )
    token_grad = (grad_middle + grad_rows_self).reshape(local_len, batch_count, D)

    def owner_rows(matrix):
        return matrix.astype(jnp.bfloat16).reshape(owners, -1, D)

    late_vectors = jnp.concatenate(
        tuple(
            vector.reshape(owners, -1)
            for vector in (
                grad_self_gain,
                grad_self_shift,
                grad_query_bias,
                grad_value_bias,
                grad_attn_out_bias,
                grad_cross_gain,
                grad_cross_shift,
                grad_cross_query_bias,
                grad_cross_value_bias,
                grad_cross_out_bias,
                grad_mlp_gain,
                grad_mlp_shift,
                grad_fc_out_bias,
                grad_fc_in_bias,
            )
        ),
        axis=1,
    )
    late_block = jnp.pad(
        late_vectors.astype(jnp.bfloat16),
        ((0, 0), (0, vector_rows * D - late_vectors.shape[1])),
    ).reshape(owners, vector_rows, D)
    late_grads = jnp.concatenate(
        (
            owner_rows(grad_query_weight),
            owner_rows(grad_key_weight),
            owner_rows(grad_value_weight),
            owner_rows(grad_attn_out_weight),
            owner_rows(grad_cross_query_weight),
            owner_rows(grad_cross_key_weight),
            owner_rows(grad_cross_value_weight),
            owner_rows(grad_cross_out_weight),
            late_block,
        ),
        axis=1,
    )
    owned_late = lax.psum_scatter(
        late_grads, ("dp", "seq"), scatter_dimension=0, tiled=False
    ).astype(jnp.float32)
    memory_grad = lax.all_gather(
        part_memory_grad.astype(jnp.bfloat16), "seq", axis=0, tiled=True
    ).astype(jnp.float32)
    owned_vectors = owned_late[8 * shard_rows :].reshape(-1)

    def own_square(slot):
        return owned_late[slot * shard_rows : (slot + 1) * shard_rows]

    def own_vector(slot):
        return owned_vectors[slot * shard_rows : (slot + 1) * shard_rows]

    owned_fc_in_bias = owned_vectors[13 * shard_rows : 13 * shard_rows + fc_in_bias.shape[0]]
    return (
        output,
        token_grad,
        memory_grad,
        own_vector(0),
        own_vector(1),
        own_square(0),
        own_vector(2),
        own_square(1),
        own_square(2),
        own_vector(3),
        own_square(3),
        own_vector(4),
        own_vector(5),
        own_vector(6),
        own_square(4),
        own_vector(7),
        own_square(5),
        own_square(6),
        own_vector(8),
        own_square(7),
        own_vector(9),
        own_vector(10),
        own_vector(11),
        owned_fc_in,
        owned_fc_in_bias,
        owned_fc_out,
        own_vector(12),
    )


def solution(mesh):
    in_specs = (
        P("seq", "dp", None),
        P(None, "dp", None),
        P("dp", None),
        P("dp"),
        P(("dp", "seq")),
        P(("dp", "seq")),
        P(("dp", "seq"), None),
        P(("dp", "seq")),
        P(("dp", "seq"), None),
        P(("dp", "seq"), None),
        P(("dp", "seq")),
        P(("dp", "seq"), None),
        P(("dp", "seq")),
        P(("dp", "seq")),
        P(("dp", "seq")),
        P(("dp", "seq"), None),
        P(("dp", "seq")),
        P(("dp", "seq"), None),
        P(("dp", "seq"), None),
        P(("dp", "seq")),
        P(("dp", "seq"), None),
        P(("dp", "seq")),
        P(("dp", "seq")),
        P(("dp", "seq")),
        P(("dp", "seq"), None),
        P(("dp", "seq")),
        P(("dp", "seq"), None),
        P(("dp", "seq")),
        P("seq", "dp", None),
    )
    out_specs = (
        P("seq", "dp", None),
        P("seq", "dp", None),
        P(None, "dp", None),
        P(("dp", "seq")),
        P(("dp", "seq")),
        P(("dp", "seq"), None),
        P(("dp", "seq")),
        P(("dp", "seq"), None),
        P(("dp", "seq"), None),
        P(("dp", "seq")),
        P(("dp", "seq"), None),
        P(("dp", "seq")),
        P(("dp", "seq")),
        P(("dp", "seq")),
        P(("dp", "seq"), None),
        P(("dp", "seq")),
        P(("dp", "seq"), None),
        P(("dp", "seq"), None),
        P(("dp", "seq")),
        P(("dp", "seq"), None),
        P(("dp", "seq")),
        P(("dp", "seq")),
        P(("dp", "seq")),
        P(("dp", "seq"), None),
        P(("dp", "seq")),
        P(("dp", "seq"), None),
        P(("dp", "seq")),
    )
    by_heads = mesh.shape["dp"] == 4 and mesh.shape["seq"] == 8

    def layer(*arrays):
        return local_heads(*arrays)

    return jax.shard_map(
        layer if by_heads else local,
        mesh=mesh,
        in_specs=in_specs,
        out_specs=out_specs,
        check_vma=False,
    )
```
